32 devices in a mesh: group: 4 (over y, x), replica: 8 (over z, core).
Axes of the slice: x: 2, y: 2, z: 4, core: 2. Of those that a mesh axis runs over, the one named last changes fastest.
Arguments:
- tokens: bfloat16 [32, 256, 1024], P(('group', 'replica')), may hold values from -6 to 6
- frames: bfloat16 [32, 1024, 1024], P(('group', 'replica')), may hold values from -6 to 6
- cotangent: bfloat16 [32, 256, 1024], P(('group', 'replica')), may hold values from -6 to 6
- self_qkv: bfloat16 [3, 1024, 1024], P(None, 'group'), may hold values from -0.1875 to 0.1875
- self_out: bfloat16 [1024, 1024], P('group'), may hold values from -0.75 to 0.75
- cross_qkv: bfloat16 [3, 1024, 1024], P(None, 'group'), may hold values from -0.1875 to 0.1875
- cross_out: bfloat16 [1024, 1024], P('group'), may hold values from -1 to 1
- fc1_weight: bfloat16 [1024, 4096], P('group'), may hold values from -0.1875 to 0.1875
- fc2_weight: bfloat16 [4096, 1024], P('group'), may hold values from -0.09375 to 0.09375
- gains: bfloat16 [3, 1024], P(None, 'group'), may hold values from 0.099609375 to 1.8984375
- biases: bfloat16 [10, 1024], P(None, 'group'), may hold values from -3 to 3
- fc1_bias: bfloat16 [4096], P('group'), may hold values from -3 to 3
Outputs:
- output: bfloat16 [32, 256, 1024], P(('group', 'replica'))
- grad_tokens: float32 [32, 256, 1024], P(('group', 'replica'))
- grad_frames: float32 [32, 1024, 1024], P(('group', 'replica'))
- grad_self_qkv: float32 [3, 1024, 1024], P(None, 'group')
- grad_self_out: float32 [1024, 1024], P('group')
- grad_cross_qkv: float32 [3, 1024, 1024], P(None, 'group')
- grad_cross_out: float32 [1024, 1024], P('group')
- grad_fc1: float32 [1024, 4096], P('group')
- grad_fc2: float32 [4096, 1024], P('group')
- grad_gains: float32 [3, 1024], P(None, 'group')
- grad_biases: float32 [10, 1024], P(None, 'group')
- grad_fc1_bias: float32 [4096], P('group')
The draws below stay inside these ranges and needn't reach their ends.
All inputs are finite; a program needn't handle non-finite values.
Results may differ from the reference program's by a relative error of at most 0.02.
Values may be sent and summed in bfloat16 or wider, within the bound.
A program may use at most 256 MiB of HBM per device.

```python
import math
import jax
import jax.numpy as jnp
from jax import lax

D = 1024
FF = 4096
HEADS = 16
HEAD_DIM = 64
LEN = 256
FRAMES = 1024
SEQS = 32


def steps_of(rng, dims, split, low, top_value):
    factor_of = 1.0
    for dim, shards_of in split:
        draws = jax.random.uniform(jax.random.fold_in(jax.random.fold_in(rng, 6), dim), (shards_of,), jnp.float32, low / len(split), top_value / len(split))
        factor_of = factor_of * jnp.repeat(jnp.exp(draws), dims[dim] // shards_of).reshape((-1,) + (1,) * (len(dims) - 1 - dim))
    return factor_of


def scatter_about(rng, dims, deviation, limit, split=(), held_as=jnp.bfloat16):
    array = deviation * jax.random.normal(rng, dims, jnp.float32)
    if split:
        array = array * steps_of(rng, dims, split, -0.22, 0.18)
    return jnp.clip(array, -limit, limit).astype(held_as)


def setup_inputs(seed: int = 0) -> dict:
    seeds = jax.random.split(jax.random.key(seed), 13)
    return {
        "tokens": scatter_about(seeds[0], (SEQS, LEN, D), 1.0, 6.0, ((0, 32),)),
        "frames": scatter_about(seeds[1], (SEQS, FRAMES, D), 1.0, 6.0, ((0, 32),)),
        "cotangent": scatter_about(seeds[2], (SEQS, LEN, D), 1.0, 6.0, ((0, 32),)),
        "self_qkv": scatter_about(seeds[3], (3, D, D), D ** -0.5, 0.1875, ((1, 4),)),
        "self_out": scatter_about(seeds[4], (D, D), (D // 16) ** -0.5, 0.75, ((0, 4),)),
        "cross_qkv": scatter_about(seeds[5], (3, D, D), D ** -0.5, 0.1875, ((1, 4),)),
        "cross_out": scatter_about(seeds[6], (D, D), (D // 32) ** -0.5, 1.0, ((0, 4),)),
        "fc1_weight": scatter_about(seeds[7], (D, FF), D ** -0.5, 0.1875, ((0, 4),)),
        "fc2_weight": scatter_about(seeds[8], (FF, D), FF ** -0.5, 0.09375, ((0, 4),)),
        "gains": jnp.clip(1.0 + 0.18 * jax.random.normal(seeds[9], (3, D), jnp.float32), 0.099609375, 1.8984375).astype(jnp.bfloat16),
        "biases": scatter_about(seeds[10], (10, D), 0.5, 3.0, ((1, 4),)),
        "fc1_bias": scatter_about(seeds[11], (FF,), 0.5, 3.0, ((0, 4),)),
    }


@jax.custom_vjp
def low(v):
    return lax.optimization_barrier(v.astype(jnp.bfloat16)).astype(jnp.float32)

@jax.custom_vjp
def low_back(v):
    return v

def low_keep(v):
    return (low(v), None)

def low_pass(kept, grad):
    return (grad,)

def back_keep(v):
    return (v, None)

def back_low(kept, grad):
    return (low(grad),)
low.defvjp(low_keep, low_pass)
low_back.defvjp(back_keep, back_low)
EPSILON = 1e-05
HIGHEST = lax.Precision.HIGHEST

def layer_norm(values, gain, shift):
    center = values - lax.optimization_barrier(jnp.mean(values, axis=-1, keepdims=True))
    spread = lax.optimization_barrier(jnp.mean(center * center, axis=-1, keepdims=True))
    return center * lax.rsqrt(spread + EPSILON) * gain + shift

def project(rows, weight):
    return jnp.einsum('bld,de->ble', rows, weight, precision=HIGHEST)

def attend(queries, keys, values, masked):
    batch, length, width = queries.shape
    query_heads = queries.reshape(batch, length, HEADS, width // HEADS)
    key_heads = keys.reshape(batch, keys.shape[1], HEADS, width // HEADS)
    value_heads = values.reshape(batch, keys.shape[1], HEADS, width // HEADS)
    scores = low_back(jnp.einsum('bqhd,bkhd->bhqk', query_heads, key_heads, precision=HIGHEST))
    if masked:
        rows_idx = lax.broadcasted_iota(jnp.int32, (length, keys.shape[1]), 0)
        cols_idx = lax.broadcasted_iota(jnp.int32, (length, keys.shape[1]), 1)
        scores = jnp.where(rows_idx >= cols_idx, scores, -jnp.inf)
    probs = low(jax.nn.softmax(scores, axis=-1))
    mixed = jnp.einsum('bhqk,bkhd->bqhd', probs, value_heads, precision=HIGHEST)
    return low(low_back(mixed.reshape(batch, length, width)))

def forward(params, tokens, frames):
    self_qkv, self_out, cross_qkv, cross_out, fc1_weight, fc2_weight, gains, biases, fc1_bias = params
    scale = 1.0 / math.sqrt(HEAD_DIM)
    normed1 = low(layer_norm(tokens, gains[0], biases[0]))
    query1 = low(low_back((project(normed1, self_qkv[0]) + biases[1]) * scale))
    key1 = low(low_back(project(normed1, self_qkv[1])))
    value1 = low(low_back(project(normed1, self_qkv[2]) + biases[2]))
    mixed1 = attend(query1, key1, value1, True)
    resid1 = tokens + low_back(project(mixed1, self_out) + biases[3])
    normed2 = low(layer_norm(resid1, gains[1], biases[4]))
    query2 = low(low_back((project(normed2, cross_qkv[0]) + biases[5]) * scale))
    key2 = low(low_back(project(frames, cross_qkv[1])))
    value2 = low(low_back(project(frames, cross_qkv[2]) + biases[6]))
    mixed2 = attend(query2, key2, value2, False)
    resid2 = resid1 + low_back(project(mixed2, cross_out) + biases[7])
    normed3 = low(layer_norm(resid2, gains[2], biases[8]))
    hidden_pre = low_back(project(normed3, fc1_weight) + fc1_bias)
    hidden = low(jax.nn.gelu(hidden_pre, approximate=False))
    return resid2 + low_back(project(hidden, fc2_weight) + biases[9])

def reference(tokens, frames, cotangent, self_qkv, self_out, cross_qkv, cross_out, fc1_weight, fc2_weight, gains, biases, fc1_bias):
    params = tuple((item.astype(jnp.float32) for item in (self_qkv, self_out, cross_qkv, cross_out, fc1_weight, fc2_weight, gains, biases, fc1_bias)))
    count = math.gcd(SEQS, 8)
    blocks = SEQS // count
    tok_blocks = tokens.astype(jnp.float32).reshape(blocks, count, LEN, D)
    frame_blocks = frames.astype(jnp.float32).reshape(blocks, count, FRAMES, D)
    cot_blocks = cotangent.astype(jnp.float32).reshape(blocks, count, LEN, D)

    def step(total, item):
        tok_part, frame_part, cot_part = item
        result, pullback = jax.vjp(forward, params, tok_part, frame_part)
        grads, grad_tok, grad_frame = pullback(cot_part)
        total = jax.tree.map(lambda left, right: left + right, total, grads)
        return (total, (result, grad_tok, grad_frame))
    start = jax.tree.map(jnp.zeros_like, params)
    total, (results, grad_toks, grad_frames) = lax.scan(step, start, (tok_blocks, frame_blocks, cot_blocks))
    return (results.reshape(SEQS, LEN, D).astype(jnp.bfloat16), grad_toks.reshape(SEQS, LEN, D), grad_frames.reshape(SEQS, FRAMES, D), total[0], total[1], total[2], total[3], total[4], total[5], total[6], total[7], total[8])
```

```python
from functools import partial
import math

import jax
import jax.numpy as jnp
from jax import lax
from jax.experimental import pallas as pl
from jax.experimental.pallas import tpu as pltpu
from jax.sharding import PartitionSpec as P

HEADS = 16
HEAD_DIM = 64


EPSILON = 1e-05


def layer_norm(values, gain, shift):
    center = values - jnp.mean(values, axis=-1, keepdims=True)
    spread = jnp.mean(center * center, axis=-1, keepdims=True)
    return center * lax.rsqrt(spread + EPSILON) * gain + shift


def norm_back(values, gain, shift, grad):
    result, pullback = jax.vjp(layer_norm, values, gain, shift)
    return pullback(grad)


def dense(left, right):
    return jnp.dot(left, right, preferred_element_type=jnp.float32)


def left_dense(left, right):
    return lax.dot_general(
        left, right, (((0,), (0,)), ((), ())), preferred_element_type=jnp.float32
    )


def right_dense(grad, weight):
    return lax.dot_general(
        grad, weight, (((1,), (1,)), ((), ())), preferred_element_type=jnp.float32
    )


def column_sum(values):
    return jnp.sum(values.astype(jnp.float32), axis=0)


def split_heads(rows, batch):
    return rows.reshape(batch, -1, HEADS, rows.shape[-1] // HEADS)


def scores_of(query_heads, key_heads, masked):
    scores = jnp.einsum(
        "bqhd,bkhd->bhqk", query_heads, key_heads, preferred_element_type=jnp.float32
    )
    if masked:
        shape = (query_heads.shape[1], key_heads.shape[1])
        allowed = lax.broadcasted_iota(jnp.int32, shape, 0) >= lax.broadcasted_iota(
            jnp.int32, shape, 1
        )
        scores = jnp.where(allowed, scores, -jnp.inf)
    return scores


def attend(queries, keys, values, batch, masked):
    query_heads = split_heads(queries, batch)
    key_heads = split_heads(keys, batch)
    value_heads = split_heads(values, batch)
    scores = scores_of(query_heads, key_heads, masked)
    highest = jnp.max(scores, axis=-1, keepdims=True)
    expo = jnp.exp(scores - highest)
    total = jnp.sum(expo, axis=-1, keepdims=True)
    probs = (expo / total).astype(jnp.bfloat16)
    mixed = jnp.einsum("bhqk,bkhd->bqhd", probs, value_heads, preferred_element_type=jnp.float32)
    return (mixed.reshape(queries.shape).astype(jnp.bfloat16), highest + jnp.log(total))


def attend_back(queries, keys, values, grad_mixed, logsum, batch, masked):
    query_heads = split_heads(queries, batch)
    key_heads = split_heads(keys, batch)
    value_heads = split_heads(values, batch)
    grad_heads = split_heads(grad_mixed, batch)
    probs = jnp.exp(scores_of(query_heads, key_heads, masked) - logsum)
    probs_low = probs.astype(jnp.bfloat16)
    grad_probs = jnp.einsum(
        "bqhd,bkhd->bhqk", grad_heads, value_heads, preferred_element_type=jnp.float32
    )
    grad_values = jnp.einsum(
        "bhqk,bqhd->bkhd", probs_low, grad_heads, preferred_element_type=jnp.float32
    )
    center = jnp.sum(probs * grad_probs, axis=-1, keepdims=True)
    grad_scores = (probs * (grad_probs - center)).astype(jnp.bfloat16)
    grad_queries = jnp.einsum(
        "bhqk,bkhd->bqhd", grad_scores, key_heads, preferred_element_type=jnp.float32
    )
    grad_keys = jnp.einsum(
        "bhqk,bqhd->bkhd", grad_scores, query_heads, preferred_element_type=jnp.float32
    )
    return (
        grad_queries.reshape(queries.shape),
        grad_keys.reshape(keys.shape),
        grad_values.reshape(keys.shape),
    )


def forward(tokens, frames, weights):
    self_qkv, self_out, cross_qkv, cross_out, fc1_weight, fc2_weight, gains, biases, fc1_bias = (
        weights
    )
    batch = tokens.shape[0]
    width = tokens.shape[2]
    scale = 1.0 / math.sqrt(HEAD_DIM)
    gain_rows = gains.astype(jnp.float32)
    bias_rows = biases.astype(jnp.float32)
    resid0 = tokens.reshape(-1, width).astype(jnp.float32)
    frame_rows = frames.reshape(-1, width)
    normed1 = layer_norm(resid0, gain_rows[0], bias_rows[0]).astype(jnp.bfloat16)
    query1 = ((dense(normed1, self_qkv[0]) + bias_rows[1]) * scale).astype(jnp.bfloat16)
    key1 = dense(normed1, self_qkv[1]).astype(jnp.bfloat16)
    value1 = (dense(normed1, self_qkv[2]) + bias_rows[2]).astype(jnp.bfloat16)
    mixed1, logsum1 = attend(query1, key1, value1, batch, True)
    resid1 = resid0 + dense(mixed1, self_out) + bias_rows[3]
    normed2 = layer_norm(resid1, gain_rows[1], bias_rows[4]).astype(jnp.bfloat16)
    query2 = ((dense(normed2, cross_qkv[0]) + bias_rows[5]) * scale).astype(jnp.bfloat16)
    key2 = dense(frame_rows, cross_qkv[1]).astype(jnp.bfloat16)
    value2 = (dense(frame_rows, cross_qkv[2]) + bias_rows[6]).astype(jnp.bfloat16)
    mixed2, logsum2 = attend(query2, key2, value2, batch, False)
    resid2 = resid1 + dense(mixed2, cross_out) + bias_rows[7]
    normed3 = layer_norm(resid2, gain_rows[2], bias_rows[8]).astype(jnp.bfloat16)
    hidden_pre = dense(normed3, fc1_weight) + fc1_bias.astype(jnp.float32)
    hidden = jax.nn.gelu(hidden_pre, approximate=False).astype(jnp.bfloat16)
    result = resid2 + dense(hidden, fc2_weight) + bias_rows[9]
    saved = (
        resid0,
        frame_rows,
        normed1,
        query1,
        key1,
        value1,
        mixed1,
        logsum1,
        resid1,
        normed2,
        query2,
        key2,
        value2,
        mixed2,
        logsum2,
        resid2,
        normed3,
        hidden_pre,
        hidden,
    )
    return (result, saved)


def backward(cotangent, weights, saved, settle_mlp, settle_cross, settle_self):
    self_qkv, self_out, cross_qkv, cross_out, fc1_weight, fc2_weight, gains, biases, fc1_bias = (
        weights
    )
    (
        resid0,
        frame_rows,
        normed1,
        query1,
        key1,
        value1,
        mixed1,
        logsum1,
        resid1,
        normed2,
        query2,
        key2,
        value2,
        mixed2,
        logsum2,
        resid2,
        normed3,
        hidden_pre,
        hidden,
    ) = saved
    batch = cotangent.shape[0]
    width = cotangent.shape[2]
    scale = 1.0 / math.sqrt(HEAD_DIM)
    gain_rows = gains.astype(jnp.float32)
    bias_rows = biases.astype(jnp.float32)
    grad_out = cotangent.reshape(-1, width).astype(jnp.float32)
    grad_branch3 = grad_out.astype(jnp.bfloat16)
    fc2_grad = left_dense(hidden, grad_branch3)
    bias9 = column_sum(grad_branch3)
    grad_hidden = right_dense(grad_branch3, fc2_weight)
    unused, gelu_pull = jax.vjp(partial(jax.nn.gelu, approximate=False), hidden_pre)
    grad_pre = gelu_pull(grad_hidden)[0].astype(jnp.bfloat16)
    fc1_grad = left_dense(normed3, grad_pre)
    fc1_bias_grad = column_sum(grad_pre)
    mlp_part = settle_mlp((fc1_grad, fc2_grad, fc1_bias_grad))
    grad_resid2, gain3, shift3 = norm_back(
        resid2, gain_rows[2], bias_rows[8], right_dense(grad_pre, fc1_weight)
    )
    grad_resid2 = grad_out + grad_resid2
    grad_branch2 = grad_resid2.astype(jnp.bfloat16)
    cross_out_grad = left_dense(mixed2, grad_branch2)
    bias7 = column_sum(grad_branch2)
    grad_mixed2 = right_dense(grad_branch2, cross_out).astype(jnp.bfloat16)
    grad_q2, grad_k2, grad_v2 = attend_back(
        query2, key2, value2, grad_mixed2, logsum2, batch, False
    )
    grad_q2 = (grad_q2.astype(jnp.bfloat16).astype(jnp.float32) * scale).astype(jnp.bfloat16)
    grad_k2 = grad_k2.astype(jnp.bfloat16)
    grad_v2 = grad_v2.astype(jnp.bfloat16)
    cross_qkv_grad = [
        left_dense(normed2, grad_q2),
        left_dense(frame_rows, grad_k2),
        left_dense(frame_rows, grad_v2),
    ]
    bias5 = column_sum(grad_q2)
    bias6 = column_sum(grad_v2)
    cross_part = settle_cross((cross_qkv_grad, cross_out_grad))
    grad_frames = right_dense(grad_k2, cross_qkv[1]) + right_dense(grad_v2, cross_qkv[2])
    grad_resid1, gain2, shift2 = norm_back(
        resid1, gain_rows[1], bias_rows[4], right_dense(grad_q2, cross_qkv[0])
    )
    grad_resid1 = grad_resid2 + grad_resid1
    grad_branch1 = grad_resid1.astype(jnp.bfloat16)
    self_out_grad = left_dense(mixed1, grad_branch1)
    bias3 = column_sum(grad_branch1)
    grad_mixed1 = right_dense(grad_branch1, self_out).astype(jnp.bfloat16)
    grad_q1, grad_k1, grad_v1 = attend_back(query1, key1, value1, grad_mixed1, logsum1, batch, True)
    grad_q1 = (grad_q1.astype(jnp.bfloat16).astype(jnp.float32) * scale).astype(jnp.bfloat16)
    grad_k1 = grad_k1.astype(jnp.bfloat16)
    grad_v1 = grad_v1.astype(jnp.bfloat16)
    self_qkv_grad = [
        left_dense(normed1, grad_q1),
        left_dense(normed1, grad_k1),
        left_dense(normed1, grad_v1),
    ]
    bias1 = column_sum(grad_q1)
    bias2 = column_sum(grad_v1)
    grad_normed1 = (
        right_dense(grad_q1, self_qkv[0])
        + right_dense(grad_k1, self_qkv[1])
        + right_dense(grad_v1, self_qkv[2])
    )
    grad_resid0, gain1, shift1 = norm_back(resid0, gain_rows[0], bias_rows[0], grad_normed1)
    grad_tokens = grad_resid1 + grad_resid0
    gains_grad = jnp.stack([gain1, gain2, gain3])
    biases_grad = jnp.stack(
        [shift1, bias1, bias2, bias3, shift2, bias5, bias6, bias7, shift3, bias9]
    )
    self_part = settle_self((self_qkv_grad, self_out_grad, gains_grad, biases_grad))
    return (grad_tokens, grad_frames, mlp_part, cross_part, self_part)


def unchanged(grads):
    return grads


def shards_any(
    tokens,
    frames,
    cotangent,
    self_qkv,
    self_out,
    cross_qkv,
    cross_out,
    fc1_weight,
    fc2_weight,
    gains,
    biases,
    fc1_bias,
):
    weights = (
        lax.all_gather(self_qkv, "group", axis=1, tiled=True),
        lax.all_gather(self_out, "group", axis=0, tiled=True),
        lax.all_gather(cross_qkv, "group", axis=1, tiled=True),
        lax.all_gather(cross_out, "group", axis=0, tiled=True),
        lax.all_gather(fc1_weight, "group", axis=0, tiled=True),
        lax.all_gather(fc2_weight, "group", axis=0, tiled=True),
        lax.all_gather(gains, "group", axis=1, tiled=True),
        lax.all_gather(biases, "group", axis=1, tiled=True),
        lax.all_gather(fc1_bias, "group", axis=0, tiled=True),
    )
    result, saved = forward(tokens, frames, weights)
    grad_tokens, grad_frames, mlp_part, cross_part, self_part = backward(
        cotangent, weights, saved, unchanged, unchanged, unchanged
    )
    shares = (
        lax.psum_scatter(
            jnp.stack(self_part[0]).astype(jnp.bfloat16), "group", scatter_dimension=1, tiled=True
        ).astype(jnp.float32),
        lax.psum_scatter(
            self_part[1].astype(jnp.bfloat16), "group", scatter_dimension=0, tiled=True
        ).astype(jnp.float32),
        lax.psum_scatter(
            jnp.stack(cross_part[0]).astype(jnp.bfloat16), "group", scatter_dimension=1, tiled=True
        ).astype(jnp.float32),
        lax.psum_scatter(
            cross_part[1].astype(jnp.bfloat16), "group", scatter_dimension=0, tiled=True
        ).astype(jnp.float32),
        lax.psum_scatter(
            mlp_part[0].astype(jnp.bfloat16), "group", scatter_dimension=0, tiled=True
        ).astype(jnp.float32),
        lax.psum_scatter(
            mlp_part[1].astype(jnp.bfloat16), "group", scatter_dimension=0, tiled=True
        ).astype(jnp.float32),
        lax.psum_scatter(
            self_part[2].astype(jnp.bfloat16), "group", scatter_dimension=1, tiled=True
        ).astype(jnp.float32),
        lax.psum_scatter(
            self_part[3].astype(jnp.bfloat16), "group", scatter_dimension=1, tiled=True
        ).astype(jnp.float32),
        lax.psum_scatter(
            mlp_part[2].astype(jnp.bfloat16), "group", scatter_dimension=0, tiled=True
        ).astype(jnp.float32),
    )
    summed = (
        lax.psum(shares[0].astype(jnp.bfloat16), "replica").astype(jnp.float32),
        lax.psum(shares[1].astype(jnp.bfloat16), "replica").astype(jnp.float32),
        lax.psum(shares[2].astype(jnp.bfloat16), "replica").astype(jnp.float32),
        lax.psum(shares[3].astype(jnp.bfloat16), "replica").astype(jnp.float32),
        lax.psum(shares[4].astype(jnp.bfloat16), "replica").astype(jnp.float32),
        lax.psum(shares[5].astype(jnp.bfloat16), "replica").astype(jnp.float32),
        lax.psum(shares[6].astype(jnp.bfloat16), "replica").astype(jnp.float32),
        lax.psum(shares[7].astype(jnp.bfloat16), "replica").astype(jnp.float32),
        lax.psum(shares[8].astype(jnp.bfloat16), "replica").astype(jnp.float32),
    )
    (
        self_qkv_grad,
        self_out_grad,
        cross_qkv_grad,
        cross_out_grad,
        fc1_grad,
        fc2_grad,
        gains_grad,
        biases_grad,
        fc1_bias_grad,
    ) = summed
    return (
        result.reshape(tokens.shape).astype(jnp.bfloat16),
        grad_tokens.reshape(tokens.shape),
        grad_frames.reshape(frames.shape),
        self_qkv_grad,
        self_out_grad,
        cross_qkv_grad,
        cross_out_grad,
        fc1_grad,
        fc2_grad,
        gains_grad,
        biases_grad,
        fc1_bias_grad,
    )


MESH = pl.DeviceIdType.MESH
VMEM_LIMIT = 64 * 1024 * 1024 - 128 * 1024


class Spot:
    def __init__(self):
        self.g = lax.axis_index("group")
        self.r = lax.axis_index("replica")
        self.core = lax.rem(self.r, 2)
        self.z = lax.div(self.r, 2)
        self.zb = lax.rem(self.z, 2)
        self.gx = self.g + 1 - 2 * lax.rem(self.g, 2)
        self.gy = lax.rem(self.g + 2, 4)
        self.gd = self.gx + 2 - 4 * lax.div(self.gx, 2)
        self.rc = self.r + 1 - 2 * self.core
        self.rz = self.r + 2 - 4 * self.zb
        self.x_id = (self.gx, self.r)
        self.y_id = (self.gy, self.r)
        self.d_id = (self.gd, self.r)
        self.c_id = (self.g, self.rc)
        self.z_id = (self.g, self.rz)


def meet(*ids):
    barrier = pltpu.get_barrier_semaphore()
    for device in ids:
        pl.semaphore_signal(barrier, inc=1, device_id=device, device_id_type=MESH)
    pl.semaphore_wait(barrier, len(ids))


GATHER_CHUNKS = (
    [(0, m, 0, 256, 0, 1024, m != 0) for m in range(3)]
    + [(1, None, 0, 256, 0, 1024, False)]
    + [(2, m, 0, 256, 0, 1024, m != 0) for m in range(3)]
    + [(3, None, 0, 256, 0, 1024, False)]
    + [(4, None, 0, 256, 1024 * m, 1024, m != 3) for m in range(4)]
    + [(5, None, 256 * m, 256, 0, 1024, m != 3) for m in range(4)]
)
N_GATHER = len(GATHER_CHUNKS)


def gather_kernel(*refs):
    shards, small = refs[:6], refs[6]
    fulls, small_full = refs[7:13], refs[13]
    stages = refs[14:20]
    small_stage, load_sem, put_sem, send_sem, recv_sem, small_send, small_recv, small_local = refs[20:]
    at = Spot()
    partners = (at.x_id, at.y_id, at.d_id, at.c_id, at.z_id)

    loads = [pltpu.make_async_copy(shards[n], stages[n], load_sem.at[n]) for n in range(6)]
    small_load = pltpu.make_async_copy(small, small_stage, small_local.at[0])
    for load in loads:
        load.start()
    small_load.start()
    meet(*partners)
    small_copies = []
    for n, device in enumerate((at.x_id, at.y_id, at.d_id)):
        small_copies.append(
            pltpu.make_async_remote_copy(
                small, small_full.at[at.g], small_send.at[n], small_recv.at[n],
                device_id=device, device_id_type=MESH,
            )
        )

    def full(i, g, start, rows):
        n, lead, first, _, column, columns, _ = GATHER_CHUNKS[i]
        where = (g, pl.ds(first + start, rows), pl.ds(column, columns))
        return fulls[n].at[where if lead is None else (lead,) + where]

    def shard(i, start, rows):
        n, lead, first, _, column, columns, _ = GATHER_CHUNKS[i]
        where = (pl.ds(first + start, rows), pl.ds(column, columns))
        return shards[n].at[where if lead is None else (lead,) + where]

    def put(i, k, src, g, start, rows, device):
        return pltpu.make_async_remote_copy(
            src, full(i, g, start, rows), send_sem.at[i, k], recv_sem.at[i, k],
            device_id=device, device_id_type=MESH,
        )

    def plan(i):
        rows, split = GATHER_CHUNKS[i][3], GATHER_CHUNKS[i][6]
        half = rows // 2
        base = pl.multiple_of(at.core * half, half)
        core_base = base
        if split:
            half = half // 2
            base = pl.multiple_of(base + at.zb * half, half)
        quarter = half // 2
        moves = [
            put(i, 0, shard(i, base, half), at.g, base, half, at.x_id),
            put(i, 1, shard(i, base, half), at.g, base, half, at.y_id),
            put(i, 2, full(i, at.gy, base + quarter, quarter), at.gy, base + quarter, quarter, at.x_id),
            put(i, 3, full(i, at.gx, base, quarter), at.gx, base, quarter, at.y_id),
        ]
        for k, g in enumerate((at.gx, at.gy, at.gd)):
            moves.append(put(i, 4 + k, full(i, g, core_base, rows // 2), g, core_base, rows // 2, at.c_id))
        if split:
            for k, g in enumerate((at.gx, at.gy, at.gd)):
                moves.append(put(i, 7 + k, full(i, g, base, half), g, base, half, at.z_id))
        return moves, split

    plans = [plan(i) for i in range(N_GATHER)]
    puts = []

    def begin(i):
        moves, _ = plans[i]
        moves[0].start()
        moves[1].start()

    def second(i):
        moves, split = plans[i]
        moves[0].wait_recv()
        moves[1].wait_recv()
        moves[2].start()
        moves[3].start()
        for k in ((7, 8) if split else (4, 5)):
            moves[k].start()

    def third(i):
        moves, split = plans[i]
        moves[2].wait_recv()
        moves[3].wait_recv()
        moves[9 if split else 6].start()

    def fourth(i):
        moves, split = plans[i]
        if split:
            for k in (7, 8, 9):
                moves[k].wait_recv()
            for k in (4, 5, 6):
                moves[k].start()

    begin(0)
    begin(1)
    for copy in small_copies:
        copy.start()
    small_load.wait()
    small_put = pltpu.make_async_copy(small_stage, small_full.at[at.g], small_local.at[1])
    small_put.start()
    for n in range(6):
        loads[n].wait()
        where = (slice(None), at.g) if n in (0, 2) else (at.g,)
        own = pltpu.make_async_copy(stages[n], fulls[n].at[where], put_sem.at[n])
        own.start()
        puts.append(own)
    for i in range(N_GATHER + 2):
        if i < N_GATHER:
            second(i)
        if i + 2 < N_GATHER:
            begin(i + 2)
        if 0 <= i - 1 < N_GATHER:
            third(i - 1)
        if 0 <= i - 2 < N_GATHER:
            fourth(i - 2)
    for own in puts:
        own.wait()
    small_put.wait()
    for copy in small_copies:
        copy.wait()
    for moves, split in plans:
        for k in range(10 if split else 7):
            moves[k].wait_send()
        for k in (4, 5, 6):
            moves[k].wait_recv()


def gather_weights(self_qkv, self_out, cross_qkv, cross_out, fc1_weight, fc2_weight, small):
    shards = (self_qkv, self_out, cross_qkv, cross_out, fc1_weight, fc2_weight)
    shapes = []
    for array in shards:
        lead, tail = array.shape[:-2], array.shape[-2:]
        shapes.append(jax.ShapeDtypeStruct(lead + (4,) + tail, array.dtype))
    shapes.append(jax.ShapeDtypeStruct((4,) + small.shape, small.dtype))
    anywhere = pl.BlockSpec(memory_space=pl.ANY)
    outs = pl.pallas_call(
        gather_kernel,
        name="gather_weights",
        out_shape=shapes,
        in_specs=[anywhere] * 7,
        out_specs=[anywhere] * 7,
        scratch_shapes=[pltpu.VMEM(array.shape, array.dtype) for array in shards]
        + [
            pltpu.VMEM(small.shape, small.dtype),
            pltpu.SemaphoreType.DMA((6,)),
            pltpu.SemaphoreType.DMA((6,)),
            pltpu.SemaphoreType.DMA((N_GATHER, 10)),
            pltpu.SemaphoreType.DMA((N_GATHER, 10)),
            pltpu.SemaphoreType.DMA((3,)),
            pltpu.SemaphoreType.DMA((3,)),
            pltpu.SemaphoreType.DMA((2,)),
        ],
        compiler_params=pltpu.CompilerParams(
            collective_id=0, has_side_effects=True, vmem_limit_bytes=VMEM_LIMIT
        ),
    )(*shards, small)
    return outs


REDUCE_UNITS = (
    [(0, 256 * m, 0, 5, None) for m in range(4)]
    + [(1, 0, 1024 * m, 4, None) for m in range(4)]
    + [(2, 0, 0, 3, None)]
    + [(3 + m, 0, 0, 2, m) for m in range(3)]
    + [(6, 0, 0, 1, None)]
    + [(7 + m, 0, 0, 0, m) for m in range(3)]
)
N_REDUCE = len(REDUCE_UNITS)
RING = 4


def toggled(bit, flip):
    return bit + flip - 2 * bit * flip


class Lane:
    def __init__(self, own, other, one_a, one_b, in_a, in_b, two_a, two_b, fin_a, fin_b, acc, up, mid, za, zb, tot, fin, out):
        self.own, self.other = own, other
        self.one_a, self.one_b, self.in_a, self.in_b = one_a, one_b, in_a, in_b
        self.two_a, self.two_b, self.fin_a, self.fin_b = two_a, two_b, fin_a, fin_b
        self.acc, self.up, self.mid, self.za, self.zb, self.tot, self.fin, self.out = acc, up, mid, za, zb, tot, fin, out


def lane_shapes(units, ring, rows, columns, dtype):
    half, quarter = rows // 2, rows // 4
    return [
        pltpu.VMEM((ring, 4, half, columns), dtype),
        pltpu.VMEM((units, 4, half, columns), dtype),
        pltpu.VMEM((ring, 4, quarter, columns), dtype),
        pltpu.VMEM((ring, 4, quarter, columns), dtype),
        pltpu.VMEM((units, 2, quarter, columns), dtype),
        pltpu.VMEM((units, 2, quarter, columns), dtype),
        pltpu.VMEM((ring, quarter, columns), dtype),
        pltpu.VMEM((ring, quarter, columns), dtype),
        pltpu.VMEM((units, quarter, columns), dtype),
        pltpu.VMEM((units, quarter, columns), dtype),
        pltpu.VMEM((ring, half, columns), jnp.float32),
        pltpu.VMEM((ring, half, columns), dtype),
        pltpu.VMEM((ring, half, columns), dtype),
        pltpu.VMEM((units, half, columns), dtype),
        pltpu.VMEM((units, half, columns), dtype),
        pltpu.VMEM((ring, half, columns), dtype),
        pltpu.VMEM((units, half, columns), dtype),
        pltpu.VMEM((min(ring, 2), rows, columns), jnp.float32),
    ]


LANE_REFS = 18


def f32(value):
    return value.astype(jnp.float32)


def reduce_kernel(*refs):
    grads, small = refs[:10], refs[10]
    outs, small_out = refs[11:17], refs[17]
    wide = Lane(*refs[18 : 18 + LANE_REFS])
    thin = Lane(*refs[18 + LANE_REFS : 18 + 2 * LANE_REFS])
    load_sem, out_sem, send_sem, recv_sem = refs[18 + 2 * LANE_REFS :]
    at = Spot()
    bx, by = lax.rem(at.g, 2), lax.div(at.g, 2)
    middle = lax.div(at.z * (3 - at.z), 2)
    is_end, is_mid = middle == 0, middle == 1
    r_mid = at.r + middle * (6 - 4 * at.z) + (1 - middle) * (2 - 4 * at.zb)
    m_id = (at.g, r_mid)
    total = N_REDUCE + 1

    class Unit:
        def __init__(self, u):
            self.u = u
            self.small = u == 0
            if self.small:
                self.lane, self.n, rows = thin, 0, 32
                self.slot, self.out_slot = 0, 0
            else:
                self.lane, self.n, rows = wide, u - 1, 256
                self.slot, self.out_slot = self.n % RING, self.n % 2
            self.half, self.quarter = rows // 2, rows // 4
            lane, n, slot = self.lane, self.n, self.slot
            half = self.half

            def grad(start):
                if self.small:
                    return small.at[:, pl.ds(start, half), :]
                k, row, column = REDUCE_UNITS[n][:3]
                return grads[k].at[:, pl.ds(row + start, half), pl.ds(column, 1024)]

            mine = pl.multiple_of(at.core * half, half)
            theirs = pl.multiple_of((1 - at.core) * half, half)
            self.mine, self.theirs = mine, theirs
            self.load = pltpu.make_async_copy(grad(mine), lane.own.at[slot], load_sem.at[u])

            def move(k, src, dst, device):
                return pltpu.make_async_remote_copy(
                    src, dst, send_sem.at[u, k], recv_sem.at[u, k], device_id=device, device_id_type=MESH
                )

            self.core = move(0, grad(theirs), lane.other.at[n], at.c_id)
            self.one_a = move(1, lane.one_a.at[slot, pl.ds(2, 2)], lane.in_a.at[n], at.x_id)
            self.one_b = move(2, lane.one_b.at[slot, pl.ds(2, 2)], lane.in_b.at[n], at.y_id)
            self.two_a = move(3, lane.two_a.at[slot], lane.fin_a.at[n], at.y_id)
            self.two_b = move(4, lane.two_b.at[slot], lane.fin_b.at[n], at.x_id)
            self.up = move(5, lane.up.at[slot], lane.za.at[n], at.z_id)
            self.mid = move(6, lane.mid.at[slot], lane.zb.at[n], m_id)
            self.down = move(7, lane.tot.at[slot], lane.za.at[n], at.z_id)
            self.fin_mid = move(8, lane.tot.at[slot], lane.fin.at[n], at.c_id)
            self.fin_end = move(8, lane.za.at[n], lane.fin.at[n], at.c_id)
            if self.small:
                target = small_out
            else:
                k, lead = REDUCE_UNITS[n][3:]
                target = outs[k]
                if lead is not None:
                    target = target.at[lead]
                row, column = REDUCE_UNITS[n][1:3]
                target = target.at[pl.ds(row, 256), pl.ds(column, 1024)]
            self.store = pltpu.make_async_copy(lane.out.at[self.out_slot], target, out_sem.at[u])

    units = [Unit(u) for u in range(total)]

    def before(u):
        return units[u - RING] if u - RING >= 1 else None

    def begin(u):
        units[u].core.start()
        units[u].load.start()

    def join(u):
        unit, lane = units[u], units[u].lane
        unit.core.wait_recv()
        unit.load.wait()
        old = before(u)
        if old is not None:
            old.one_a.wait_send()
            old.one_b.wait_send()
        q, s, n = unit.quarter, unit.slot, unit.n

        def body(j, carry):
            first, second = lax.rem(j, 2), lax.div(j, 2)
            ga = toggled(bx, second) + 2 * toggled(by, first)
            gb = toggled(bx, first) + 2 * toggled(by, second)
            dtype = lane.one_a.dtype
            lane.one_a[s, j] = (f32(lane.own[s, ga, 0:q]) + f32(lane.other[n, ga, 0:q])).astype(dtype)
            lane.one_b[s, j] = (f32(lane.own[s, gb, q : 2 * q]) + f32(lane.other[n, gb, q : 2 * q])).astype(dtype)
            return carry

        lax.fori_loop(0, 4, body, 0)
        unit.one_a.start()
        unit.one_b.start()

    def cross(u):
        unit, lane = units[u], units[u].lane
        unit.one_a.wait_recv()
        unit.one_b.wait_recv()
        old = before(u)
        if old is not None:
            old.two_a.wait_send()
            old.two_b.wait_send()
        q, s, n = unit.quarter, unit.slot, unit.n
        dtype = lane.one_a.dtype
        lane.two_a[s] = (f32(lane.one_a[s, 1]) + f32(lane.in_a[n, 1])).astype(dtype)
        lane.two_b[s] = (f32(lane.one_b[s, 1]) + f32(lane.in_b[n, 1])).astype(dtype)
        unit.two_a.start()
        unit.two_b.start()
        lane.acc[s, 0:q] = f32(lane.one_a[s, 0]) + f32(lane.in_a[n, 0])
        lane.acc[s, q : 2 * q] = f32(lane.one_b[s, 0]) + f32(lane.in_b[n, 0])

    def close(u):
        unit, lane = units[u], units[u].lane
        unit.two_a.wait_recv()
        unit.two_b.wait_recv()
        old = before(u)
        q, s, n = unit.quarter, unit.slot, unit.n
        dtype = lane.one_a.dtype

        @pl.when(is_end)
        def _():
            if old is not None:
                old.up.wait_send()
            lane.up[s, 0:q] = (lane.acc[s, 0:q] + f32(lane.fin_a[n])).astype(dtype)
            lane.up[s, q : 2 * q] = (lane.acc[s, q : 2 * q] + f32(lane.fin_b[n])).astype(dtype)
            unit.up.start()

        @pl.when(is_mid)
        def _():
            lane.acc[s, 0:q] = lane.acc[s, 0:q] + f32(lane.fin_a[n])
            lane.acc[s, q : 2 * q] = lane.acc[s, q : 2 * q] + f32(lane.fin_b[n])

    def climb(u):
        unit, lane = units[u], units[u].lane
        old = before(u)
        s, n = unit.slot, unit.n

        @pl.when(is_mid)
        def _():
            unit.up.wait_recv()
            if old is not None:
                old.mid.wait_send()
            lane.mid[s] = (lane.acc[s] + f32(lane.za[n])).astype(lane.mid.dtype)
            unit.mid.start()

    def peak(u):
        unit, lane = units[u], units[u].lane
        old = before(u)
        s, n = unit.slot, unit.n

        @pl.when(is_mid)
        def _():
            unit.mid.wait_recv()
            if old is not None:
                old.down.wait_send()
                old.fin_mid.wait_send()
            lane.tot[s] = (f32(lane.mid[s]) + f32(lane.zb[n])).astype(lane.tot.dtype)
            unit.down.start()
            unit.fin_mid.start()

    def land(u):
        unit = units[u]

        @pl.when(is_end)
        def _():
            unit.down.wait_recv()
            unit.fin_end.start()

    def finish(u):
        unit, lane = units[u], units[u].lane
        s, n, o, h = unit.slot, unit.n, unit.out_slot, unit.half
        unit.fin_mid.wait_recv()
        if not unit.small and unit.n >= 2:
            units[u - 2].store.wait()

        @pl.when(is_mid)
        def _():
            lane.out[o, pl.ds(unit.mine, h)] = f32(lane.tot[s])

        @pl.when(is_end)
        def _():
            lane.out[o, pl.ds(unit.mine, h)] = f32(lane.za[n])

        lane.out[o, pl.ds(unit.theirs, h)] = f32(lane.fin[n])
        unit.store.start()

    barrier = pltpu.get_barrier_semaphore()
    for device in (at.x_id, at.y_id, at.c_id, at.z_id):
        pl.semaphore_signal(barrier, inc=1, device_id=device, device_id_type=MESH)

    @pl.when(is_mid)
    def _():
        pl.semaphore_signal(barrier, inc=1, device_id=m_id, device_id_type=MESH)

    pl.semaphore_wait(barrier, 4 + middle)
    begin(0)
    begin(1)
    stages = (begin, join, cross, close, climb, peak, land, finish)
    lags = (0, 1, 2, 3, 4, 5, 6, 7)
    for t in range(total + lags[-1]):
        for stage, lag in zip(stages, lags):
            u = t - lag
            if 0 <= u < total and not (stage is begin and u < 2):
                stage(u)
    for u in range(total):
        unit = units[u]
        unit.core.wait_send()
        if u == 0 or u + RING >= total:
            for move in (unit.one_a, unit.one_b, unit.two_a, unit.two_b):
                move.wait_send()

            @pl.when(is_end)
            def _():
                unit.up.wait_send()

            @pl.when(is_mid)
            def _():
                unit.mid.wait_send()
                unit.down.wait_send()
                unit.fin_mid.wait_send()

        @pl.when(is_end)
        def _():
            unit.fin_end.wait_send()

        if u == 0 or u + 2 >= total:
            unit.store.wait()


def reduce_grads(grads, small):
    anywhere = pl.BlockSpec(memory_space=pl.ANY)
    d = grads[2].shape[-1]
    out_shape = [
        jax.ShapeDtypeStruct((3, 256, d), jnp.float32),
        jax.ShapeDtypeStruct((256, d), jnp.float32),
        jax.ShapeDtypeStruct((3, 256, d), jnp.float32),
        jax.ShapeDtypeStruct((256, d), jnp.float32),
        jax.ShapeDtypeStruct((256, 4 * d), jnp.float32),
        jax.ShapeDtypeStruct((d, d), jnp.float32),
        jax.ShapeDtypeStruct((32, 256), jnp.float32),
    ]
    return pl.pallas_call(
        reduce_kernel,
        name="reduce_grads",
        out_shape=out_shape,
        in_specs=[anywhere] * 11,
        out_specs=[anywhere] * 7,
        scratch_shapes=lane_shapes(N_REDUCE, RING, 256, 1024, jnp.bfloat16)
        + lane_shapes(1, 1, 32, 256, jnp.float32)
        + [
            pltpu.SemaphoreType.DMA((N_REDUCE + 1,)),
            pltpu.SemaphoreType.DMA((N_REDUCE + 1,)),
            pltpu.SemaphoreType.DMA((N_REDUCE + 1, 9)),
            pltpu.SemaphoreType.DMA((N_REDUCE + 1, 9)),
        ],
        compiler_params=pltpu.CompilerParams(
            collective_id=1, has_side_effects=True, vmem_limit_bytes=VMEM_LIMIT
        ),
    )(*grads, small)

def shards_here(
    tokens,
    frames,
    cotangent,
    self_qkv,
    self_out,
    cross_qkv,
    cross_out,
    fc1_weight,
    fc2_weight,
    gains,
    biases,
    fc1_bias,
):
    part = gains.shape[1]
    small = jnp.concatenate(
        [gains, biases, fc1_bias.reshape(4, part), jnp.zeros((15, part), jnp.bfloat16)], axis=0
    )
    full = gather_weights(self_qkv, self_out, cross_qkv, cross_out, fc1_weight, fc2_weight, small)
    width = tokens.shape[2]
    small_rows = full[6]
    weights = (
        full[0].reshape(3, width, width),
        full[1].reshape(width, width),
        full[2].reshape(3, width, width),
        full[3].reshape(width, width),
        full[4].reshape(width, -1),
        full[5].reshape(-1, width),
        small_rows[:, 0:3].transpose(1, 0, 2).reshape(3, width),
        small_rows[:, 3:13].transpose(1, 0, 2).reshape(10, width),
        small_rows[:, 13:17].reshape(-1),
    )
    result, saved = forward(tokens, frames, weights)
    grad_tokens, grad_frames, mlp_part, cross_part, self_part = backward(
        cotangent, weights, saved, unchanged, unchanged, unchanged
    )
    low = jnp.bfloat16
    grads = (
        mlp_part[1].astype(low).reshape(4, width, width),
        mlp_part[0].astype(low).reshape(4, part, -1),
        cross_part[1].astype(low).reshape(4, part, width),
        *(grad.astype(low).reshape(4, part, width) for grad in cross_part[0]),
        self_part[1].astype(low).reshape(4, part, width),
        *(grad.astype(low).reshape(4, part, width) for grad in self_part[0]),
    )
    small_grads = jnp.concatenate(
        [
            self_part[2].reshape(3, 4, part).transpose(1, 0, 2),
            self_part[3].reshape(10, 4, part).transpose(1, 0, 2),
            mlp_part[2].reshape(4, 4, part),
            jnp.zeros((4, 15, part), jnp.float32),
        ],
        axis=1,
    )
    done = reduce_grads(grads, small_grads)
    return (
        result.reshape(tokens.shape).astype(jnp.bfloat16),
        grad_tokens.reshape(tokens.shape),
        grad_frames.reshape(frames.shape),
        *done[:6],
        done[6][0:3],
        done[6][3:13],
        done[6][13:17].reshape(-1),
    )


def solution(mesh):
    in_specs = (
        P(("group", "replica"), None, None),
        P(("group", "replica"), None, None),
        P(("group", "replica"), None, None),
        P(None, "group", None),
        P("group", None),
        P(None, "group", None),
        P("group", None),
        P("group", None),
        P("group", None),
        P(None, "group"),
        P(None, "group"),
        P("group"),
    )
    out_specs = (
        P(("group", "replica"), None, None),
        P(("group", "replica"), None, None),
        P(("group", "replica"), None, None),
        P(None, "group", None),
        P("group", None),
        P(None, "group", None),
        P("group", None),
        P("group", None),
        P("group", None),
        P(None, "group"),
        P(None, "group"),
        P("group"),
    )
    here = mesh.shape["group"] == 4 and mesh.shape["replica"] == 8
    body = shards_here if here else shards_any
    return jax.shard_map(body, mesh=mesh, in_specs=in_specs, out_specs=out_specs, check_vma=False)
```

```python
from functools import partial
import math

import jax
import jax.numpy as jnp
from jax import lax
from jax.experimental import pallas as pl
from jax.experimental.pallas import tpu as pltpu
from jax.sharding import PartitionSpec as P

HEADS = 16
HEAD_DIM = 64


EPSILON = 1e-05


def layer_norm(values, gain, shift):
    center = values - jnp.mean(values, axis=-1, keepdims=True)
    spread = jnp.mean(center * center, axis=-1, keepdims=True)
    return center * lax.rsqrt(spread + EPSILON) * gain + shift


def norm_back(values, gain, shift, grad):
    result, pullback = jax.vjp(layer_norm, values, gain, shift)
    return pullback(grad)


def dense(left, right):
    return jnp.dot(left, right, preferred_element_type=jnp.float32)


def left_dense(left, right):
    return lax.dot_general(
        left, right, (((0,), (0,)), ((), ())), preferred_element_type=jnp.float32
    )


def right_dense(grad, weight):
    return lax.dot_general(
        grad, weight, (((1,), (1,)), ((), ())), preferred_element_type=jnp.float32
    )


def column_sum(values):
    return jnp.sum(values.astype(jnp.float32), axis=0)


def split_heads(rows, batch):
    return rows.reshape(batch, -1, HEADS, rows.shape[-1] // HEADS)


def scores_of(query_heads, key_heads, masked):
    scores = jnp.einsum(
        "bqhd,bkhd->bhqk", query_heads, key_heads, preferred_element_type=jnp.float32
    )
    if masked:
        shape = (query_heads.shape[1], key_heads.shape[1])
        allowed = lax.broadcasted_iota(jnp.int32, shape, 0) >= lax.broadcasted_iota(
            jnp.int32, shape, 1
        )
        scores = jnp.where(allowed, scores, -jnp.inf)
    return scores


def attend(queries, keys, values, batch, masked):
    query_heads = split_heads(queries, batch)
    key_heads = split_heads(keys, batch)
    value_heads = split_heads(values, batch)
    scores = scores_of(query_heads, key_heads, masked)
    highest = jnp.max(scores, axis=-1, keepdims=True)
    expo = jnp.exp(scores - highest)
    total = jnp.sum(expo, axis=-1, keepdims=True)
    probs = (expo / total).astype(jnp.bfloat16)
    mixed = jnp.einsum("bhqk,bkhd->bqhd", probs, value_heads, preferred_element_type=jnp.float32)
    return (mixed.reshape(queries.shape).astype(jnp.bfloat16), highest + jnp.log(total))


def attend_back(queries, keys, values, grad_mixed, logsum, batch, masked):
    query_heads = split_heads(queries, batch)
    key_heads = split_heads(keys, batch)
    value_heads = split_heads(values, batch)
    grad_heads = split_heads(grad_mixed, batch)
    probs = jnp.exp(scores_of(query_heads, key_heads, masked) - logsum)
    probs_low = probs.astype(jnp.bfloat16)
    grad_probs = jnp.einsum(
        "bqhd,bkhd->bhqk", grad_heads, value_heads, preferred_element_type=jnp.float32
    )
    grad_values = jnp.einsum(
        "bhqk,bqhd->bkhd", probs_low, grad_heads, preferred_element_type=jnp.float32
    )
    center = jnp.sum(probs * grad_probs, axis=-1, keepdims=True)
    grad_scores = (probs * (grad_probs - center)).astype(jnp.bfloat16)
    grad_queries = jnp.einsum(
        "bhqk,bkhd->bqhd", grad_scores, key_heads, preferred_element_type=jnp.float32
    )
    grad_keys = jnp.einsum(
        "bhqk,bqhd->bkhd", grad_scores, query_heads, preferred_element_type=jnp.float32
    )
    return (
        grad_queries.reshape(queries.shape),
        grad_keys.reshape(keys.shape),
        grad_values.reshape(keys.shape),
    )


def forward(tokens, frames, weights):
    self_qkv, self_out, cross_qkv, cross_out, fc1_weight, fc2_weight, gains, biases, fc1_bias = (
        weights
    )
    batch = tokens.shape[0]
    width = tokens.shape[2]
    scale = 1.0 / math.sqrt(HEAD_DIM)
    gain_rows = gains.astype(jnp.float32)
    bias_rows = biases.astype(jnp.float32)
    resid0 = tokens.reshape(-1, width).astype(jnp.float32)
    frame_rows = frames.reshape(-1, width)
    normed1 = layer_norm(resid0, gain_rows[0], bias_rows[0]).astype(jnp.bfloat16)
    query1 = ((dense(normed1, self_qkv[0]) + bias_rows[1]) * scale).astype(jnp.bfloat16)
    key1 = dense(normed1, self_qkv[1]).astype(jnp.bfloat16)
    value1 = (dense(normed1, self_qkv[2]) + bias_rows[2]).astype(jnp.bfloat16)
    mixed1, logsum1 = attend(query1, key1, value1, batch, True)
    resid1 = resid0 + dense(mixed1, self_out) + bias_rows[3]
    normed2 = layer_norm(resid1, gain_rows[1], bias_rows[4]).astype(jnp.bfloat16)
    query2 = ((dense(normed2, cross_qkv[0]) + bias_rows[5]) * scale).astype(jnp.bfloat16)
    key2 = dense(frame_rows, cross_qkv[1]).astype(jnp.bfloat16)
    value2 = (dense(frame_rows, cross_qkv[2]) + bias_rows[6]).astype(jnp.bfloat16)
    mixed2, logsum2 = attend(query2, key2, value2, batch, False)
    resid2 = resid1 + dense(mixed2, cross_out) + bias_rows[7]
    normed3 = layer_norm(resid2, gain_rows[2], bias_rows[8]).astype(jnp.bfloat16)
    hidden_pre = dense(normed3, fc1_weight) + fc1_bias.astype(jnp.float32)
    hidden = jax.nn.gelu(hidden_pre, approximate=False).astype(jnp.bfloat16)
    result = resid2 + dense(hidden, fc2_weight) + bias_rows[9]
    saved = (
        resid0,
        frame_rows,
        normed1,
        query1,
        key1,
        value1,
        mixed1,
        logsum1,
        resid1,
        normed2,
        query2,
        key2,
        value2,
        mixed2,
        logsum2,
        resid2,
        normed3,
        hidden_pre,
        hidden,
    )
    return (result, saved)


def backward(cotangent, weights, saved, settle_mlp, settle_cross, settle_self, sloped=False):
    self_qkv, self_out, cross_qkv, cross_out, fc1_weight, fc2_weight, gains, biases, fc1_bias = (
        weights
    )
    (
        resid0,
        frame_rows,
        normed1,
        query1,
        key1,
        value1,
        mixed1,
        logsum1,
        resid1,
        normed2,
        query2,
        key2,
        value2,
        mixed2,
        logsum2,
        resid2,
        normed3,
        hidden_pre,
        hidden,
    ) = saved
    batch = cotangent.shape[0]
    width = cotangent.shape[2]
    scale = 1.0 / math.sqrt(HEAD_DIM)
    gain_rows = gains.astype(jnp.float32)
    bias_rows = biases.astype(jnp.float32)
    grad_out = cotangent.reshape(-1, width).astype(jnp.float32)
    grad_branch3 = grad_out.astype(jnp.bfloat16)
    fc2_grad = left_dense(hidden, grad_branch3)
    bias9 = column_sum(grad_branch3)
    grad_hidden = right_dense(grad_branch3, fc2_weight)
    if sloped:
        grad_pre = (grad_hidden * hidden_pre).astype(jnp.bfloat16)
    else:
        unused, gelu_pull = jax.vjp(partial(jax.nn.gelu, approximate=False), hidden_pre)
        grad_pre = gelu_pull(grad_hidden)[0].astype(jnp.bfloat16)
    fc1_grad = left_dense(normed3, grad_pre)
    fc1_bias_grad = column_sum(grad_pre)
    mlp_part = settle_mlp((fc1_grad, fc2_grad, fc1_bias_grad))
    grad_resid2, gain3, shift3 = norm_back(
        resid2, gain_rows[2], bias_rows[8], right_dense(grad_pre, fc1_weight)
    )
    grad_resid2 = grad_out + grad_resid2
    grad_branch2 = grad_resid2.astype(jnp.bfloat16)
    cross_out_grad = left_dense(mixed2, grad_branch2)
    bias7 = column_sum(grad_branch2)
    grad_mixed2 = right_dense(grad_branch2, cross_out).astype(jnp.bfloat16)
    grad_q2, grad_k2, grad_v2 = attend_back(
        query2, key2, value2, grad_mixed2, logsum2, batch, False
    )
    grad_q2 = (grad_q2.astype(jnp.bfloat16).astype(jnp.float32) * scale).astype(jnp.bfloat16)
    grad_k2 = grad_k2.astype(jnp.bfloat16)
    grad_v2 = grad_v2.astype(jnp.bfloat16)
    cross_qkv_grad = [
        left_dense(normed2, grad_q2),
        left_dense(frame_rows, grad_k2),
        left_dense(frame_rows, grad_v2),
    ]
    bias5 = column_sum(grad_q2)
    bias6 = column_sum(grad_v2)
    cross_part = settle_cross((cross_qkv_grad, cross_out_grad))
    grad_frames = right_dense(grad_k2, cross_qkv[1]) + right_dense(grad_v2, cross_qkv[2])
    grad_resid1, gain2, shift2 = norm_back(
        resid1, gain_rows[1], bias_rows[4], right_dense(grad_q2, cross_qkv[0])
    )
    grad_resid1 = grad_resid2 + grad_resid1
    grad_branch1 = grad_resid1.astype(jnp.bfloat16)
    self_out_grad = left_dense(mixed1, grad_branch1)
    bias3 = column_sum(grad_branch1)
    grad_mixed1 = right_dense(grad_branch1, self_out).astype(jnp.bfloat16)
    grad_q1, grad_k1, grad_v1 = attend_back(query1, key1, value1, grad_mixed1, logsum1, batch, True)
    grad_q1 = (grad_q1.astype(jnp.bfloat16).astype(jnp.float32) * scale).astype(jnp.bfloat16)
    grad_k1 = grad_k1.astype(jnp.bfloat16)
    grad_v1 = grad_v1.astype(jnp.bfloat16)
    self_qkv_grad = [
        left_dense(normed1, grad_q1),
        left_dense(normed1, grad_k1),
        left_dense(normed1, grad_v1),
    ]
    bias1 = column_sum(grad_q1)
    bias2 = column_sum(grad_v1)
    grad_normed1 = (
        right_dense(grad_q1, self_qkv[0])
        + right_dense(grad_k1, self_qkv[1])
        + right_dense(grad_v1, self_qkv[2])
    )
    grad_resid0, gain1, shift1 = norm_back(resid0, gain_rows[0], bias_rows[0], grad_normed1)
    grad_tokens = grad_resid1 + grad_resid0
    gains_grad = jnp.stack([gain1, gain2, gain3])
    biases_grad = jnp.stack(
        [shift1, bias1, bias2, bias3, shift2, bias5, bias6, bias7, shift3, bias9]
    )
    self_part = settle_self((self_qkv_grad, self_out_grad, gains_grad, biases_grad))
    return (grad_tokens, grad_frames, mlp_part, cross_part, self_part)


def unchanged(grads):
    return grads


def shards_any(
    tokens,
    frames,
    cotangent,
    self_qkv,
    self_out,
    cross_qkv,
    cross_out,
    fc1_weight,
    fc2_weight,
    gains,
    biases,
    fc1_bias,
):
    weights = (
        lax.all_gather(self_qkv, "group", axis=1, tiled=True),
        lax.all_gather(self_out, "group", axis=0, tiled=True),
        lax.all_gather(cross_qkv, "group", axis=1, tiled=True),
        lax.all_gather(cross_out, "group", axis=0, tiled=True),
        lax.all_gather(fc1_weight, "group", axis=0, tiled=True),
        lax.all_gather(fc2_weight, "group", axis=0, tiled=True),
        lax.all_gather(gains, "group", axis=1, tiled=True),
        lax.all_gather(biases, "group", axis=1, tiled=True),
        lax.all_gather(fc1_bias, "group", axis=0, tiled=True),
    )
    result, saved = forward(tokens, frames, weights)
    grad_tokens, grad_frames, mlp_part, cross_part, self_part = backward(
        cotangent, weights, saved, unchanged, unchanged, unchanged
    )
    shares = (
        lax.psum_scatter(
            jnp.stack(self_part[0]).astype(jnp.bfloat16), "group", scatter_dimension=1, tiled=True
        ).astype(jnp.float32),
        lax.psum_scatter(
            self_part[1].astype(jnp.bfloat16), "group", scatter_dimension=0, tiled=True
        ).astype(jnp.float32),
        lax.psum_scatter(
            jnp.stack(cross_part[0]).astype(jnp.bfloat16), "group", scatter_dimension=1, tiled=True
        ).astype(jnp.float32),
        lax.psum_scatter(
            cross_part[1].astype(jnp.bfloat16), "group", scatter_dimension=0, tiled=True
        ).astype(jnp.float32),
        lax.psum_scatter(
            mlp_part[0].astype(jnp.bfloat16), "group", scatter_dimension=0, tiled=True
        ).astype(jnp.float32),
        lax.psum_scatter(
            mlp_part[1].astype(jnp.bfloat16), "group", scatter_dimension=0, tiled=True
        ).astype(jnp.float32),
        lax.psum_scatter(
            self_part[2].astype(jnp.bfloat16), "group", scatter_dimension=1, tiled=True
        ).astype(jnp.float32),
        lax.psum_scatter(
            self_part[3].astype(jnp.bfloat16), "group", scatter_dimension=1, tiled=True
        ).astype(jnp.float32),
        lax.psum_scatter(
            mlp_part[2].astype(jnp.bfloat16), "group", scatter_dimension=0, tiled=True
        ).astype(jnp.float32),
    )
    summed = (
        lax.psum(shares[0].astype(jnp.bfloat16), "replica").astype(jnp.float32),
        lax.psum(shares[1].astype(jnp.bfloat16), "replica").astype(jnp.float32),
        lax.psum(shares[2].astype(jnp.bfloat16), "replica").astype(jnp.float32),
        lax.psum(shares[3].astype(jnp.bfloat16), "replica").astype(jnp.float32),
        lax.psum(shares[4].astype(jnp.bfloat16), "replica").astype(jnp.float32),
        lax.psum(shares[5].astype(jnp.bfloat16), "replica").astype(jnp.float32),
        lax.psum(shares[6].astype(jnp.bfloat16), "replica").astype(jnp.float32),
        lax.psum(shares[7].astype(jnp.bfloat16), "replica").astype(jnp.float32),
        lax.psum(shares[8].astype(jnp.bfloat16), "replica").astype(jnp.float32),
    )
    (
        self_qkv_grad,
        self_out_grad,
        cross_qkv_grad,
        cross_out_grad,
        fc1_grad,
        fc2_grad,
        gains_grad,
        biases_grad,
        fc1_bias_grad,
    ) = summed
    return (
        result.reshape(tokens.shape).astype(jnp.bfloat16),
        grad_tokens.reshape(tokens.shape),
        grad_frames.reshape(frames.shape),
        self_qkv_grad,
        self_out_grad,
        cross_qkv_grad,
        cross_out_grad,
        fc1_grad,
        fc2_grad,
        gains_grad,
        biases_grad,
        fc1_bias_grad,
    )


MESH = pl.DeviceIdType.MESH
VMEM_LIMIT = 64 * 1024 * 1024 - 128 * 1024


class Spot:
    def __init__(self):
        self.g = lax.axis_index("group")
        self.r = lax.axis_index("replica")
        self.core = lax.rem(self.r, 2)
        self.z = lax.div(self.r, 2)
        self.zb = lax.rem(self.z, 2)
        self.gx = self.g + 1 - 2 * lax.rem(self.g, 2)
        self.gy = lax.rem(self.g + 2, 4)
        self.gd = self.gx + 2 - 4 * lax.div(self.gx, 2)
        self.rc = self.r + 1 - 2 * self.core
        self.rz = self.r + 2 - 4 * self.zb
        self.x_id = (self.gx, self.r)
        self.y_id = (self.gy, self.r)
        self.d_id = (self.gd, self.r)
        self.c_id = (self.g, self.rc)
        self.z_id = (self.g, self.rz)


def meet(*ids):
    barrier = pltpu.get_barrier_semaphore()
    for device in ids:
        pl.semaphore_signal(barrier, inc=1, device_id=device, device_id_type=MESH)
    pl.semaphore_wait(barrier, len(ids))


GATHER_CHUNKS = (
    [(0, m, 0, 256, 0, 1024, m != 0) for m in range(3)]
    + [(1, None, 0, 256, 0, 1024, False)]
    + [(2, m, 0, 256, 0, 1024, m != 0) for m in range(3)]
    + [(3, None, 0, 256, 0, 1024, False)]
    + [(4, None, 0, 256, 1024 * m, 1024, m != 3) for m in range(4)]
    + [(5, None, 256 * m, 256, 0, 1024, m != 3) for m in range(4)]
)
N_GATHER = len(GATHER_CHUNKS)


class Gather:
    def __init__(self, at, shards, small, fulls, small_full, stages, small_stage, sems):
        self.load_sem, self.put_sem, self.send_sem, self.recv_sem, small_send, small_recv, small_local = sems
        self.at, self.shards, self.fulls = at, shards, fulls
        self.loads = [pltpu.make_async_copy(shards[n], stages[n], self.load_sem.at[n]) for n in range(6)]
        self.small_load = pltpu.make_async_copy(small, small_stage, small_local.at[0])
        self.small_put = pltpu.make_async_copy(small_stage, small_full.at[at.g], small_local.at[1])
        self.small_copies = [
            pltpu.make_async_remote_copy(
                small, small_full.at[at.g], small_send.at[n], small_recv.at[n],
                device_id=device, device_id_type=MESH,
            )
            for n, device in enumerate((at.x_id, at.y_id, at.d_id))
        ]
        self.puts = []
        for n in range(6):
            where = (slice(None), at.g) if n in (0, 2) else (at.g,)
            self.puts.append(pltpu.make_async_copy(stages[n], fulls[n].at[where], self.put_sem.at[n]))
        self.plans = [self.plan(i) for i in range(N_GATHER)]
        self.arrived, self.placed = set(), set()

    def full(self, i, g, start, rows):
        n, lead, first, _, column, columns, _ = GATHER_CHUNKS[i]
        where = (g, pl.ds(first + start, rows), pl.ds(column, columns))
        return self.fulls[n].at[where if lead is None else (lead,) + where]

    def shard(self, i, start, rows):
        n, lead, first, _, column, columns, _ = GATHER_CHUNKS[i]
        where = (pl.ds(first + start, rows), pl.ds(column, columns))
        return self.shards[n].at[where if lead is None else (lead,) + where]

    def plan(self, i):
        at = self.at

        def put(k, src, g, start, rows, device):
            return pltpu.make_async_remote_copy(
                src, self.full(i, g, start, rows), self.send_sem.at[i, k], self.recv_sem.at[i, k],
                device_id=device, device_id_type=MESH,
            )

        rows, split = GATHER_CHUNKS[i][3], GATHER_CHUNKS[i][6]
        half = rows // 2
        base = pl.multiple_of(at.core * half, half)
        core_base = base
        if split:
            half = half // 2
            base = pl.multiple_of(base + at.zb * half, half)
        quarter = half // 2
        mine = self.shard(i, base, half)
        moves = [
            put(0, mine, at.g, base, half, at.x_id),
            put(1, mine, at.g, base, half, at.y_id),
            put(2, self.full(i, at.gy, base + quarter, quarter), at.gy, base + quarter, quarter, at.x_id),
            put(3, self.full(i, at.gx, base, quarter), at.gx, base, quarter, at.y_id),
        ]
        for k, g in enumerate((at.gx, at.gy, at.gd)):
            moves.append(put(4 + k, self.full(i, g, core_base, rows // 2), g, core_base, rows // 2, at.c_id))
        if split:
            for k, g in enumerate((at.gx, at.gy, at.gd)):
                moves.append(put(7 + k, self.full(i, g, base, half), g, base, half, at.z_id))
        return moves, split

    def open(self):
        at = self.at
        for load in self.loads:
            load.start()
        self.small_load.start()
        meet(at.x_id, at.y_id, at.d_id, at.c_id, at.z_id)
        self.begin(0)
        for copy in self.small_copies:
            copy.start()
        self.begin(1)
        self.small_load.wait()
        self.small_put.start()
        for n in range(6):
            self.loads[n].wait()
            self.puts[n].start()

    def small_ready(self):
        self.small_put.wait()
        for copy in self.small_copies:
            copy.wait()

    def begin(self, i):
        moves, _ = self.plans[i]
        moves[0].start()
        moves[1].start()

    def second(self, i):
        moves, split = self.plans[i]
        moves[0].wait_recv()
        moves[1].wait_recv()
        moves[2].start()
        moves[3].start()
        for k in (7, 8) if split else (4, 5):
            moves[k].start()

    def third(self, i):
        moves, split = self.plans[i]
        moves[2].wait_recv()
        moves[3].wait_recv()
        moves[9 if split else 6].start()

    def fourth(self, i):
        moves, split = self.plans[i]
        if split:
            for k in (7, 8, 9):
                moves[k].wait_recv()
            for k in (4, 5, 6):
                moves[k].start()

    ticks = N_GATHER + 2

    def tick(self, i):
        if i < N_GATHER:
            self.second(i)
        if i + 2 < N_GATHER:
            self.begin(i + 2)
        if 0 <= i - 1 < N_GATHER:
            self.third(i - 1)
        if 0 <= i - 2 < N_GATHER:
            self.fourth(i - 2)

    def ready(self, i):
        n = GATHER_CHUNKS[i][0]
        if n not in self.placed:
            self.placed.add(n)
            self.puts[n].wait()
        if i not in self.arrived:
            self.arrived.add(i)
            for k in (4, 5, 6):
                self.plans[i][0][k].wait_recv()

    def close(self):
        for i in range(N_GATHER):
            self.ready(i)
            moves, split = self.plans[i]
            for k in range(10 if split else 7):
                moves[k].wait_send()


def f32(value):
    return value.astype(jnp.float32)


def dot(left, right):
    return jnp.dot(left, right, preferred_element_type=jnp.float32)


def dot_tn(left, right):
    return lax.dot_general(left, right, (((0,), (0,)), ((), ())), preferred_element_type=jnp.float32)


def dot_nt(left, right):
    return lax.dot_general(left, right, (((1,), (1,)), ((), ())), preferred_element_type=jnp.float32)


def loop(count, body):
    def step(i, carry):
        body(i)
        return carry

    lax.fori_loop(0, count, step, 0)


def cut(i, size):
    return pl.ds(pl.multiple_of(i * size, size), size)


def norm_rows(src, dst, gain, shift):
    def body(i):
        values = f32(src[cut(i, 32)])
        center = values - jnp.mean(values, axis=-1, keepdims=True)
        spread = jnp.mean(center * center, axis=-1, keepdims=True)
        dst[cut(i, 32)] = (center * lax.rsqrt(spread + EPSILON) * gain[...] + shift[...]).astype(dst.dtype)

    loop(src.shape[0] // 32, body)


def product(left, weight, store, tile=256):
    def body(j):
        columns = cut(j, tile)
        store(columns, dot(left[...], weight[:, :, columns].reshape(-1, tile)))

    loop(weight.shape[-1] // tile, body)


def attend_pair(p, q, k, v, o, lse, scores, probs, causal):
    columns = cut(p, 128)
    keys, count = k.shape[0], q.shape[0]
    qq, kk, vv = q[:, columns], k[:, columns], v[:, columns]
    lane = lax.broadcasted_iota(jnp.int32, qq.shape, 1)
    vt = vv.T
    block = 128
    sides = []
    for a in range(2):
        qa = jnp.where((lane < 64) if a == 0 else (lane >= 64), qq, jnp.zeros_like(qq))
        scores[...] = dot_nt(kk, qa)

        def rows_of(j):
            part = scores[cut(j, block)]
            if causal:
                key = lax.broadcasted_iota(jnp.int32, part.shape, 0) + j * block
                query = lax.broadcasted_iota(jnp.int32, part.shape, 1)
                part = jnp.where(query >= key, part, -jnp.inf)
            return part

        def top(j, carry):
            return jnp.maximum(carry, jnp.max(rows_of(j), axis=0, keepdims=True))

        highest = lax.fori_loop(0, keys // block, top, jnp.full((1, count), -jnp.inf, jnp.float32))

        def expo(j, carry):
            e = jnp.exp(rows_of(j) - highest)
            probs[cut(j, block)] = e.astype(probs.dtype)
            return carry + jnp.sum(e, axis=0, keepdims=True)

        total = lax.fori_loop(0, keys // block, expo, jnp.zeros((1, count), jnp.float32))
        lse[2 * p + a] = jnp.broadcast_to(highest + jnp.log(total), (8, count))
        sides.append(dot(vt[64 * a : 64 * a + 64], probs[...]) * (1.0 / total))
    o[:, columns] = jnp.concatenate(sides, axis=0).T.astype(o.dtype)


def attend_back_pair(p, q, k, v, go, lse, scores, gscores, probs, gs, gq, gk, gv, causal):
    columns = cut(p, 128)
    keys, count = k.shape[0], q.shape[0]
    qq, kk, vv, dd = q[:, columns], k[:, columns], v[:, columns], go[:, columns]
    lane = lax.broadcasted_iota(jnp.int32, qq.shape, 1)
    zero = jnp.zeros_like(qq)
    kt = kk.T
    block = 128
    sides, qs, ds = [], [], []
    for a in range(2):
        here = (lane < 64) if a == 0 else (lane >= 64)
        qa, da = jnp.where(here, qq, zero), jnp.where(here, dd, zero)
        qs.append(qa)
        ds.append(da)
        scores[...] = dot_nt(kk, qa)
        gscores[...] = dot_nt(vv, da)
        line = lse[2 * p + a][0:1]
        across = slice(a * count, (a + 1) * count)

        def first(j, carry):
            part = scores[cut(j, block)]
            if causal:
                key = lax.broadcasted_iota(jnp.int32, part.shape, 0) + j * block
                query = lax.broadcasted_iota(jnp.int32, part.shape, 1)
                part = jnp.where(query >= key, part, -jnp.inf)
            e = jnp.exp(part - line)
            scores[cut(j, block)] = e
            probs[cut(j, block), across] = e.astype(probs.dtype)
            return carry + jnp.sum(e * gscores[cut(j, block)], axis=0, keepdims=True)

        center = lax.fori_loop(0, keys // block, first, jnp.zeros((1, count), jnp.float32))

        def second(j):
            rows = cut(j, block)
            gs[rows, across] = (scores[rows] * (gscores[rows] - center)).astype(gs.dtype)

        loop(keys // block, second)
        sides.append(dot(kt[64 * a : 64 * a + 64], gs[:, across]))
    gv[:, columns] = dot(probs[...], jnp.concatenate(ds, axis=0)).astype(gv.dtype)
    gk[:, columns] = dot(gs[...], jnp.concatenate(qs, axis=0)).astype(gk.dtype)
    side = jnp.concatenate(sides, axis=0).T.astype(jnp.bfloat16)
    gq[:, columns] = (f32(side) * SCALE).astype(gq.dtype)

def woven(ticks, period, first, steps):
    order, now, tick = [], 0.0, 0
    left = list(range(len(steps)))
    while left or tick < ticks:
        due = first + tick * period
        if left and steps[left[0]][0] < tick and (now < due or tick >= ticks):
            now += steps[left[0]][1]
            order.append(("step", left.pop(0)))
        else:
            now = max(now, due)
            order.append(("tick", tick))
            tick += 1
    return order


ACTS = (
    [("n1", (256, 1024), jnp.bfloat16), ("q1", (256, 1024), jnp.bfloat16), ("k1", (256, 1024), jnp.bfloat16)]
    + [("v1", (256, 1024), jnp.bfloat16), ("o1", (256, 1024), jnp.bfloat16), ("lse1", (16, 8, 256), jnp.float32)]
    + [("h1", (256, 1024), jnp.float32), ("n2", (256, 1024), jnp.bfloat16), ("q2", (256, 1024), jnp.bfloat16)]
    + [("k2", (1024, 1024), jnp.bfloat16), ("v2", (1024, 1024), jnp.bfloat16), ("o2", (256, 1024), jnp.bfloat16)]
    + [("lse2", (16, 8, 256), jnp.float32), ("h2", (256, 1024), jnp.float32), ("n3", (256, 1024), jnp.bfloat16)]
    + [("slope", (4, 256, 1024), jnp.float32), ("g", (4, 256, 1024), jnp.bfloat16)]
)
N_ACTS = len(ACTS)
SCALE = 0.125


def set_rows(small_full, rows, hidden):
    for g in range(4):
        for k in range(13):
            rows[k : k + 1, 256 * g : 256 * g + 256] = f32(small_full[g, k : k + 1])
        for k in range(4):
            hidden[g : g + 1, 256 * k : 256 * k + 256] = f32(small_full[g, 13 + k : 14 + k])


def forward_kernel(*refs):
    shards, small, tokens, frames = refs[:6], refs[6], refs[7], refs[8]
    fulls, small_full = refs[9:15], refs[15]
    saved = refs[16 : 16 + N_ACTS]
    refs = refs[16 + N_ACTS :]
    acts = dict(zip([name for name, _, _ in ACTS], refs[:N_ACTS]))
    refs = refs[N_ACTS:]
    stages, small_stage, sems = refs[:6], refs[6], refs[7:14]
    x, kept, table, rows, hidden, ring, scores1, probs1, scores2, probs2, in_sem, ring_sem, save_sem = refs[14:]
    at = Spot()
    gather = Gather(at, shards, small, fulls, small_full, stages, small_stage, sems)

    x_load = pltpu.make_async_copy(tokens, x, in_sem.at[0])
    frames_load = pltpu.make_async_copy(frames, kept, in_sem.at[1])
    table_load = pltpu.make_async_copy(small_full, table, in_sem.at[2])
    x_load.start()
    frames_load.start()
    gather.open()
    saves = []

    def save(*names):
        for name in names:
            k = [n for n, _, _ in ACTS].index(name)
            copy = pltpu.make_async_copy(acts[name], saved[k], save_sem.at[k])
            copy.start()
            saves.append(copy)

    def fetch(i):
        n, lead, _, _, column, columns, _ = GATHER_CHUNKS[i]
        source = fulls[n] if lead is None else fulls[n].at[lead]
        if n == 4:
            source = source.at[:, :, pl.ds(column, columns)]
        return pltpu.make_async_copy(source, ring.at[i % 3], ring_sem.at[i])

    fetched = set()
    done_ticks = [0]

    def weight(i):
        for k in (i, i + 1):
            if k not in fetched and k < 12 and (k == i or k + 2 < done_ticks[0]):
                fetched.add(k)
                gather.ready(k)
                fetch(k).start()
        fetch(i).wait()
        return ring.at[i % 3]

    def row(k):
        return rows.at[k : k + 1]

    def start():
        gather.small_ready()
        table_load.start()
        x_load.wait()
        table_load.wait()
        set_rows(table, rows, hidden)
        norm_rows(x, acts["n1"], row(0), row(3))
        save("n1")

    def project(name, i, source, bias, scale):
        def run():
            w, target = weight(i), acts[name]

            def store(columns, value):
                if bias is not None:
                    value = value + rows[bias : bias + 1, columns]
                if scale:
                    value = value * SCALE
                target[:, columns] = value.astype(target.dtype)

            product(acts[source], w, store)
            save(name)

        return run

    def project_frames(name, i, bias):
        def run():
            if i == 5:
                frames_load.wait()
            w, target = weight(i), acts[name]

            def body(j):
                columns = cut(j, 256)
                value = dot(kept[...], w[:, :, columns].reshape(-1, 256))
                if bias is not None:
                    value = value + rows[bias : bias + 1, columns]
                target[:, columns] = value.astype(target.dtype)

            loop(4, body)
            save(name)

        return run

    def attend(first, count, q, k, v, o, lse, scores, probs, causal, last):
        def run():
            loop(
                count,
                lambda p: attend_pair(
                    p + first, acts[q], acts[k], acts[v], acts[o], acts[lse], scores, probs, causal
                ),
            )
            if last:
                save(o, lse)

        return run

    def join(i, source, base, bias, target, gain, shift, normed):
        def run():
            w, out = weight(i), acts[target]

            def store(columns, value):
                out[:, columns] = f32(base[:, columns]) + value + rows[bias : bias + 1, columns]

            product(acts[source], w, store)
            norm_rows(out, acts[normed], row(gain), row(shift))
            save(target, normed)

        return run

    def expand(m):
        def run():
            w = weight(8 + m)
            slope, g = acts["slope"], acts["g"]

            def store(columns, value):
                z = value + hidden[m : m + 1, columns]
                below = 0.5 + 0.5 * lax.erf(z * math.sqrt(0.5))
                slope[m, :, columns] = below + z * (jnp.exp(-0.5 * z * z) * (1.0 / math.sqrt(2.0 * math.pi)))
                g[m, :, columns] = (z * below).astype(g.dtype)

            product(acts["n3"], w, store)
            if m == 3:
                save("slope", "g")

        return run

    steps = [(0, 3, start)]
    steps += [(2, 3, project("q1", 0, "n1", 3 + 1, True)), (3, 3, project("k1", 1, "n1", None, False))]
    steps += [(4, 3, project("v1", 2, "n1", 3 + 2, False))]
    for part in range(2):
        steps.append((4, 6, attend(4 * part, 4, "q1", "k1", "v1", "o1", "lse1", scores1, probs1, True, part == 1)))
    steps.append((5, 5, join(3, "o1", x, 3 + 3, "h1", 1, 3 + 4, "n2")))
    steps += [(6, 3, project("q2", 4, "n2", 3 + 5, True)), (7, 6, project_frames("k2", 5, None))]
    steps += [(8, 6, project_frames("v2", 6, 3 + 6))]
    for part in range(4):
        steps.append((8, 5, attend(2 * part, 2, "q2", "k2", "v2", "o2", "lse2", scores2, probs2, False, part == 3)))
    steps.append((9, 5, join(7, "o2", acts["h1"], 3 + 7, "h2", 2, 3 + 8, "n3")))
    for m in range(4):
        steps.append((10 + m, 6, expand(m)))
    for kind, i in woven(gather.ticks, 6.3, 12.0, steps):
        if kind == "tick":
            gather.tick(i)
            done_ticks[0] = i + 1
        else:
            steps[i][2]()
    gather.close()
    for copy in saves:
        copy.wait()


def forward_all(shards, small, tokens, frames):
    shapes = []
    for array in shards:
        lead, tail = array.shape[:-2], array.shape[-2:]
        shapes.append(jax.ShapeDtypeStruct(lead + (4,) + tail, array.dtype))
    shapes.append(jax.ShapeDtypeStruct((4,) + small.shape, small.dtype))
    shapes += [jax.ShapeDtypeStruct(shape, dtype) for _, shape, dtype in ACTS]
    anywhere = pl.BlockSpec(memory_space=pl.ANY)
    low = jnp.bfloat16
    return pl.pallas_call(
        forward_kernel,
        name="gather_and_forward",
        out_shape=shapes,
        in_specs=[anywhere] * 9,
        out_specs=[anywhere] * len(shapes),
        scratch_shapes=[pltpu.VMEM(shape, dtype) for _, shape, dtype in ACTS]
        + [pltpu.VMEM(array.shape, array.dtype) for array in shards]
        + [
            pltpu.VMEM(small.shape, small.dtype),
            pltpu.SemaphoreType.DMA((6,)),
            pltpu.SemaphoreType.DMA((6,)),
            pltpu.SemaphoreType.DMA((N_GATHER, 10)),
            pltpu.SemaphoreType.DMA((N_GATHER, 10)),
            pltpu.SemaphoreType.DMA((3,)),
            pltpu.SemaphoreType.DMA((3,)),
            pltpu.SemaphoreType.DMA((2,)),
            pltpu.VMEM(tokens.shape, low),
            pltpu.VMEM(frames.shape, low),
            pltpu.VMEM((4,) + small.shape, low),
            pltpu.VMEM((16, 1024), jnp.float32),
            pltpu.VMEM((8, 1024), jnp.float32),
            pltpu.VMEM((3, 4, 256, 1024), low),
            pltpu.VMEM((256, 256), jnp.float32),
            pltpu.VMEM((256, 256), low),
            pltpu.VMEM((1024, 256), jnp.float32),
            pltpu.VMEM((1024, 256), low),
            pltpu.SemaphoreType.DMA((3,)),
            pltpu.SemaphoreType.DMA((12,)),
            pltpu.SemaphoreType.DMA((N_ACTS,)),
        ],
        compiler_params=pltpu.CompilerParams(
            collective_id=0, has_side_effects=True, vmem_limit_bytes=VMEM_LIMIT
        ),
    )(*shards, small, tokens, frames)


REDUCE_UNITS = (
    [(0, 256 * m, 0, 5, None) for m in range(4)]
    + [(1, 0, 1024 * m, 4, None) for m in range(4)]
    + [(2, 0, 0, 3, None)]
    + [(3 + m, 0, 0, 2, m) for m in range(3)]
    + [(6, 0, 0, 1, None)]
    + [(7 + m, 0, 0, 0, m) for m in range(3)]
)
N_REDUCE = len(REDUCE_UNITS)
RING = 4


def toggled(bit, flip):
    return bit + flip - 2 * bit * flip


class Lane:
    def __init__(self, own, other, one_a, one_b, in_a, in_b, two_a, two_b, fin_a, fin_b, acc, up, mid, za, zb, tot, fin, out):
        self.own, self.other = own, other
        self.one_a, self.one_b, self.in_a, self.in_b = one_a, one_b, in_a, in_b
        self.two_a, self.two_b, self.fin_a, self.fin_b = two_a, two_b, fin_a, fin_b
        self.acc, self.up, self.mid, self.za, self.zb, self.tot, self.fin, self.out = acc, up, mid, za, zb, tot, fin, out


def lane_shapes(units, ring, rows, columns, dtype):
    half, quarter = rows // 2, rows // 4
    return [
        pltpu.VMEM((ring, 4, half, columns), dtype),
        pltpu.VMEM((units, 4, half, columns), dtype),
        pltpu.VMEM((ring, 4, quarter, columns), dtype),
        pltpu.VMEM((ring, 4, quarter, columns), dtype),
        pltpu.VMEM((units, 2, quarter, columns), dtype),
        pltpu.VMEM((units, 2, quarter, columns), dtype),
        pltpu.VMEM((ring, quarter, columns), dtype),
        pltpu.VMEM((ring, quarter, columns), dtype),
        pltpu.VMEM((units, quarter, columns), dtype),
        pltpu.VMEM((units, quarter, columns), dtype),
        pltpu.VMEM((ring, half, columns), jnp.float32),
        pltpu.VMEM((ring, half, columns), dtype),
        pltpu.VMEM((ring, half, columns), dtype),
        pltpu.VMEM((units, half, columns), dtype),
        pltpu.VMEM((units, half, columns), dtype),
        pltpu.VMEM((ring, half, columns), dtype),
        pltpu.VMEM((units, half, columns), dtype),
        pltpu.VMEM((min(ring, 2), rows, columns), jnp.float32),
    ]


LANE_REFS = 18


def reduce_kernel(*refs):
    grads, small = refs[:10], refs[10]
    outs, small_out = refs[11:17], refs[17]
    wide = Lane(*refs[18 : 18 + LANE_REFS])
    thin = Lane(*refs[18 + LANE_REFS : 18 + 2 * LANE_REFS])
    load_sem, out_sem, send_sem, recv_sem = refs[18 + 2 * LANE_REFS :]
    at = Spot()
    bx, by = lax.rem(at.g, 2), lax.div(at.g, 2)
    middle = lax.div(at.z * (3 - at.z), 2)
    is_end, is_mid = middle == 0, middle == 1
    r_mid = at.r + middle * (6 - 4 * at.z) + (1 - middle) * (2 - 4 * at.zb)
    m_id = (at.g, r_mid)
    total = N_REDUCE + 1

    class Unit:
        def __init__(self, u):
            self.u = u
            self.small = u == 0
            if self.small:
                self.lane, self.n, rows = thin, 0, 32
                self.slot, self.out_slot = 0, 0
            else:
                self.lane, self.n, rows = wide, u - 1, 256
                self.slot, self.out_slot = self.n % RING, self.n % 2
            self.half, self.quarter = rows // 2, rows // 4
            lane, n, slot = self.lane, self.n, self.slot
            half = self.half

            def grad(start):
                if self.small:
                    return small.at[:, pl.ds(start, half), :]
                k, row, column = REDUCE_UNITS[n][:3]
                return grads[k].at[:, pl.ds(row + start, half), pl.ds(column, 1024)]

            mine = pl.multiple_of(at.core * half, half)
            theirs = pl.multiple_of((1 - at.core) * half, half)
            self.mine, self.theirs = mine, theirs
            self.load = pltpu.make_async_copy(grad(mine), lane.own.at[slot], load_sem.at[u])

            def move(k, src, dst, device):
                return pltpu.make_async_remote_copy(
                    src, dst, send_sem.at[u, k], recv_sem.at[u, k], device_id=device, device_id_type=MESH
                )

            self.core = move(0, grad(theirs), lane.other.at[n], at.c_id)
            self.one_a = move(1, lane.one_a.at[slot, pl.ds(2, 2)], lane.in_a.at[n], at.x_id)
            self.one_b = move(2, lane.one_b.at[slot, pl.ds(2, 2)], lane.in_b.at[n], at.y_id)
            self.two_a = move(3, lane.two_a.at[slot], lane.fin_a.at[n], at.y_id)
            self.two_b = move(4, lane.two_b.at[slot], lane.fin_b.at[n], at.x_id)
            self.up = move(5, lane.up.at[slot], lane.za.at[n], at.z_id)
            self.mid = move(6, lane.mid.at[slot], lane.zb.at[n], m_id)
            self.down = move(7, lane.tot.at[slot], lane.za.at[n], at.z_id)
            self.fin_mid = move(8, lane.tot.at[slot], lane.fin.at[n], at.c_id)
            self.fin_end = move(8, lane.za.at[n], lane.fin.at[n], at.c_id)
            if self.small:
                target = small_out
            else:
                k, lead = REDUCE_UNITS[n][3:]
                target = outs[k]
                if lead is not None:
                    target = target.at[lead]
                row, column = REDUCE_UNITS[n][1:3]
                target = target.at[pl.ds(row, 256), pl.ds(column, 1024)]
            self.store = pltpu.make_async_copy(lane.out.at[self.out_slot], target, out_sem.at[u])

    units = [Unit(u) for u in range(total)]

    def before(u):
        return units[u - RING] if u - RING >= 1 else None

    def begin(u):
        units[u].core.start()
        units[u].load.start()

    def join(u):
        unit, lane = units[u], units[u].lane
        unit.core.wait_recv()
        unit.load.wait()
        old = before(u)
        if old is not None:
            old.one_a.wait_send()
            old.one_b.wait_send()
        q, s, n = unit.quarter, unit.slot, unit.n

        def body(j, carry):
            first, second = lax.rem(j, 2), lax.div(j, 2)
            ga = toggled(bx, second) + 2 * toggled(by, first)
            gb = toggled(bx, first) + 2 * toggled(by, second)
            dtype = lane.one_a.dtype
            lane.one_a[s, j] = (f32(lane.own[s, ga, 0:q]) + f32(lane.other[n, ga, 0:q])).astype(dtype)
            lane.one_b[s, j] = (f32(lane.own[s, gb, q : 2 * q]) + f32(lane.other[n, gb, q : 2 * q])).astype(dtype)
            return carry

        lax.fori_loop(0, 4, body, 0)
        unit.one_a.start()
        unit.one_b.start()

    def cross(u):
        unit, lane = units[u], units[u].lane
        unit.one_a.wait_recv()
        unit.one_b.wait_recv()
        old = before(u)
        if old is not None:
            old.two_a.wait_send()
            old.two_b.wait_send()
        q, s, n = unit.quarter, unit.slot, unit.n
        dtype = lane.one_a.dtype
        lane.two_a[s] = (f32(lane.one_a[s, 1]) + f32(lane.in_a[n, 1])).astype(dtype)
        lane.two_b[s] = (f32(lane.one_b[s, 1]) + f32(lane.in_b[n, 1])).astype(dtype)
        unit.two_a.start()
        unit.two_b.start()
        lane.acc[s, 0:q] = f32(lane.one_a[s, 0]) + f32(lane.in_a[n, 0])
        lane.acc[s, q : 2 * q] = f32(lane.one_b[s, 0]) + f32(lane.in_b[n, 0])

    def close(u):
        unit, lane = units[u], units[u].lane
        unit.two_a.wait_recv()
        unit.two_b.wait_recv()
        old = before(u)
        q, s, n = unit.quarter, unit.slot, unit.n
        dtype = lane.one_a.dtype

        @pl.when(is_end)
        def _():
            if old is not None:
                old.up.wait_send()
            lane.up[s, 0:q] = (lane.acc[s, 0:q] + f32(lane.fin_a[n])).astype(dtype)
            lane.up[s, q : 2 * q] = (lane.acc[s, q : 2 * q] + f32(lane.fin_b[n])).astype(dtype)
            unit.up.start()

        @pl.when(is_mid)
        def _():
            lane.acc[s, 0:q] = lane.acc[s, 0:q] + f32(lane.fin_a[n])
            lane.acc[s, q : 2 * q] = lane.acc[s, q : 2 * q] + f32(lane.fin_b[n])

    def climb(u):
        unit, lane = units[u], units[u].lane
        old = before(u)
        s, n = unit.slot, unit.n

        @pl.when(is_mid)
        def _():
            unit.up.wait_recv()
            if old is not None:
                old.mid.wait_send()
            lane.mid[s] = (lane.acc[s] + f32(lane.za[n])).astype(lane.mid.dtype)
            unit.mid.start()

    def peak(u):
        unit, lane = units[u], units[u].lane
        old = before(u)
        s, n = unit.slot, unit.n

        @pl.when(is_mid)
        def _():
            unit.mid.wait_recv()
            if old is not None:
                old.down.wait_send()
                old.fin_mid.wait_send()
            lane.tot[s] = (f32(lane.mid[s]) + f32(lane.zb[n])).astype(lane.tot.dtype)
            unit.down.start()
            unit.fin_mid.start()

    def land(u):
        unit = units[u]

        @pl.when(is_end)
        def _():
            unit.down.wait_recv()
            unit.fin_end.start()

    def finish(u):
        unit, lane = units[u], units[u].lane
        s, n, o, h = unit.slot, unit.n, unit.out_slot, unit.half
        unit.fin_mid.wait_recv()
        if not unit.small and unit.n >= 2:
            units[u - 2].store.wait()

        @pl.when(is_mid)
        def _():
            lane.out[o, pl.ds(unit.mine, h)] = f32(lane.tot[s])

        @pl.when(is_end)
        def _():
            lane.out[o, pl.ds(unit.mine, h)] = f32(lane.za[n])

        lane.out[o, pl.ds(unit.theirs, h)] = f32(lane.fin[n])
        unit.store.start()

    barrier = pltpu.get_barrier_semaphore()
    for device in (at.x_id, at.y_id, at.c_id, at.z_id):
        pl.semaphore_signal(barrier, inc=1, device_id=device, device_id_type=MESH)

    @pl.when(is_mid)
    def _():
        pl.semaphore_signal(barrier, inc=1, device_id=m_id, device_id_type=MESH)

    pl.semaphore_wait(barrier, 4 + middle)
    begin(0)
    begin(1)
    stages = (begin, join, cross, close, climb, peak, land, finish)
    lags = (0, 1, 2, 3, 4, 5, 6, 7)
    for t in range(total + lags[-1]):
        for stage, lag in zip(stages, lags):
            u = t - lag
            if 0 <= u < total and not (stage is begin and u < 2):
                stage(u)
    for u in range(total):
        unit = units[u]
        unit.core.wait_send()
        if u == 0 or u + RING >= total:
            for move in (unit.one_a, unit.one_b, unit.two_a, unit.two_b):
                move.wait_send()

            @pl.when(is_end)
            def _():
                unit.up.wait_send()

            @pl.when(is_mid)
            def _():
                unit.mid.wait_send()
                unit.down.wait_send()
                unit.fin_mid.wait_send()

        @pl.when(is_end)
        def _():
            unit.fin_end.wait_send()

        if u == 0 or u + 2 >= total:
            unit.store.wait()


def reduce_grads(grads, small):
    anywhere = pl.BlockSpec(memory_space=pl.ANY)
    d = grads[2].shape[-1]
    out_shape = [
        jax.ShapeDtypeStruct((3, 256, d), jnp.float32),
        jax.ShapeDtypeStruct((256, d), jnp.float32),
        jax.ShapeDtypeStruct((3, 256, d), jnp.float32),
        jax.ShapeDtypeStruct((256, d), jnp.float32),
        jax.ShapeDtypeStruct((256, 4 * d), jnp.float32),
        jax.ShapeDtypeStruct((d, d), jnp.float32),
        jax.ShapeDtypeStruct((32, 256), jnp.float32),
    ]
    return pl.pallas_call(
        reduce_kernel,
        name="reduce_grads",
        out_shape=out_shape,
        in_specs=[anywhere] * 11,
        out_specs=[anywhere] * 7,
        scratch_shapes=lane_shapes(N_REDUCE, RING, 256, 1024, jnp.bfloat16)
        + lane_shapes(1, 1, 32, 256, jnp.float32)
        + [
            pltpu.SemaphoreType.DMA((N_REDUCE + 1,)),
            pltpu.SemaphoreType.DMA((N_REDUCE + 1,)),
            pltpu.SemaphoreType.DMA((N_REDUCE + 1, 9)),
            pltpu.SemaphoreType.DMA((N_REDUCE + 1, 9)),
        ],
        compiler_params=pltpu.CompilerParams(
            collective_id=1, has_side_effects=True, vmem_limit_bytes=VMEM_LIMIT
        ),
    )(*grads, small)


def shards_here(
    tokens,
    frames,
    cotangent,
    self_qkv,
    self_out,
    cross_qkv,
    cross_out,
    fc1_weight,
    fc2_weight,
    gains,
    biases,
    fc1_bias,
):
    part = gains.shape[1]
    width = tokens.shape[2]
    small = jnp.concatenate(
        [gains, biases, fc1_bias.reshape(4, part), jnp.zeros((15, part), jnp.bfloat16)], axis=0
    )
    shards = (self_qkv, self_out, cross_qkv, cross_out, fc1_weight, fc2_weight)
    full = forward_all(shards, small, tokens[0], frames[0])
    small_rows = full[6]
    weights = (
        full[0].reshape(3, width, width),
        full[1].reshape(width, width),
        full[2].reshape(3, width, width),
        full[3].reshape(width, width),
        full[4].reshape(width, -1),
        full[5].reshape(-1, width),
        small_rows[:, 0:3].transpose(1, 0, 2).reshape(3, width),
        small_rows[:, 3:13].transpose(1, 0, 2).reshape(10, width),
        small_rows[:, 13:17].reshape(-1),
    )
    n1, q1, k1, v1, o1, lse1, h1, n2, q2, k2, v2, o2, lse2, h2, n3, slope, g = full[7:]
    g = g.transpose(1, 0, 2).reshape(part, -1)
    slope = slope.transpose(1, 0, 2).reshape(part, -1)
    result = h2 + dense(g, weights[5]) + weights[7][9].astype(jnp.float32)
    x = tokens[0].astype(jnp.float32)
    lse1, lse2 = lse1[None, :, 0, :, None], lse2[None, :, 0, :, None]
    saved = (x, frames[0], n1, q1, k1, v1, o1, lse1, h1, n2, q2, k2, v2, o2, lse2, h2, n3, slope, g)
    grad_tokens, grad_frames, mlp_part, cross_part, self_part = backward(
        cotangent, weights, saved, unchanged, unchanged, unchanged, True
    )
    low = jnp.bfloat16
    grads = (
        mlp_part[1].astype(low).reshape(4, width, width),
        mlp_part[0].astype(low).reshape(4, part, -1),
        cross_part[1].astype(low).reshape(4, part, width),
        *(grad.astype(low).reshape(4, part, width) for grad in cross_part[0]),
        self_part[1].astype(low).reshape(4, part, width),
        *(grad.astype(low).reshape(4, part, width) for grad in self_part[0]),
    )
    small_grads = jnp.concatenate(
        [
            self_part[2].reshape(3, 4, part).transpose(1, 0, 2),
            self_part[3].reshape(10, 4, part).transpose(1, 0, 2),
            mlp_part[2].reshape(4, 4, part),
            jnp.zeros((4, 15, part), jnp.float32),
        ],
        axis=1,
    )
    done = reduce_grads(grads, small_grads)
    return (
        result.reshape(tokens.shape).astype(jnp.bfloat16),
        grad_tokens.reshape(tokens.shape),
        grad_frames.reshape(frames.shape),
        *done[:6],
        done[6][0:3],
        done[6][3:13],
        done[6][13:17].reshape(-1),
    )


def solution(mesh):
    in_specs = (
        P(("group", "replica"), None, None),
        P(("group", "replica"), None, None),
        P(("group", "replica"), None, None),
        P(None, "group", None),
        P("group", None),
        P(None, "group", None),
        P("group", None),
        P("group", None),
        P("group", None),
        P(None, "group"),
        P(None, "group"),
        P("group"),
    )
    out_specs = (
        P(("group", "replica"), None, None),
        P(("group", "replica"), None, None),
        P(("group", "replica"), None, None),
        P(None, "group", None),
        P("group", None),
        P(None, "group", None),
        P("group", None),
        P("group", None),
        P("group", None),
        P(None, "group"),
        P(None, "group"),
        P("group"),
    )
    here = mesh.shape["group"] == 4 and mesh.shape["replica"] == 8
    body = shards_here if here else shards_any
    return jax.shard_map(body, mesh=mesh, in_specs=in_specs, out_specs=out_specs, check_vma=False)
```

```python
from functools import partial
import math

import jax
import jax.numpy as jnp
from jax import lax
from jax.experimental import pallas as pl
from jax.experimental.pallas import tpu as pltpu
from jax.sharding import PartitionSpec as P

HEADS = 16
HEAD_DIM = 64


EPSILON = 1e-05


def layer_norm(values, gain, shift):
    center = values - jnp.mean(values, axis=-1, keepdims=True)
    spread = jnp.mean(center * center, axis=-1, keepdims=True)
    return center * lax.rsqrt(spread + EPSILON) * gain + shift


def norm_back(values, gain, shift, grad):
    result, pullback = jax.vjp(layer_norm, values, gain, shift)
    return pullback(grad)


def dense(left, right):
    return jnp.dot(left, right, preferred_element_type=jnp.float32)


def left_dense(left, right):
    return lax.dot_general(
        left, right, (((0,), (0,)), ((), ())), preferred_element_type=jnp.float32
    )


def right_dense(grad, weight):
    return lax.dot_general(
        grad, weight, (((1,), (1,)), ((), ())), preferred_element_type=jnp.float32
    )


def column_sum(values):
    return jnp.sum(values.astype(jnp.float32), axis=0)


def split_heads(rows, batch):
    return rows.reshape(batch, -1, HEADS, rows.shape[-1] // HEADS)


def scores_of(query_heads, key_heads, masked):
    scores = jnp.einsum(
        "bqhd,bkhd->bhqk", query_heads, key_heads, preferred_element_type=jnp.float32
    )
    if masked:
        shape = (query_heads.shape[1], key_heads.shape[1])
        allowed = lax.broadcasted_iota(jnp.int32, shape, 0) >= lax.broadcasted_iota(
            jnp.int32, shape, 1
        )
        scores = jnp.where(allowed, scores, -jnp.inf)
    return scores


def attend(queries, keys, values, batch, masked):
    query_heads = split_heads(queries, batch)
    key_heads = split_heads(keys, batch)
    value_heads = split_heads(values, batch)
    scores = scores_of(query_heads, key_heads, masked)
    highest = jnp.max(scores, axis=-1, keepdims=True)
    expo = jnp.exp(scores - highest)
    total = jnp.sum(expo, axis=-1, keepdims=True)
    probs = (expo / total).astype(jnp.bfloat16)
    mixed = jnp.einsum("bhqk,bkhd->bqhd", probs, value_heads, preferred_element_type=jnp.float32)
    return (mixed.reshape(queries.shape).astype(jnp.bfloat16), highest + jnp.log(total))


def attend_back(queries, keys, values, grad_mixed, logsum, batch, masked):
    query_heads = split_heads(queries, batch)
    key_heads = split_heads(keys, batch)
    value_heads = split_heads(values, batch)
    grad_heads = split_heads(grad_mixed, batch)
    probs = jnp.exp(scores_of(query_heads, key_heads, masked) - logsum)
    probs_low = probs.astype(jnp.bfloat16)
    grad_probs = jnp.einsum(
        "bqhd,bkhd->bhqk", grad_heads, value_heads, preferred_element_type=jnp.float32
    )
    grad_values = jnp.einsum(
        "bhqk,bqhd->bkhd", probs_low, grad_heads, preferred_element_type=jnp.float32
    )
    center = jnp.sum(probs * grad_probs, axis=-1, keepdims=True)
    grad_scores = (probs * (grad_probs - center)).astype(jnp.bfloat16)
    grad_queries = jnp.einsum(
        "bhqk,bkhd->bqhd", grad_scores, key_heads, preferred_element_type=jnp.float32
    )
    grad_keys = jnp.einsum(
        "bhqk,bqhd->bkhd", grad_scores, query_heads, preferred_element_type=jnp.float32
    )
    return (
        grad_queries.reshape(queries.shape),
        grad_keys.reshape(keys.shape),
        grad_values.reshape(keys.shape),
    )


def forward(tokens, frames, weights):
    self_qkv, self_out, cross_qkv, cross_out, fc1_weight, fc2_weight, gains, biases, fc1_bias = (
        weights
    )
    batch = tokens.shape[0]
    width = tokens.shape[2]
    scale = 1.0 / math.sqrt(HEAD_DIM)
    gain_rows = gains.astype(jnp.float32)
    bias_rows = biases.astype(jnp.float32)
    resid0 = tokens.reshape(-1, width).astype(jnp.float32)
    frame_rows = frames.reshape(-1, width)
    normed1 = layer_norm(resid0, gain_rows[0], bias_rows[0]).astype(jnp.bfloat16)
    query1 = ((dense(normed1, self_qkv[0]) + bias_rows[1]) * scale).astype(jnp.bfloat16)
    key1 = dense(normed1, self_qkv[1]).astype(jnp.bfloat16)
    value1 = (dense(normed1, self_qkv[2]) + bias_rows[2]).astype(jnp.bfloat16)
    mixed1, logsum1 = attend(query1, key1, value1, batch, True)
    resid1 = resid0 + dense(mixed1, self_out) + bias_rows[3]
    normed2 = layer_norm(resid1, gain_rows[1], bias_rows[4]).astype(jnp.bfloat16)
    query2 = ((dense(normed2, cross_qkv[0]) + bias_rows[5]) * scale).astype(jnp.bfloat16)
    key2 = dense(frame_rows, cross_qkv[1]).astype(jnp.bfloat16)
    value2 = (dense(frame_rows, cross_qkv[2]) + bias_rows[6]).astype(jnp.bfloat16)
    mixed2, logsum2 = attend(query2, key2, value2, batch, False)
    resid2 = resid1 + dense(mixed2, cross_out) + bias_rows[7]
    normed3 = layer_norm(resid2, gain_rows[2], bias_rows[8]).astype(jnp.bfloat16)
    hidden_pre = dense(normed3, fc1_weight) + fc1_bias.astype(jnp.float32)
    hidden = jax.nn.gelu(hidden_pre, approximate=False).astype(jnp.bfloat16)
    result = resid2 + dense(hidden, fc2_weight) + bias_rows[9]
    saved = (
        resid0,
        frame_rows,
        normed1,
        query1,
        key1,
        value1,
        mixed1,
        logsum1,
        resid1,
        normed2,
        query2,
        key2,
        value2,
        mixed2,
        logsum2,
        resid2,
        normed3,
        hidden_pre,
        hidden,
    )
    return (result, saved)


def backward(cotangent, weights, saved, settle_mlp, settle_cross, settle_self):
    self_qkv, self_out, cross_qkv, cross_out, fc1_weight, fc2_weight, gains, biases, fc1_bias = (
        weights
    )
    (
        resid0,
        frame_rows,
        normed1,
        query1,
        key1,
        value1,
        mixed1,
        logsum1,
        resid1,
        normed2,
        query2,
        key2,
        value2,
        mixed2,
        logsum2,
        resid2,
        normed3,
        hidden_pre,
        hidden,
    ) = saved
    batch = cotangent.shape[0]
    width = cotangent.shape[2]
    scale = 1.0 / math.sqrt(HEAD_DIM)
    gain_rows = gains.astype(jnp.float32)
    bias_rows = biases.astype(jnp.float32)
    grad_out = cotangent.reshape(-1, width).astype(jnp.float32)
    grad_branch3 = grad_out.astype(jnp.bfloat16)
    fc2_grad = left_dense(hidden, grad_branch3)
    bias9 = column_sum(grad_branch3)
    grad_hidden = right_dense(grad_branch3, fc2_weight)
    unused, gelu_pull = jax.vjp(partial(jax.nn.gelu, approximate=False), hidden_pre)
    grad_pre = gelu_pull(grad_hidden)[0].astype(jnp.bfloat16)
    fc1_grad = left_dense(normed3, grad_pre)
    fc1_bias_grad = column_sum(grad_pre)
    mlp_part = settle_mlp((fc1_grad, fc2_grad, fc1_bias_grad))
    grad_resid2, gain3, shift3 = norm_back(
        resid2, gain_rows[2], bias_rows[8], right_dense(grad_pre, fc1_weight)
    )
    grad_resid2 = grad_out + grad_resid2
    grad_branch2 = grad_resid2.astype(jnp.bfloat16)
    cross_out_grad = left_dense(mixed2, grad_branch2)
    bias7 = column_sum(grad_branch2)
    grad_mixed2 = right_dense(grad_branch2, cross_out).astype(jnp.bfloat16)
    grad_q2, grad_k2, grad_v2 = attend_back(
        query2, key2, value2, grad_mixed2, logsum2, batch, False
    )
    grad_q2 = (grad_q2.astype(jnp.bfloat16).astype(jnp.float32) * scale).astype(jnp.bfloat16)
    grad_k2 = grad_k2.astype(jnp.bfloat16)
    grad_v2 = grad_v2.astype(jnp.bfloat16)
    cross_qkv_grad = [
        left_dense(normed2, grad_q2),
        left_dense(frame_rows, grad_k2),
        left_dense(frame_rows, grad_v2),
    ]
    bias5 = column_sum(grad_q2)
    bias6 = column_sum(grad_v2)
    cross_part = settle_cross((cross_qkv_grad, cross_out_grad))
    grad_frames = right_dense(grad_k2, cross_qkv[1]) + right_dense(grad_v2, cross_qkv[2])
    grad_resid1, gain2, shift2 = norm_back(
        resid1, gain_rows[1], bias_rows[4], right_dense(grad_q2, cross_qkv[0])
    )
    grad_resid1 = grad_resid2 + grad_resid1
    grad_branch1 = grad_resid1.astype(jnp.bfloat16)
    self_out_grad = left_dense(mixed1, grad_branch1)
    bias3 = column_sum(grad_branch1)
    grad_mixed1 = right_dense(grad_branch1, self_out).astype(jnp.bfloat16)
    grad_q1, grad_k1, grad_v1 = attend_back(query1, key1, value1, grad_mixed1, logsum1, batch, True)
    grad_q1 = (grad_q1.astype(jnp.bfloat16).astype(jnp.float32) * scale).astype(jnp.bfloat16)
    grad_k1 = grad_k1.astype(jnp.bfloat16)
    grad_v1 = grad_v1.astype(jnp.bfloat16)
    self_qkv_grad = [
        left_dense(normed1, grad_q1),
        left_dense(normed1, grad_k1),
        left_dense(normed1, grad_v1),
    ]
    bias1 = column_sum(grad_q1)
    bias2 = column_sum(grad_v1)
    grad_normed1 = (
        right_dense(grad_q1, self_qkv[0])
        + right_dense(grad_k1, self_qkv[1])
        + right_dense(grad_v1, self_qkv[2])
    )
    grad_resid0, gain1, shift1 = norm_back(resid0, gain_rows[0], bias_rows[0], grad_normed1)
    grad_tokens = grad_resid1 + grad_resid0
    gains_grad = jnp.stack([gain1, gain2, gain3])
    biases_grad = jnp.stack(
        [shift1, bias1, bias2, bias3, shift2, bias5, bias6, bias7, shift3, bias9]
    )
    self_part = settle_self((self_qkv_grad, self_out_grad, gains_grad, biases_grad))
    return (grad_tokens, grad_frames, mlp_part, cross_part, self_part)


def unchanged(grads):
    return grads


def shards_any(
    tokens,
    frames,
    cotangent,
    self_qkv,
    self_out,
    cross_qkv,
    cross_out,
    fc1_weight,
    fc2_weight,
    gains,
    biases,
    fc1_bias,
):
    weights = (
        lax.all_gather(self_qkv, "group", axis=1, tiled=True),
        lax.all_gather(self_out, "group", axis=0, tiled=True),
        lax.all_gather(cross_qkv, "group", axis=1, tiled=True),
        lax.all_gather(cross_out, "group", axis=0, tiled=True),
        lax.all_gather(fc1_weight, "group", axis=0, tiled=True),
        lax.all_gather(fc2_weight, "group", axis=0, tiled=True),
        lax.all_gather(gains, "group", axis=1, tiled=True),
        lax.all_gather(biases, "group", axis=1, tiled=True),
        lax.all_gather(fc1_bias, "group", axis=0, tiled=True),
    )
    result, saved = forward(tokens, frames, weights)
    grad_tokens, grad_frames, mlp_part, cross_part, self_part = backward(
        cotangent, weights, saved, unchanged, unchanged, unchanged
    )
    shares = (
        lax.psum_scatter(
            jnp.stack(self_part[0]).astype(jnp.bfloat16), "group", scatter_dimension=1, tiled=True
        ).astype(jnp.float32),
        lax.psum_scatter(
            self_part[1].astype(jnp.bfloat16), "group", scatter_dimension=0, tiled=True
        ).astype(jnp.float32),
        lax.psum_scatter(
            jnp.stack(cross_part[0]).astype(jnp.bfloat16), "group", scatter_dimension=1, tiled=True
        ).astype(jnp.float32),
        lax.psum_scatter(
            cross_part[1].astype(jnp.bfloat16), "group", scatter_dimension=0, tiled=True
        ).astype(jnp.float32),
        lax.psum_scatter(
            mlp_part[0].astype(jnp.bfloat16), "group", scatter_dimension=0, tiled=True
        ).astype(jnp.float32),
        lax.psum_scatter(
            mlp_part[1].astype(jnp.bfloat16), "group", scatter_dimension=0, tiled=True
        ).astype(jnp.float32),
        lax.psum_scatter(
            self_part[2].astype(jnp.bfloat16), "group", scatter_dimension=1, tiled=True
        ).astype(jnp.float32),
        lax.psum_scatter(
            self_part[3].astype(jnp.bfloat16), "group", scatter_dimension=1, tiled=True
        ).astype(jnp.float32),
        lax.psum_scatter(
            mlp_part[2].astype(jnp.bfloat16), "group", scatter_dimension=0, tiled=True
        ).astype(jnp.float32),
    )
    summed = (
        lax.psum(shares[0].astype(jnp.bfloat16), "replica").astype(jnp.float32),
        lax.psum(shares[1].astype(jnp.bfloat16), "replica").astype(jnp.float32),
        lax.psum(shares[2].astype(jnp.bfloat16), "replica").astype(jnp.float32),
        lax.psum(shares[3].astype(jnp.bfloat16), "replica").astype(jnp.float32),
        lax.psum(shares[4].astype(jnp.bfloat16), "replica").astype(jnp.float32),
        lax.psum(shares[5].astype(jnp.bfloat16), "replica").astype(jnp.float32),
        lax.psum(shares[6].astype(jnp.bfloat16), "replica").astype(jnp.float32),
        lax.psum(shares[7].astype(jnp.bfloat16), "replica").astype(jnp.float32),
        lax.psum(shares[8].astype(jnp.bfloat16), "replica").astype(jnp.float32),
    )
    (
        self_qkv_grad,
        self_out_grad,
        cross_qkv_grad,
        cross_out_grad,
        fc1_grad,
        fc2_grad,
        gains_grad,
        biases_grad,
        fc1_bias_grad,
    ) = summed
    return (
        result.reshape(tokens.shape).astype(jnp.bfloat16),
        grad_tokens.reshape(tokens.shape),
        grad_frames.reshape(frames.shape),
        self_qkv_grad,
        self_out_grad,
        cross_qkv_grad,
        cross_out_grad,
        fc1_grad,
        fc2_grad,
        gains_grad,
        biases_grad,
        fc1_bias_grad,
    )


MESH = pl.DeviceIdType.MESH
VMEM_LIMIT = 64 * 1024 * 1024 - 128 * 1024


class Spot:
    def __init__(self):
        self.g = lax.axis_index("group")
        self.r = lax.axis_index("replica")
        self.core = lax.rem(self.r, 2)
        self.z = lax.div(self.r, 2)
        self.zb = lax.rem(self.z, 2)
        self.gx = self.g + 1 - 2 * lax.rem(self.g, 2)
        self.gy = lax.rem(self.g + 2, 4)
        self.gd = self.gx + 2 - 4 * lax.div(self.gx, 2)
        self.rc = self.r + 1 - 2 * self.core
        self.rz = self.r + 2 - 4 * self.zb
        self.x_id = (self.gx, self.r)
        self.y_id = (self.gy, self.r)
        self.d_id = (self.gd, self.r)
        self.c_id = (self.g, self.rc)
        self.z_id = (self.g, self.rz)


def meet(*ids):
    barrier = pltpu.get_barrier_semaphore()
    for device in ids:
        pl.semaphore_signal(barrier, inc=1, device_id=device, device_id_type=MESH)
    pl.semaphore_wait(barrier, len(ids))


GATHER_CHUNKS = (
    [(0, m, 0, 256, 0, 1024, m != 0) for m in range(3)]
    + [(1, None, 0, 256, 0, 1024, False)]
    + [(2, m, 0, 256, 0, 1024, m != 0) for m in range(3)]
    + [(3, None, 0, 256, 0, 1024, False)]
    + [(4, None, 0, 256, 1024 * m, 1024, m != 3) for m in range(4)]
    + [(5, None, 256 * m, 256, 0, 1024, m != 3) for m in range(4)]
)
N_GATHER = len(GATHER_CHUNKS)


class Gather:
    def __init__(self, at, shards, small, fulls, small_full, stages, small_stage, sems):
        self.load_sem, self.put_sem, self.send_sem, self.recv_sem, small_send, small_recv, small_local = sems
        self.at, self.shards, self.fulls = at, shards, fulls
        self.loads = [pltpu.make_async_copy(shards[n], stages[n], self.load_sem.at[n]) for n in range(6)]
        self.small_load = pltpu.make_async_copy(small, small_stage, small_local.at[0])
        self.small_put = pltpu.make_async_copy(small_stage, small_full.at[at.g], small_local.at[1])
        self.small_copies = [
            pltpu.make_async_remote_copy(
                small, small_full.at[at.g], small_send.at[n], small_recv.at[n],
                device_id=device, device_id_type=MESH,
            )
            for n, device in enumerate((at.x_id, at.y_id, at.d_id))
        ]
        self.puts = []
        for n in range(6):
            where = (slice(None), at.g) if n in (0, 2) else (at.g,)
            self.puts.append(pltpu.make_async_copy(stages[n], fulls[n].at[where], self.put_sem.at[n]))
        self.plans = [self.plan(i) for i in range(N_GATHER)]
        self.arrived, self.placed = set(), set()

    def full(self, i, g, start, rows):
        n, lead, first, _, column, columns, _ = GATHER_CHUNKS[i]
        where = (g, pl.ds(first + start, rows), pl.ds(column, columns))
        return self.fulls[n].at[where if lead is None else (lead,) + where]

    def shard(self, i, start, rows):
        n, lead, first, _, column, columns, _ = GATHER_CHUNKS[i]
        where = (pl.ds(first + start, rows), pl.ds(column, columns))
        return self.shards[n].at[where if lead is None else (lead,) + where]

    def plan(self, i):
        at = self.at

        def put(k, src, g, start, rows, device):
            return pltpu.make_async_remote_copy(
                src, self.full(i, g, start, rows), self.send_sem.at[i, k], self.recv_sem.at[i, k],
                device_id=device, device_id_type=MESH,
            )

        rows, split = GATHER_CHUNKS[i][3], GATHER_CHUNKS[i][6]
        half = rows // 2
        base = pl.multiple_of(at.core * half, half)
        core_base = base
        if split:
            half = half // 2
            base = pl.multiple_of(base + at.zb * half, half)
        quarter = half // 2
        mine = self.shard(i, base, half)
        moves = [
            put(0, mine, at.g, base, half, at.x_id),
            put(1, mine, at.g, base, half, at.y_id),
            put(2, self.full(i, at.gy, base + quarter, quarter), at.gy, base + quarter, quarter, at.x_id),
            put(3, self.full(i, at.gx, base, quarter), at.gx, base, quarter, at.y_id),
        ]
        for k, g in enumerate((at.gx, at.gy, at.gd)):
            moves.append(put(4 + k, self.full(i, g, core_base, rows // 2), g, core_base, rows // 2, at.c_id))
        if split:
            for k, g in enumerate((at.gx, at.gy, at.gd)):
                moves.append(put(7 + k, self.full(i, g, base, half), g, base, half, at.z_id))
        return moves, split

    def open(self):
        at = self.at
        for load in self.loads:
            load.start()
        self.small_load.start()
        meet(at.x_id, at.y_id, at.d_id, at.c_id, at.z_id)
        self.begin(0)
        for copy in self.small_copies:
            copy.start()
        self.begin(1)
        self.small_load.wait()
        self.small_put.start()
        for n in range(6):
            self.loads[n].wait()
            self.puts[n].start()

    def small_ready(self):
        self.small_put.wait()
        for copy in self.small_copies:
            copy.wait()

    def begin(self, i):
        moves, _ = self.plans[i]
        moves[0].start()
        moves[1].start()

    def second(self, i):
        moves, split = self.plans[i]
        moves[0].wait_recv()
        moves[1].wait_recv()
        moves[2].start()
        moves[3].start()
        for k in (7, 8) if split else (4, 5):
            moves[k].start()

    def third(self, i):
        moves, split = self.plans[i]
        moves[2].wait_recv()
        moves[3].wait_recv()
        moves[9 if split else 6].start()

    def fourth(self, i):
        moves, split = self.plans[i]
        if split:
            for k in (7, 8, 9):
                moves[k].wait_recv()
            for k in (4, 5, 6):
                moves[k].start()

    ticks = N_GATHER + 2

    def tick(self, i):
        if i < N_GATHER:
            self.second(i)
        if i + 2 < N_GATHER:
            self.begin(i + 2)
        if 0 <= i - 1 < N_GATHER:
            self.third(i - 1)
        if 0 <= i - 2 < N_GATHER:
            self.fourth(i - 2)

    def ready(self, i):
        n = GATHER_CHUNKS[i][0]
        if n not in self.placed:
            self.placed.add(n)
            self.puts[n].wait()
        if i not in self.arrived:
            self.arrived.add(i)
            for k in (4, 5, 6):
                self.plans[i][0][k].wait_recv()

    def close(self):
        for i in range(N_GATHER):
            self.ready(i)
            moves, split = self.plans[i]
            for k in range(10 if split else 7):
                moves[k].wait_send()


def f32(value):
    return value.astype(jnp.float32)


def dot(left, right):
    return jnp.dot(left, right, preferred_element_type=jnp.float32)


def dot_tn(left, right):
    return lax.dot_general(left, right, (((0,), (0,)), ((), ())), preferred_element_type=jnp.float32)


def dot_nt(left, right):
    return lax.dot_general(left, right, (((1,), (1,)), ((), ())), preferred_element_type=jnp.float32)


def loop(count, body):
    def step(i, carry):
        body(i)
        return carry

    lax.fori_loop(0, count, step, 0)


def cut(i, size):
    return pl.ds(pl.multiple_of(i * size, size), size)


def norm_rows(src, dst, gain, shift):
    def body(i):
        values = f32(src[cut(i, 32)])
        center = values - jnp.mean(values, axis=-1, keepdims=True)
        spread = jnp.mean(center * center, axis=-1, keepdims=True)
        dst[cut(i, 32)] = (center * lax.rsqrt(spread + EPSILON) * gain[...] + shift[...]).astype(dst.dtype)

    loop(src.shape[0] // 32, body)


def product(left, weight, store, tile=256):
    def body(j):
        columns = cut(j, tile)
        store(columns, dot(left[...], weight[:, :, columns].reshape(-1, tile)))

    loop(weight.shape[-1] // tile, body)


def attend_pair(p, q, k, v, o, lse, scores, probs, causal):
    columns = cut(p, 128)
    keys, count = k.shape[0], q.shape[0]
    qq, kk, vv = q[:, columns], k[:, columns], v[:, columns]
    lane = lax.broadcasted_iota(jnp.int32, qq.shape, 1)
    vt = vv.T
    block = 128
    sides = []
    for a in range(2):
        qa = jnp.where((lane < 64) if a == 0 else (lane >= 64), qq, jnp.zeros_like(qq))
        scores[...] = dot_nt(kk, qa)

        def rows_of(j):
            part = scores[cut(j, block)]
            if causal:
                key = lax.broadcasted_iota(jnp.int32, part.shape, 0) + j * block
                query = lax.broadcasted_iota(jnp.int32, part.shape, 1)
                part = jnp.where(query >= key, part, -jnp.inf)
            return part

        def top(j, carry):
            return jnp.maximum(carry, jnp.max(rows_of(j), axis=0, keepdims=True))

        highest = lax.fori_loop(0, keys // block, top, jnp.full((1, count), -jnp.inf, jnp.float32))

        def expo(j, carry):
            e = jnp.exp(rows_of(j) - highest)
            scores[cut(j, block)] = e
            return carry + jnp.sum(e, axis=0, keepdims=True)

        total = lax.fori_loop(0, keys // block, expo, jnp.zeros((1, count), jnp.float32))
        share = 1.0 / total

        def rounded(j):
            probs[cut(j, block)] = (scores[cut(j, block)] * share).astype(probs.dtype)

        loop(keys // block, rounded)
        lse[2 * p + a] = jnp.broadcast_to(highest + jnp.log(total), (8, count))
        sides.append(dot(vt[64 * a : 64 * a + 64], probs[...]))
    o[:, columns] = jnp.concatenate(sides, axis=0).T.astype(o.dtype)


def attend_back_pair(p, q, k, v, go, lse, scores, gscores, probs, gs, gq, gk, gv, causal):
    columns = cut(p, 128)
    keys, count = k.shape[0], q.shape[0]
    qq, kk, vv, dd = q[:, columns], k[:, columns], v[:, columns], go[:, columns]
    lane = lax.broadcasted_iota(jnp.int32, qq.shape, 1)
    zero = jnp.zeros_like(qq)
    kt = kk.T
    block = 128
    sides, qs, ds = [], [], []
    for a in range(2):
        here = (lane < 64) if a == 0 else (lane >= 64)
        qa, da = jnp.where(here, qq, zero), jnp.where(here, dd, zero)
        qs.append(qa)
        ds.append(da)
        scores[...] = dot_nt(kk, qa)
        gscores[...] = dot_nt(vv, da)
        line = lse[2 * p + a][0:1]
        across = slice(a * count, (a + 1) * count)

        def first(j, carry):
            part = scores[cut(j, block)]
            if causal:
                key = lax.broadcasted_iota(jnp.int32, part.shape, 0) + j * block
                query = lax.broadcasted_iota(jnp.int32, part.shape, 1)
                part = jnp.where(query >= key, part, -jnp.inf)
            e = jnp.exp(part - line)
            scores[cut(j, block)] = e
            probs[cut(j, block), across] = e.astype(probs.dtype)
            return carry + jnp.sum(e * gscores[cut(j, block)], axis=0, keepdims=True)

        center = lax.fori_loop(0, keys // block, first, jnp.zeros((1, count), jnp.float32))

        def second(j):
            rows = cut(j, block)
            gs[rows, across] = (scores[rows] * (gscores[rows] - center)).astype(gs.dtype)

        loop(keys // block, second)
        sides.append(dot(kt[64 * a : 64 * a + 64], gs[:, across]))
    gv[:, columns] = dot(probs[...], jnp.concatenate(ds, axis=0)).astype(gv.dtype)
    gk[:, columns] = dot(gs[...], jnp.concatenate(qs, axis=0)).astype(gk.dtype)
    side = jnp.concatenate(sides, axis=0).T.astype(jnp.bfloat16)
    gq[:, columns] = (f32(side) * SCALE).astype(gq.dtype)

def woven(ticks, period, first, steps):
    order, now, tick = [], 0.0, 0
    left = list(range(len(steps)))
    while left or tick < ticks:
        due = first + tick * period
        if left and steps[left[0]][0] < tick and (now < due or tick >= ticks):
            now += steps[left[0]][1]
            order.append(("step", left.pop(0)))
        else:
            now = max(now, due)
            order.append(("tick", tick))
            tick += 1
    return order


ACTS = (
    [("n1", (256, 1024), jnp.bfloat16), ("q1", (256, 1024), jnp.bfloat16), ("k1", (256, 1024), jnp.bfloat16)]
    + [("v1", (256, 1024), jnp.bfloat16), ("o1", (256, 1024), jnp.bfloat16), ("lse1", (16, 8, 256), jnp.float32)]
    + [("h1", (256, 1024), jnp.float32), ("n2", (256, 1024), jnp.bfloat16), ("q2", (256, 1024), jnp.bfloat16)]
    + [("k2", (1024, 1024), jnp.bfloat16), ("v2", (1024, 1024), jnp.bfloat16), ("o2", (256, 1024), jnp.bfloat16)]
    + [("lse2", (16, 8, 256), jnp.float32), ("h2", (256, 1024), jnp.float32), ("n3", (256, 1024), jnp.bfloat16)]
    + [("slope", (4, 256, 1024), jnp.float32), ("g", (4, 256, 1024), jnp.bfloat16)]
)
N_ACTS = len(ACTS)
SCALE = 0.125


def set_rows(small_full, rows, hidden):
    for g in range(4):
        for k in range(13):
            rows[k : k + 1, 256 * g : 256 * g + 256] = f32(small_full[g, k : k + 1])
        for k in range(4):
            hidden[g : g + 1, 256 * k : 256 * k + 256] = f32(small_full[g, 13 + k : 14 + k])


def forward_kernel(*refs):
    shards, small, tokens, frames = refs[:6], refs[6], refs[7], refs[8]
    fulls, small_full = refs[9:15], refs[15]
    saved = refs[16 : 16 + N_ACTS]
    refs = refs[16 + N_ACTS :]
    acts = dict(zip([name for name, _, _ in ACTS], refs[:N_ACTS]))
    refs = refs[N_ACTS:]
    stages, small_stage, sems = refs[:6], refs[6], refs[7:14]
    x, kept, table, rows, hidden, ring, scores1, probs1, scores2, probs2, in_sem, ring_sem, save_sem = refs[14:]
    at = Spot()
    gather = Gather(at, shards, small, fulls, small_full, stages, small_stage, sems)

    x_load = pltpu.make_async_copy(tokens, x, in_sem.at[0])
    frames_load = pltpu.make_async_copy(frames, kept, in_sem.at[1])
    table_load = pltpu.make_async_copy(small_full, table, in_sem.at[2])
    x_load.start()
    frames_load.start()
    gather.open()
    saves = []

    def save(*names):
        for name in names:
            k = [n for n, _, _ in ACTS].index(name)
            copy = pltpu.make_async_copy(acts[name], saved[k], save_sem.at[k])
            copy.start()
            saves.append(copy)

    def fetch(i):
        n, lead, _, _, column, columns, _ = GATHER_CHUNKS[i]
        source = fulls[n] if lead is None else fulls[n].at[lead]
        if n == 4:
            source = source.at[:, :, pl.ds(column, columns)]
        return pltpu.make_async_copy(source, ring.at[i % 3], ring_sem.at[i])

    fetched = set()
    done_ticks = [0]

    def weight(i):
        for k in (i, i + 1):
            if k not in fetched and k < 12 and (k == i or k + 2 < done_ticks[0]):
                fetched.add(k)
                gather.ready(k)
                fetch(k).start()
        fetch(i).wait()
        return ring.at[i % 3]

    def row(k):
        return rows.at[k : k + 1]

    def start():
        gather.small_ready()
        table_load.start()
        x_load.wait()
        table_load.wait()
        set_rows(table, rows, hidden)
        norm_rows(x, acts["n1"], row(0), row(3))
        save("n1")

    def project(name, i, source, bias, scale):
        def run():
            w, target = weight(i), acts[name]

            def store(columns, value):
                if bias is not None:
                    value = value + rows[bias : bias + 1, columns]
                if scale:
                    value = value * SCALE
                target[:, columns] = value.astype(target.dtype)

            product(acts[source], w, store)
            save(name)

        return run

    def project_frames(name, i, bias):
        def run():
            if i == 5:
                frames_load.wait()
            w, target = weight(i), acts[name]

            def body(j):
                columns = cut(j, 256)
                value = dot(kept[...], w[:, :, columns].reshape(-1, 256))
                if bias is not None:
                    value = value + rows[bias : bias + 1, columns]
                target[:, columns] = value.astype(target.dtype)

            loop(4, body)
            save(name)

        return run

    def attend(first, count, q, k, v, o, lse, scores, probs, causal, last):
        def run():
            loop(
                count,
                lambda p: attend_pair(
                    p + first, acts[q], acts[k], acts[v], acts[o], acts[lse], scores, probs, causal
                ),
            )
            if last:
                save(o, lse)

        return run

    def join(i, source, base, bias, target, gain, shift, normed):
        def run():
            w, out = weight(i), acts[target]

            def store(columns, value):
                out[:, columns] = f32(base[:, columns]) + value + rows[bias : bias + 1, columns]

            product(acts[source], w, store)
            norm_rows(out, acts[normed], row(gain), row(shift))
            save(target, normed)

        return run

    def expand(m):
        def run():
            w = weight(8 + m)
            slope, g = acts["slope"], acts["g"]

            def store(columns, value):
                z = value + hidden[m : m + 1, columns]
                below = 0.5 + 0.5 * lax.erf(z * math.sqrt(0.5))
                slope[m, :, columns] = below + z * (jnp.exp(-0.5 * z * z) * (1.0 / math.sqrt(2.0 * math.pi)))
                g[m, :, columns] = (z * below).astype(g.dtype)

            product(acts["n3"], w, store)
            if m == 3:
                save("slope", "g")

        return run

    steps = [(0, 3, start)]
    steps += [(2, 3, project("q1", 0, "n1", 3 + 1, True)), (3, 3, project("k1", 1, "n1", None, False))]
    steps += [(4, 3, project("v1", 2, "n1", 3 + 2, False))]
    for part in range(2):
        steps.append((4, 6, attend(4 * part, 4, "q1", "k1", "v1", "o1", "lse1", scores1, probs1, True, part == 1)))
    steps.append((5, 5, join(3, "o1", x, 3 + 3, "h1", 1, 3 + 4, "n2")))
    steps += [(6, 3, project("q2", 4, "n2", 3 + 5, True)), (7, 6, project_frames("k2", 5, None))]
    steps += [(8, 6, project_frames("v2", 6, 3 + 6))]
    for part in range(4):
        steps.append((8, 5, attend(2 * part, 2, "q2", "k2", "v2", "o2", "lse2", scores2, probs2, False, part == 3)))
    steps.append((9, 5, join(7, "o2", acts["h1"], 3 + 7, "h2", 2, 3 + 8, "n3")))
    for m in range(4):
        steps.append((10 + m, 6, expand(m)))
    for kind, i in woven(gather.ticks, 6.3, 12.0, steps):
        if kind == "tick":
            gather.tick(i)
            done_ticks[0] = i + 1
        else:
            steps[i][2]()
    gather.close()
    for copy in saves:
        copy.wait()


def forward_all(shards, small, tokens, frames):
    shapes = []
    for array in shards:
        lead, tail = array.shape[:-2], array.shape[-2:]
        shapes.append(jax.ShapeDtypeStruct(lead + (4,) + tail, array.dtype))
    shapes.append(jax.ShapeDtypeStruct((4,) + small.shape, small.dtype))
    shapes += [jax.ShapeDtypeStruct(shape, dtype) for _, shape, dtype in ACTS]
    anywhere = pl.BlockSpec(memory_space=pl.ANY)
    low = jnp.bfloat16
    return pl.pallas_call(
        forward_kernel,
        name="gather_and_forward",
        out_shape=shapes,
        in_specs=[anywhere] * 9,
        out_specs=[anywhere] * len(shapes),
        scratch_shapes=[pltpu.VMEM(shape, dtype) for _, shape, dtype in ACTS]
        + [pltpu.VMEM(array.shape, array.dtype) for array in shards]
        + [
            pltpu.VMEM(small.shape, small.dtype),
            pltpu.SemaphoreType.DMA((6,)),
            pltpu.SemaphoreType.DMA((6,)),
            pltpu.SemaphoreType.DMA((N_GATHER, 10)),
            pltpu.SemaphoreType.DMA((N_GATHER, 10)),
            pltpu.SemaphoreType.DMA((3,)),
            pltpu.SemaphoreType.DMA((3,)),
            pltpu.SemaphoreType.DMA((2,)),
            pltpu.VMEM(tokens.shape, low),
            pltpu.VMEM(frames.shape, low),
            pltpu.VMEM((4,) + small.shape, low),
            pltpu.VMEM((16, 1024), jnp.float32),
            pltpu.VMEM((8, 1024), jnp.float32),
            pltpu.VMEM((3, 4, 256, 1024), low),
            pltpu.VMEM((256, 256), jnp.float32),
            pltpu.VMEM((256, 256), low),
            pltpu.VMEM((1024, 256), jnp.float32),
            pltpu.VMEM((1024, 256), low),
            pltpu.SemaphoreType.DMA((3,)),
            pltpu.SemaphoreType.DMA((12,)),
            pltpu.SemaphoreType.DMA((N_ACTS,)),
        ],
        compiler_params=pltpu.CompilerParams(
            collective_id=0, has_side_effects=True, vmem_limit_bytes=VMEM_LIMIT
        ),
    )(*shards, small, tokens, frames)


REDUCE_WIDE = 16
RING, OTHERS, HELD, FINALS = 3, 4, 4, 8


def each(rows, body):
    block = min(rows, 16)
    loop(rows // block, lambda i: body(cut(i, block), lambda k: pl.ds(pl.multiple_of(k + i * block, block), block)))


def toggled(bit, flip):
    return bit + flip - 2 * bit * flip


class Lane:
    NAMES = ["other", "one_a", "one_b", "in_a", "in_b", "two_a", "two_b", "fin_a"]
    NAMES += ["fin_b", "acc", "up", "mid", "za", "zb", "tot", "fin"]

    def __init__(self, refs):
        for name, ref in zip(self.NAMES, refs):
            setattr(self, name, ref)


def lane_shapes(ring, others, held, finals, rows, columns, dtype):
    half, quarter = rows // 2, rows // 4
    return [
        pltpu.VMEM((others, 4, half, columns), dtype),
        pltpu.VMEM((ring, 4, quarter, columns), dtype),
        pltpu.VMEM((ring, 4, quarter, columns), dtype),
        pltpu.VMEM((held, 2, quarter, columns), dtype),
        pltpu.VMEM((held, 2, quarter, columns), dtype),
        pltpu.VMEM((ring, quarter, columns), dtype),
        pltpu.VMEM((ring, quarter, columns), dtype),
        pltpu.VMEM((held, quarter, columns), dtype),
        pltpu.VMEM((held, quarter, columns), dtype),
        pltpu.VMEM((ring, half, columns), jnp.float32),
        pltpu.VMEM((ring, half, columns), dtype),
        pltpu.VMEM((ring, half, columns), dtype),
        pltpu.VMEM((held + 1, half, columns), dtype),
        pltpu.VMEM((held, half, columns), dtype),
        pltpu.VMEM((ring, half, columns), dtype),
        pltpu.VMEM((finals, half, columns), dtype),
    ]


class Unit:
    def __init__(self, reduce, u):
        at = reduce.at
        self.u, self.small = u, u == REDUCE_WIDE
        if self.small:
            self.lane, self.source, rows = reduce.thin, reduce.small, 32
            self.s, self.o, self.h, self.f, self.z = 0, 0, 0, 0, 0
        else:
            self.lane, self.source, rows = reduce.wide, reduce.grads.at[u % 2], 256
            self.s, self.o, self.h, self.f = u % RING, u % OTHERS, u % HELD, u % FINALS
            self.z = u % (HELD + 1)
        half = rows // 2
        lane, s, h, f, z = self.lane, self.s, self.h, self.f, self.z
        self.half, self.quarter = half, rows // 4
        self.mine = pl.multiple_of(at.core * half, half)
        self.theirs = pl.multiple_of((1 - at.core) * half, half)

        def move(k, src, dst, device):
            return pltpu.make_async_remote_copy(
                src, dst, reduce.send_sem.at[u, k], reduce.recv_sem.at[u, k],
                device_id=device, device_id_type=MESH,
            )

        self.core = move(0, self.source.at[:, pl.ds(self.theirs, half), :], lane.other.at[self.o], at.c_id)
        self.one_a = move(1, lane.one_a.at[s, pl.ds(2, 2)], lane.in_a.at[h], at.x_id)
        self.one_b = move(2, lane.one_b.at[s, pl.ds(2, 2)], lane.in_b.at[h], at.y_id)
        self.two_a = move(3, lane.two_a.at[s], lane.fin_a.at[h], at.y_id)
        self.two_b = move(4, lane.two_b.at[s], lane.fin_b.at[h], at.x_id)
        self.up = move(5, lane.up.at[s], lane.za.at[z], at.z_id)
        self.mid = move(6, lane.mid.at[s], lane.zb.at[h], reduce.m_id)
        self.down = move(7, lane.tot.at[s], lane.za.at[z], at.z_id)
        self.fin_mid = move(8, lane.tot.at[s], lane.fin.at[f], at.c_id)
        self.fin_end = move(8, lane.za.at[z], lane.fin.at[f], at.c_id)
        target = reduce.target(u)

        def store(k, src, start):
            return pltpu.make_async_copy(src, target(start, half), reduce.out_sem.at[u, k])

        self.own_mid = store(0, lane.tot.at[s], self.mine)
        self.own_end = store(0, lane.za.at[z], self.mine)
        self.rest = store(1, lane.fin.at[f], self.theirs)


class Reduce:
    lag = 7
    ticks = REDUCE_WIDE + 1 + lag

    def __init__(self, at, grads, small, outs, small_out, wide, thin, sems):
        self.at, self.grads, self.small, self.outs, self.small_out = at, grads, small, outs, small_out
        self.wide, self.thin = Lane(wide), Lane(thin)
        self.send_sem, self.recv_sem, self.out_sem, self.credit = sems
        self.bx, self.by = lax.rem(at.g, 2), lax.div(at.g, 2)
        self.middle = lax.div(at.z * (3 - at.z), 2)
        self.is_end, self.is_mid = self.middle == 0, self.middle == 1
        self.m_id = (at.g, at.r + self.middle * (6 - 4 * at.z) + (1 - self.middle) * (2 - 4 * at.zb))
        self.units = [Unit(self, u) for u in range(REDUCE_WIDE + 1)]

    def target(self, u):
        outs = self.outs
        if u == REDUCE_WIDE:
            return lambda start, rows: self.small_out.at[pl.ds(start, rows)]
        if u < 4:
            return lambda start, rows: outs[5].at[pl.ds(256 * u + start, rows)]
        if u < 8:
            return lambda start, rows: outs[4].at[pl.ds(start, rows), pl.ds(1024 * (u - 4), 1024)]
        k, lead = {8: (3, None), 9: (2, 0), 10: (2, 1), 11: (2, 2), 12: (1, None), 13: (0, 0), 14: (0, 1), 15: (0, 2)}[u]
        return lambda start, rows: outs[k].at[(pl.ds(start, rows),) if lead is None else (lead, pl.ds(start, rows))]

    def open(self):
        at = self.at
        barrier = pltpu.get_barrier_semaphore()
        for device in (at.x_id, at.y_id, at.c_id, at.z_id):
            pl.semaphore_signal(barrier, inc=1, device_id=device, device_id_type=MESH)

        @pl.when(self.is_mid)
        def _():
            pl.semaphore_signal(barrier, inc=1, device_id=self.m_id, device_id_type=MESH)

        pl.semaphore_wait(barrier, 4 + self.middle)

    def before(self, unit, depth):
        return self.units[unit.u - depth] if unit.u >= depth and not unit.small else None

    def room(self, u):
        old = self.before(self.units[u], 2)
        if old is not None:
            old.core.wait_send()

    def begin(self, unit):
        if not unit.small and unit.u >= OTHERS:
            pl.semaphore_wait(self.credit, 1)
        unit.core.start()

    def join(self, unit):
        lane, q, s, o = unit.lane, unit.quarter, unit.s, unit.o
        unit.core.wait_recv()
        old = self.before(unit, RING)
        if old is not None:
            old.one_a.wait_send()
            old.one_b.wait_send()
        dtype = lane.one_a.dtype
        bx, by, source, mine = self.bx, self.by, unit.source, unit.mine

        def body(j):
            first, second = lax.rem(j, 2), lax.div(j, 2)
            ga = toggled(bx, second) + 2 * toggled(by, first)
            gb = toggled(bx, first) + 2 * toggled(by, second)
            rows_a, rows_b = pl.ds(mine, q), pl.ds(pl.multiple_of(mine + q, q), q)
            lane.one_a[s, j] = (f32(source[ga, rows_a]) + f32(lane.other[o, ga, 0:q])).astype(dtype)
            lane.one_b[s, j] = (f32(source[gb, rows_b]) + f32(lane.other[o, gb, q : 2 * q])).astype(dtype)

        loop(4, body)
        if not unit.small and unit.u + OTHERS < REDUCE_WIDE:
            pl.semaphore_signal(self.credit, inc=1, device_id=self.at.c_id, device_id_type=MESH)
        unit.one_a.start()
        unit.one_b.start()

    def cross(self, unit):
        lane, q, s, h = unit.lane, unit.quarter, unit.s, unit.h
        unit.one_a.wait_recv()
        unit.one_b.wait_recv()
        old = self.before(unit, RING)
        if old is not None:
            old.two_a.wait_send()
            old.two_b.wait_send()
        dtype = lane.one_a.dtype

        def body(rows, after):
            lane.two_a[s, rows] = (f32(lane.one_a[s, 1, rows]) + f32(lane.in_a[h, 1, rows])).astype(dtype)
            lane.two_b[s, rows] = (f32(lane.one_b[s, 1, rows]) + f32(lane.in_b[h, 1, rows])).astype(dtype)
            lane.acc[s, rows] = f32(lane.one_a[s, 0, rows]) + f32(lane.in_a[h, 0, rows])
            lane.acc[s, after(q)] = f32(lane.one_b[s, 0, rows]) + f32(lane.in_b[h, 0, rows])

        each(q, body)
        unit.two_a.start()
        unit.two_b.start()

    def close(self, unit):
        lane, q, s, h = unit.lane, unit.quarter, unit.s, unit.h
        unit.two_a.wait_recv()
        unit.two_b.wait_recv()
        old = self.before(unit, RING)
        dtype = lane.one_a.dtype

        @pl.when(self.is_end)
        def _():
            if old is not None:
                old.up.wait_send()

            def body(rows, after):
                lane.up[s, rows] = (lane.acc[s, rows] + f32(lane.fin_a[h, rows])).astype(dtype)
                lane.up[s, after(q)] = (lane.acc[s, after(q)] + f32(lane.fin_b[h, rows])).astype(dtype)

            each(q, body)
            unit.up.start()

        @pl.when(self.is_mid)
        def _():
            def body(rows, after):
                lane.acc[s, rows] = lane.acc[s, rows] + f32(lane.fin_a[h, rows])
                lane.acc[s, after(q)] = lane.acc[s, after(q)] + f32(lane.fin_b[h, rows])

            each(q, body)

    def climb(self, unit):
        lane, s, h = unit.lane, unit.s, unit.h
        old = self.before(unit, RING)

        @pl.when(self.is_mid)
        def _():
            unit.up.wait_recv()
            if old is not None:
                old.mid.wait_send()

            def body(rows, after):
                lane.mid[s, rows] = (lane.acc[s, rows] + f32(lane.za[unit.z, rows])).astype(lane.mid.dtype)

            each(unit.half, body)
            unit.mid.start()

    def peak(self, unit):
        lane, s, h = unit.lane, unit.s, unit.h
        old = self.before(unit, RING)

        @pl.when(self.is_mid)
        def _():
            unit.mid.wait_recv()
            if old is not None:
                old.down.wait_send()
                old.fin_mid.wait_send()
                old.own_mid.wait()

            def body(rows, after):
                lane.tot[s, rows] = (f32(lane.mid[s, rows]) + f32(lane.zb[h, rows])).astype(lane.tot.dtype)

            each(unit.half, body)
            unit.down.start()
            unit.fin_mid.start()
            unit.own_mid.start()

    def land(self, unit):
        @pl.when(self.is_end)
        def _():
            unit.down.wait_recv()
            unit.fin_end.start()
            unit.own_end.start()

    def finish(self, unit):
        unit.fin_mid.wait_recv()
        unit.rest.start()
        if unit.u > 0:
            self.units[unit.u - 1].rest.wait()

        @pl.when(self.is_end)
        def _():
            unit.fin_end.wait_send()
            unit.own_end.wait()

    def tick(self, t):
        stages = (self.begin, self.join, self.cross, self.close, self.climb, self.peak, self.land, self.finish)
        for lag, stage in enumerate(stages):
            if 0 <= t - lag <= REDUCE_WIDE:
                stage(self.units[t - lag])

    def shut(self):
        for unit in self.units:
            if unit.small or unit.u + 2 >= REDUCE_WIDE:
                unit.core.wait_send()
            if unit.small or unit.u + RING >= REDUCE_WIDE:
                for move in (unit.one_a, unit.one_b, unit.two_a, unit.two_b):
                    move.wait_send()
                pl.when(self.is_end)(unit.up.wait_send)

                @pl.when(self.is_mid)
                def _(unit=unit):
                    unit.mid.wait_send()
                    unit.down.wait_send()
                    unit.fin_mid.wait_send()
                    unit.own_mid.wait()

        self.units[-1].rest.wait()


def columns_sum(ref, block=64):
    def step(i, carry):
        return carry + jnp.sum(f32(ref[cut(i, block)]), axis=0, keepdims=True)

    return lax.fori_loop(0, ref.shape[0] // block, step, jnp.zeros((1, ref.shape[1]), jnp.float32))


def norm_back_rows(values, grad, gain, base, out, low):
    width = grad.shape[1]

    def step(i, carry):
        rows = cut(i, 32)
        v, d = f32(values[rows]), grad[rows]
        center = v - jnp.mean(v, axis=-1, keepdims=True)
        scale = lax.rsqrt(jnp.mean(center * center, axis=-1, keepdims=True) + EPSILON)
        unit = center * scale
        inner = d * gain[...]
        back = inner - jnp.mean(inner, axis=-1, keepdims=True) - unit * jnp.mean(inner * unit, axis=-1, keepdims=True)
        result = f32(base[rows]) + scale * back
        out[rows] = result
        third = carry[2]
        if low is not None:
            rounded = result.astype(jnp.bfloat16)
            low[rows] = rounded
            third = third + jnp.sum(f32(rounded), axis=0, keepdims=True)
        return (
            carry[0] + jnp.sum(d * unit, axis=0, keepdims=True),
            carry[1] + jnp.sum(d, axis=0, keepdims=True),
            third,
        )

    zero = jnp.zeros((1, width), jnp.float32)
    return lax.fori_loop(0, grad.shape[0] // 32, step, (zero, zero, zero))


BACK_WEIGHTS = [(5, 0), (4, 0), (5, 1), (4, 1), (5, 2), (4, 2), (5, 3), (4, 3)]
BACK_WEIGHTS += [(3, None), (2, 0), (1, None), (0, 0), (0, 1), (0, 2), (2, 1), (2, 2)]

BACK_ROOMS = (
    [("ct", (256, 1024), jnp.bfloat16), ("gk", (1024, 1024), jnp.bfloat16), ("slope", (2, 256, 1024), jnp.float32)]
    + [("dz", (1024, 1024), jnp.bfloat16), ("n3", (256, 1024), jnp.bfloat16), ("h", (256, 1024), jnp.float32)]
    + [("dn", (256, 1024), jnp.float32), ("dh", (256, 1024), jnp.float32), ("out", (256, 1024), jnp.float32)]
    + [("low", (256, 1024), jnp.bfloat16), ("ring", (3, 4, 256, 1024), jnp.bfloat16), ("e2", (256, 1024), jnp.bfloat16)]
    + [("o2", (256, 1024), jnp.bfloat16), ("do2", (256, 1024), jnp.bfloat16), ("q2", (256, 1024), jnp.bfloat16)]
    + [("v2", (1024, 1024), jnp.bfloat16), ("dq2", (256, 1024), jnp.bfloat16), ("dk2", (1024, 1024), jnp.bfloat16)]
    + [("dv2", (1024, 1024), jnp.bfloat16), ("n2", (256, 1024), jnp.bfloat16), ("frames", (1024, 1024), jnp.bfloat16)]
    + [("scores", (1024, 256), jnp.float32), ("gscores", (1024, 256), jnp.float32)]
    + [("probs", (1024, 512), jnp.bfloat16), ("gs", (1024, 512), jnp.bfloat16)]
    + [("lse", (16, 8, 256), jnp.float32), ("table", (4, 32, 256), jnp.bfloat16)]
    + [("rows", (16, 1024), jnp.float32), ("hidden", (8, 1024), jnp.float32)]
    + [("grads", (2, 4, 256, 1024), jnp.bfloat16), ("small", (4, 32, 256), jnp.float32)]
)
BACK_INPUTS = ["tokens", "frames", "cotangent"] + [name for name, _, _ in ACTS]


def backward_kernel(*refs):
    n_in = 7 + len(BACK_INPUTS)
    fulls, small_full = refs[:6], refs[6]
    given = dict(zip(BACK_INPUTS, refs[7:n_in]))
    result, grad_tokens, grad_frames = refs[n_in : n_in + 3]
    outs, small_out = refs[n_in + 3 : n_in + 9], refs[n_in + 9]
    refs = refs[n_in + 10 :]
    room = dict(zip([name for name, _, _ in BACK_ROOMS], refs))
    refs = refs[len(BACK_ROOMS) :]
    lane_count = len(Lane.NAMES)
    wide, thin, refs = refs[:lane_count], refs[lane_count : 2 * lane_count], refs[2 * lane_count :]
    sems, load_sem, ring_sem, store_sem = refs[:4], refs[4], refs[5], refs[6]
    at = Spot()
    reduce = Reduce(at, room["grads"], room["small"], outs, small_out, wide, thin, sems)
    ct, gk, dz, v2, small, rows = room["ct"], room["gk"], room["dz"], room["v2"], room["small"], room["rows"]
    n3, h, dn, dh, out, frames = room["n3"], room["h"], room["dn"], room["dh"], room["out"], room["frames"]

    def quarter(ref, m):
        return ref.at[pl.ds(256 * m, 256)]

    loads = {}

    def plan(name, src, dst):
        loads[name] = pltpu.make_async_copy(src, dst, load_sem.at[len(loads)])

    plan("table", small_full, room["table"])
    plan("ct", given["cotangent"], ct)
    for m in range(4):
        plan(f"g{m}", given["g"].at[m], quarter(gk, m))
        plan(f"slope{m}", given["slope"].at[m], room["slope"].at[m % 2])
    plan("n3", given["n3"], n3)
    plan("h2", given["h2"], h)
    plan("o2", given["o2"], room["o2"])
    plan("q2", given["q2"], room["q2"])
    plan("k2", given["k2"], gk)
    plan("v2", given["v2"], v2)
    plan("lse2", given["lse2"], room["lse"])
    plan("frames", given["frames"], frames)
    plan("n2", given["n2"], room["n2"])
    plan("h1", given["h1"], h)
    q1, k1, v1, o1 = (quarter(gk, m) for m in range(4))
    n1, x, e1 = (quarter(v2, m) for m in range(3))
    do1, dq1, dk1, dv1 = (quarter(dz, m) for m in range(4))
    plan("q1", given["q1"], q1)
    plan("k1", given["k1"], k1)
    plan("v1", given["v1"], v1)
    plan("o1", given["o1"], o1)
    plan("lse1", given["lse1"], room["lse"])
    plan("n1", given["n1"], n1)
    plan("x", given["tokens"], x)
    waited = set()

    def load(*names):
        for name in names:
            loads[name].start()

    def have(*names):
        for name in names:
            if name not in waited:
                waited.add(name)
                loads[name].wait()

    fetched, held = set(), set()

    def fetch(i):
        n, lead = BACK_WEIGHTS[i]
        source = fulls[n]
        if n == 4:
            source = source.at[:, :, pl.ds(1024 * lead, 1024)]
        elif lead is not None:
            source = source.at[lead]
        return pltpu.make_async_copy(source, room["ring"].at[i % 3], ring_sem.at[i])

    def weight(i, ahead=2):
        for k in range(i, min(i + ahead + 1, len(BACK_WEIGHTS))):
            if k not in fetched:
                fetched.add(k)
                fetch(k).start()
        if i not in held:
            held.add(i)
            fetch(i).wait()
        return room["ring"].at[i % 3]

    def note(k, row):
        for g in range(4):
            small[g, k : k + 1, :] = row[:, 256 * g : 256 * g + 256]

    def row(k):
        return rows.at[pl.ds(k, 1)]

    def tall(target, left, w, first):
        def body(g):
            columns = cut(g, 256)
            value = dot_nt(left[...], w[g])
            if not first:
                value = target[:, columns] + value
            target[:, columns] = value.astype(target.dtype)

        loop(4, body)

    def start():
        have("table")
        set_rows(room["table"], rows, room["hidden"])
        small[...] = jnp.zeros_like(small)
        have("ct", "g0", "g1", "g2", "g3")
        note(12, columns_sum(ct))

    def feed(m):
        def run():
            w = weight(2 * m)
            have(f"slope{m}")
            if m == 0:
                have("h2")

            def onward(j):
                columns = cut(j, 256)
                value = dot(quarter(gk, m)[...], w[:, :, columns].reshape(-1, 256))
                if m == 0:
                    value = value + h[:, columns] + rows[12:13, columns]
                else:
                    value = value + out[:, columns]
                out[:, columns] = value

            loop(4, onward)

            def back(g):
                columns = cut(g, 256)
                value = dot_nt(ct[...], w[g]) * room["slope"][m % 2, :, columns]
                dz[256 * m : 256 * m + 256, columns] = value.astype(dz.dtype)

            loop(4, back)
            if m < 2:
                load(f"slope{m + 2}")
            sums = columns_sum(quarter(dz, m))
            for k in range(4):
                small[m, 13 + k : 14 + k, :] = sums[:, 256 * k : 256 * k + 256]
            tall(dn, quarter(dz, m), weight(2 * m + 1), m == 0)

        return run

    def write(ref, target, k):
        copy = pltpu.make_async_copy(ref, target, store_sem.at[k])
        copy.start()
        return copy

    stores = []

    def norm3():
        room["low"][...] = out[...].astype(jnp.bfloat16)
        stores.append(write(room["low"], result, 0))
        gain, shift, column = norm_back_rows(h, dn, row(2), ct, dh, room["e2"])
        note(2, gain)
        note(11, shift)
        note(10, column)
        load("h1")

    def out2():
        load("k2", "lse2")
        tall(room["do2"], room["e2"], weight(8), True)

    def cross(first, count):
        def run():
            have("q2", "k2", "v2", "lse2")
            loop(
                count,
                lambda p: attend_back_pair(
                    p + first, room["q2"], gk, v2, room["do2"], room["lse"], room["scores"], room["gscores"],
                    room["probs"], room["gs"], room["dq2"], room["dk2"], room["dv2"], False,
                ),
            )

        return run

    def norm2():
        load("q1", "k1", "v1", "o1", "n1", "x", "lse1")
        note(8, columns_sum(room["dq2"]))
        note(9, columns_sum(room["dv2"]))
        tall(dn, room["dq2"], weight(9), True)
        have("h1")
        gain, shift, column = norm_back_rows(h, dn, row(1), dh, dh, e1)
        note(1, gain)
        note(7, shift)
        note(6, column)

    def out1():
        tall(do1, e1, weight(10), True)

    def self_back(first, count):
        def run():
            have("q1", "k1", "v1", "lse1")
            part = pl.ds(0, 256)
            loop(
                count,
                lambda p: attend_back_pair(
                    p + first, q1, k1, v1, do1, room["lse"], room["scores"].at[part], room["gscores"].at[part],
                    room["probs"].at[part], room["gs"].at[part], dq1, dk1, dv1, True,
                ),
            )

        return run

    def norm1():
        note(4, columns_sum(dq1))
        note(5, columns_sum(dv1))
        for k, grad in enumerate((dq1, dk1, dv1)):
            tall(dn, grad, weight(11 + k), k == 0)
        have("x")
        gain, shift, _ = norm_back_rows(x, dn, row(0), dh, out, None)
        note(0, gain)
        note(3, shift)
        stores.append(write(out, grad_tokens, 1))

    def frames_back(g):
        def run():
            wk, wv = weight(14, 1), weight(15, 0)
            stage = room["scores"] if g % 2 == 0 else room["gscores"]
            if g >= 2:
                stores[g].wait()

            def body(j):
                lines = cut(j, 256)
                stage[lines] = dot_nt(room["dk2"][lines], wk[g]) + dot_nt(room["dv2"][lines], wv[g])

            loop(4, body)
            stores.append(write(stage, grad_frames.at[:, pl.ds(256 * g, 256)], 2 + g))

        return run

    def outer(u, left, right, tokens=256):
        def body(g):
            columns = cut(g, 256)
            value = dot_tn(left[:, columns], right[...])
            room["grads"][u % 2, g] = value.astype(jnp.bfloat16)

        loop(4, body)

    def grad(u):
        reduce.room(u)
        if u < 4:
            for m in range(4):
                value = dot_tn(gk[256 * m : 256 * m + 256, 256 * u : 256 * u + 256], ct[...])
                room["grads"][u % 2, m] = value.astype(jnp.bfloat16)
        elif u < 8:
            have("n3")
            outer(u, n3, quarter(dz, u - 4))
        elif u == 8:
            have("o2")
            outer(u, room["o2"], room["e2"])
        elif u == 9:
            have("n2")
            outer(u, room["n2"], room["dq2"])
        elif u < 12:
            have("frames")
            outer(u, frames, room["dk2"] if u == 10 else room["dv2"])
        elif u == 12:
            have("o1")
            outer(u, o1, e1)
        elif u < 16:
            have("n1")
            outer(u, n1, (dq1, dk1, dv1)[u - 13])

    steps = [("start", -1, 2, start)]
    steps += [(f"feed{m}", -1, 9, feed(m)) for m in range(4)]
    steps += [("norm3", -1, 3, norm3), ("out2", 3, 2, out2)]
    steps += [(f"cross{k}", 3, 9, cross(2 * k, 2)) for k in range(4)]
    steps += [("norm2", -1, 5, norm2), ("out1", 7, 2, out1)]
    steps += [(f"self{k}", 7, 6, self_back(4 * k, 4)) for k in range(2)]
    steps += [("norm1", -1, 8, norm1)]
    steps += [(f"frames{g}", -1, 4, frames_back(g)) for g in range(4)]
    needs = ["start"] * 4 + [f"feed{m}" for m in range(4)] + ["norm3", "cross3", "cross3", "cross3", "norm2"]
    needs += ["self1"] * 3 + ["norm1"]

    load("table", "ct", "g0", "g1", "g2", "g3", "slope0", "h2", "slope1", "n3", "o2", "q2", "v2", "frames", "n2")
    reduce.open()
    done, now, tick, last = set(), 0.0, 0, -100.0
    left = list(steps)
    while left or tick < reduce.ticks:
        can_tick = tick < reduce.ticks and (tick > REDUCE_WIDE or needs[tick] in done)
        can_step = bool(left) and left[0][1] < tick
        if can_tick and (now - last >= BACK_PERIOD or not can_step):
            now = max(now, last + (BACK_PERIOD if not can_step else 0.0))
            last = now
            if tick < REDUCE_WIDE:
                grad(tick)
                now += 3.0
            reduce.tick(tick)
            now += 2.0
            tick += 1
        else:
            name, _, cost, run = left.pop(0)
            run()
            done.add(name)
            now += cost
    reduce.shut()
    stores[0].wait()
    stores[1].wait()
    stores[4].wait()
    stores[5].wait()


BACK_PERIOD = 8.4


def backward_all(full, tokens, frames, cotangent):
    low, wide = jnp.bfloat16, jnp.float32
    width = 1024
    shapes = [
        jax.ShapeDtypeStruct((256, width), low),
        jax.ShapeDtypeStruct((256, width), wide),
        jax.ShapeDtypeStruct((1024, width), wide),
        jax.ShapeDtypeStruct((3, 256, width), low),
        jax.ShapeDtypeStruct((256, width), low),
        jax.ShapeDtypeStruct((3, 256, width), low),
        jax.ShapeDtypeStruct((256, width), low),
        jax.ShapeDtypeStruct((256, 4 * width), low),
        jax.ShapeDtypeStruct((1024, width), low),
        jax.ShapeDtypeStruct((32, 256), wide),
    ]
    weights = list(full[:7])
    weights[5] = weights[5].reshape(4, 4, 256, width)
    args = (*weights, tokens, frames, cotangent, *full[7:])
    anywhere = pl.BlockSpec(memory_space=pl.ANY)
    return pl.pallas_call(
        backward_kernel,
        name="backward_and_reduce",
        out_shape=shapes,
        in_specs=[anywhere] * len(args),
        out_specs=[anywhere] * len(shapes),
        scratch_shapes=[pltpu.VMEM(shape, dtype) for _, shape, dtype in BACK_ROOMS]
        + lane_shapes(RING, OTHERS, HELD, FINALS, 256, width, low)
        + lane_shapes(1, 1, 1, 1, 32, 256, wide)
        + [
            pltpu.SemaphoreType.DMA((REDUCE_WIDE + 1, 9)),
            pltpu.SemaphoreType.DMA((REDUCE_WIDE + 1, 9)),
            pltpu.SemaphoreType.DMA((REDUCE_WIDE + 1, 2)),
            pltpu.SemaphoreType.REGULAR,
            pltpu.SemaphoreType.DMA((32,)),
            pltpu.SemaphoreType.DMA((len(BACK_WEIGHTS),)),
            pltpu.SemaphoreType.DMA((6,)),
        ],
        compiler_params=pltpu.CompilerParams(
            collective_id=1, has_side_effects=True, vmem_limit_bytes=VMEM_LIMIT
        ),
    )(*args)


def widen_pieces(refs):
    self_qkv, self_out, cross_qkv, cross_out, fc1, fc2 = refs
    pieces = [fc2.at[pl.ds(256 * m, 256)] for m in range(4)]
    pieces += [fc1.at[:, pl.ds(1024 * m, 1024)] for m in range(4)]
    pieces += [cross_out] + [cross_qkv.at[m] for m in range(3)] + [self_out] + [self_qkv.at[m] for m in range(3)]
    return pieces


def widen_kernel(*refs):
    result, grad_tokens, grad_frames, grads, small = *refs[:3], refs[3:9], refs[9]
    outs, gains, biases, hidden = refs[10:19], refs[19], refs[20], refs[21]
    low, high, v_result, v_tokens, v_frames, in_sem, out_sem = refs[22:]
    sources = widen_pieces(grads) + [result, grad_tokens, grad_frames]
    targets = widen_pieces(outs[3:]) + list(outs[:3])
    count = len(sources) - 3
    inside = [low.at[k] for k in range(count)] + [v_result, v_tokens, v_frames]
    ready = [high.at[k] for k in range(count)] + [v_result, v_tokens, v_frames]
    loads = [pltpu.make_async_copy(a, b, in_sem.at[k]) for k, (a, b) in enumerate(zip(sources, inside))]
    stores = [pltpu.make_async_copy(a, b, out_sem.at[k]) for k, (a, b) in enumerate(zip(ready, targets))]
    for load in loads:
        load.start()
    gains[...] = small[0:3]
    biases[...] = small[3:13]
    hidden[...] = small[13:17]
    for k in range(count + 3):
        loads[k].wait()
        if k < count:

            def body(i):
                high[k, cut(i, 64)] = f32(low[k, cut(i, 64)])

            loop(4, body)
        stores[k].start()
    for store in stores:
        store.wait()


def widen_all(done):
    wide = jnp.float32
    anywhere, inside = pl.BlockSpec(memory_space=pl.ANY), pl.BlockSpec(memory_space=pltpu.VMEM)
    shapes = [jax.ShapeDtypeStruct(a.shape, a.dtype if k == 0 else wide) for k, a in enumerate(done[:9])]
    shapes += [jax.ShapeDtypeStruct((rows, 256), wide) for rows in (3, 10, 4)]
    return pl.pallas_call(
        widen_kernel,
        name="widen",
        out_shape=shapes,
        in_specs=[anywhere] * 9 + [inside],
        out_specs=[anywhere] * 9 + [inside] * 3,
        scratch_shapes=[
            pltpu.VMEM((16, 256, 1024), jnp.bfloat16),
            pltpu.VMEM((16, 256, 1024), wide),
            pltpu.VMEM(done[0].shape, done[0].dtype),
            pltpu.VMEM(done[1].shape, wide),
            pltpu.VMEM(done[2].shape, wide),
            pltpu.SemaphoreType.DMA((19,)),
            pltpu.SemaphoreType.DMA((19,)),
        ],
        compiler_params=pltpu.CompilerParams(vmem_limit_bytes=VMEM_LIMIT),
    )(*done)


def shards_here(
    tokens,
    frames,
    cotangent,
    self_qkv,
    self_out,
    cross_qkv,
    cross_out,
    fc1_weight,
    fc2_weight,
    gains,
    biases,
    fc1_bias,
):
    part = gains.shape[1]
    small = jnp.concatenate(
        [gains, biases, fc1_bias.reshape(4, part), jnp.zeros((15, part), jnp.bfloat16)], axis=0
    )
    shards = (self_qkv, self_out, cross_qkv, cross_out, fc1_weight, fc2_weight)
    full = forward_all(shards, small, tokens[0], frames[0])
    done = widen_all(backward_all(full, tokens[0], frames[0], cotangent[0]))
    return (done[0][None], done[1][None], done[2][None], *done[3:11], done[11].reshape(-1))


def solution(mesh):
    in_specs = (
        P(("group", "replica"), None, None),
        P(("group", "replica"), None, None),
        P(("group", "replica"), None, None),
        P(None, "group", None),
        P("group", None),
        P(None, "group", None),
        P("group", None),
        P("group", None),
        P("group", None),
        P(None, "group"),
        P(None, "group"),
        P("group"),
    )
    out_specs = (
        P(("group", "replica"), None, None),
        P(("group", "replica"), None, None),
        P(("group", "replica"), None, None),
        P(None, "group", None),
        P("group", None),
        P(None, "group", None),
        P("group", None),
        P("group", None),
        P("group", None),
        P(None, "group"),
        P(None, "group"),
        P("group"),
    )
    here = mesh.shape["group"] == 4 and mesh.shape["replica"] == 8
    body = shards_here if here else shards_any
    return jax.shard_map(body, mesh=mesh, in_specs=in_specs, out_specs=out_specs, check_vma=False)
```

```python
from functools import partial
import math

import jax
import jax.numpy as jnp
from jax import lax
from jax.experimental import pallas as pl
from jax.experimental.pallas import tpu as pltpu
from jax.sharding import PartitionSpec as P

HEADS = 16
HEAD_DIM = 64


EPSILON = 1e-05


def layer_norm(values, gain, shift):
    center = values - jnp.mean(values, axis=-1, keepdims=True)
    spread = jnp.mean(center * center, axis=-1, keepdims=True)
    return center * lax.rsqrt(spread + EPSILON) * gain + shift


def norm_back(values, gain, shift, grad):
    result, pullback = jax.vjp(layer_norm, values, gain, shift)
    return pullback(grad)


def dense(left, right):
    return jnp.dot(left, right, preferred_element_type=jnp.float32)


def left_dense(left, right):
    return lax.dot_general(
        left, right, (((0,), (0,)), ((), ())), preferred_element_type=jnp.float32
    )


def right_dense(grad, weight):
    return lax.dot_general(
        grad, weight, (((1,), (1,)), ((), ())), preferred_element_type=jnp.float32
    )


def column_sum(values):
    return jnp.sum(values.astype(jnp.float32), axis=0)


def split_heads(rows, batch):
    return rows.reshape(batch, -1, HEADS, rows.shape[-1] // HEADS)


def scores_of(query_heads, key_heads, masked):
    scores = jnp.einsum(
        "bqhd,bkhd->bhqk", query_heads, key_heads, preferred_element_type=jnp.float32
    )
    if masked:
        shape = (query_heads.shape[1], key_heads.shape[1])
        allowed = lax.broadcasted_iota(jnp.int32, shape, 0) >= lax.broadcasted_iota(
            jnp.int32, shape, 1
        )
        scores = jnp.where(allowed, scores, -jnp.inf)
    return scores


def attend(queries, keys, values, batch, masked):
    query_heads = split_heads(queries, batch)
    key_heads = split_heads(keys, batch)
    value_heads = split_heads(values, batch)
    scores = scores_of(query_heads, key_heads, masked)
    highest = jnp.max(scores, axis=-1, keepdims=True)
    expo = jnp.exp(scores - highest)
    total = jnp.sum(expo, axis=-1, keepdims=True)
    probs = (expo / total).astype(jnp.bfloat16)
    mixed = jnp.einsum("bhqk,bkhd->bqhd", probs, value_heads, preferred_element_type=jnp.float32)
    return (mixed.reshape(queries.shape).astype(jnp.bfloat16), highest + jnp.log(total))


def attend_back(queries, keys, values, grad_mixed, logsum, batch, masked):
    query_heads = split_heads(queries, batch)
    key_heads = split_heads(keys, batch)
    value_heads = split_heads(values, batch)
    grad_heads = split_heads(grad_mixed, batch)
    probs = jnp.exp(scores_of(query_heads, key_heads, masked) - logsum)
    probs_low = probs.astype(jnp.bfloat16)
    grad_probs = jnp.einsum(
        "bqhd,bkhd->bhqk", grad_heads, value_heads, preferred_element_type=jnp.float32
    )
    grad_values = jnp.einsum(
        "bhqk,bqhd->bkhd", probs_low, grad_heads, preferred_element_type=jnp.float32
    )
    center = jnp.sum(probs * grad_probs, axis=-1, keepdims=True)
    grad_scores = (probs * (grad_probs - center)).astype(jnp.bfloat16)
    grad_queries = jnp.einsum(
        "bhqk,bkhd->bqhd", grad_scores, key_heads, preferred_element_type=jnp.float32
    )
    grad_keys = jnp.einsum(
        "bhqk,bqhd->bkhd", grad_scores, query_heads, preferred_element_type=jnp.float32
    )
    return (
        grad_queries.reshape(queries.shape),
        grad_keys.reshape(keys.shape),
        grad_values.reshape(keys.shape),
    )


def forward(tokens, frames, weights):
    self_qkv, self_out, cross_qkv, cross_out, fc1_weight, fc2_weight, gains, biases, fc1_bias = (
        weights
    )
    batch = tokens.shape[0]
    width = tokens.shape[2]
    scale = 1.0 / math.sqrt(HEAD_DIM)
    gain_rows = gains.astype(jnp.float32)
    bias_rows = biases.astype(jnp.float32)
    resid0 = tokens.reshape(-1, width).astype(jnp.float32)
    frame_rows = frames.reshape(-1, width)
    normed1 = layer_norm(resid0, gain_rows[0], bias_rows[0]).astype(jnp.bfloat16)
    query1 = ((dense(normed1, self_qkv[0]) + bias_rows[1]) * scale).astype(jnp.bfloat16)
    key1 = dense(normed1, self_qkv[1]).astype(jnp.bfloat16)
    value1 = (dense(normed1, self_qkv[2]) + bias_rows[2]).astype(jnp.bfloat16)
    mixed1, logsum1 = attend(query1, key1, value1, batch, True)
    resid1 = resid0 + dense(mixed1, self_out) + bias_rows[3]
    normed2 = layer_norm(resid1, gain_rows[1], bias_rows[4]).astype(jnp.bfloat16)
    query2 = ((dense(normed2, cross_qkv[0]) + bias_rows[5]) * scale).astype(jnp.bfloat16)
    key2 = dense(frame_rows, cross_qkv[1]).astype(jnp.bfloat16)
    value2 = (dense(frame_rows, cross_qkv[2]) + bias_rows[6]).astype(jnp.bfloat16)
    mixed2, logsum2 = attend(query2, key2, value2, batch, False)
    resid2 = resid1 + dense(mixed2, cross_out) + bias_rows[7]
    normed3 = layer_norm(resid2, gain_rows[2], bias_rows[8]).astype(jnp.bfloat16)
    hidden_pre = dense(normed3, fc1_weight) + fc1_bias.astype(jnp.float32)
    hidden = jax.nn.gelu(hidden_pre, approximate=False).astype(jnp.bfloat16)
    result = resid2 + dense(hidden, fc2_weight) + bias_rows[9]
    saved = (
        resid0,
        frame_rows,
        normed1,
        query1,
        key1,
        value1,
        mixed1,
        logsum1,
        resid1,
        normed2,
        query2,
        key2,
        value2,
        mixed2,
        logsum2,
        resid2,
        normed3,
        hidden_pre,
        hidden,
    )
    return (result, saved)


def backward(cotangent, weights, saved, settle_mlp, settle_cross, settle_self):
    self_qkv, self_out, cross_qkv, cross_out, fc1_weight, fc2_weight, gains, biases, fc1_bias = (
        weights
    )
    (
        resid0,
        frame_rows,
        normed1,
        query1,
        key1,
        value1,
        mixed1,
        logsum1,
        resid1,
        normed2,
        query2,
        key2,
        value2,
        mixed2,
        logsum2,
        resid2,
        normed3,
        hidden_pre,
        hidden,
    ) = saved
    batch = cotangent.shape[0]
    width = cotangent.shape[2]
    scale = 1.0 / math.sqrt(HEAD_DIM)
    gain_rows = gains.astype(jnp.float32)
    bias_rows = biases.astype(jnp.float32)
    grad_out = cotangent.reshape(-1, width).astype(jnp.float32)
    grad_branch3 = grad_out.astype(jnp.bfloat16)
    fc2_grad = left_dense(hidden, grad_branch3)
    bias9 = column_sum(grad_branch3)
    grad_hidden = right_dense(grad_branch3, fc2_weight)
    unused, gelu_pull = jax.vjp(partial(jax.nn.gelu, approximate=False), hidden_pre)
    grad_pre = gelu_pull(grad_hidden)[0].astype(jnp.bfloat16)
    fc1_grad = left_dense(normed3, grad_pre)
    fc1_bias_grad = column_sum(grad_pre)
    mlp_part = settle_mlp((fc1_grad, fc2_grad, fc1_bias_grad))
    grad_resid2, gain3, shift3 = norm_back(
        resid2, gain_rows[2], bias_rows[8], right_dense(grad_pre, fc1_weight)
    )
    grad_resid2 = grad_out + grad_resid2
    grad_branch2 = grad_resid2.astype(jnp.bfloat16)
    cross_out_grad = left_dense(mixed2, grad_branch2)
    bias7 = column_sum(grad_branch2)
    grad_mixed2 = right_dense(grad_branch2, cross_out).astype(jnp.bfloat16)
    grad_q2, grad_k2, grad_v2 = attend_back(
        query2, key2, value2, grad_mixed2, logsum2, batch, False
    )
    grad_q2 = (grad_q2.astype(jnp.bfloat16).astype(jnp.float32) * scale).astype(jnp.bfloat16)
    grad_k2 = grad_k2.astype(jnp.bfloat16)
    grad_v2 = grad_v2.astype(jnp.bfloat16)
    cross_qkv_grad = [
        left_dense(normed2, grad_q2),
        left_dense(frame_rows, grad_k2),
        left_dense(frame_rows, grad_v2),
    ]
    bias5 = column_sum(grad_q2)
    bias6 = column_sum(grad_v2)
    cross_part = settle_cross((cross_qkv_grad, cross_out_grad))
    grad_frames = right_dense(grad_k2, cross_qkv[1]) + right_dense(grad_v2, cross_qkv[2])
    grad_resid1, gain2, shift2 = norm_back(
        resid1, gain_rows[1], bias_rows[4], right_dense(grad_q2, cross_qkv[0])
    )
    grad_resid1 = grad_resid2 + grad_resid1
    grad_branch1 = grad_resid1.astype(jnp.bfloat16)
    self_out_grad = left_dense(mixed1, grad_branch1)
    bias3 = column_sum(grad_branch1)
    grad_mixed1 = right_dense(grad_branch1, self_out).astype(jnp.bfloat16)
    grad_q1, grad_k1, grad_v1 = attend_back(query1, key1, value1, grad_mixed1, logsum1, batch, True)
    grad_q1 = (grad_q1.astype(jnp.bfloat16).astype(jnp.float32) * scale).astype(jnp.bfloat16)
    grad_k1 = grad_k1.astype(jnp.bfloat16)
    grad_v1 = grad_v1.astype(jnp.bfloat16)
    self_qkv_grad = [
        left_dense(normed1, grad_q1),
        left_dense(normed1, grad_k1),
        left_dense(normed1, grad_v1),
    ]
    bias1 = column_sum(grad_q1)
    bias2 = column_sum(grad_v1)
    grad_normed1 = (
        right_dense(grad_q1, self_qkv[0])
        + right_dense(grad_k1, self_qkv[1])
        + right_dense(grad_v1, self_qkv[2])
    )
    grad_resid0, gain1, shift1 = norm_back(resid0, gain_rows[0], bias_rows[0], grad_normed1)
    grad_tokens = grad_resid1 + grad_resid0
    gains_grad = jnp.stack([gain1, gain2, gain3])
    biases_grad = jnp.stack(
        [shift1, bias1, bias2, bias3, shift2, bias5, bias6, bias7, shift3, bias9]
    )
    self_part = settle_self((self_qkv_grad, self_out_grad, gains_grad, biases_grad))
    return (grad_tokens, grad_frames, mlp_part, cross_part, self_part)


def unchanged(grads):
    return grads


def shards_any(
    tokens,
    frames,
    cotangent,
    self_qkv,
    self_out,
    cross_qkv,
    cross_out,
    fc1_weight,
    fc2_weight,
    gains,
    biases,
    fc1_bias,
):
    weights = (
        lax.all_gather(self_qkv, "group", axis=1, tiled=True),
        lax.all_gather(self_out, "group", axis=0, tiled=True),
        lax.all_gather(cross_qkv, "group", axis=1, tiled=True),
        lax.all_gather(cross_out, "group", axis=0, tiled=True),
        lax.all_gather(fc1_weight, "group", axis=0, tiled=True),
        lax.all_gather(fc2_weight, "group", axis=0, tiled=True),
        lax.all_gather(gains, "group", axis=1, tiled=True),
        lax.all_gather(biases, "group", axis=1, tiled=True),
        lax.all_gather(fc1_bias, "group", axis=0, tiled=True),
    )
    result, saved = forward(tokens, frames, weights)
    grad_tokens, grad_frames, mlp_part, cross_part, self_part = backward(
        cotangent, weights, saved, unchanged, unchanged, unchanged
    )
    shares = (
        lax.psum_scatter(
            jnp.stack(self_part[0]).astype(jnp.bfloat16), "group", scatter_dimension=1, tiled=True
        ).astype(jnp.float32),
        lax.psum_scatter(
            self_part[1].astype(jnp.bfloat16), "group", scatter_dimension=0, tiled=True
        ).astype(jnp.float32),
        lax.psum_scatter(
            jnp.stack(cross_part[0]).astype(jnp.bfloat16), "group", scatter_dimension=1, tiled=True
        ).astype(jnp.float32),
        lax.psum_scatter(
            cross_part[1].astype(jnp.bfloat16), "group", scatter_dimension=0, tiled=True
        ).astype(jnp.float32),
        lax.psum_scatter(
            mlp_part[0].astype(jnp.bfloat16), "group", scatter_dimension=0, tiled=True
        ).astype(jnp.float32),
        lax.psum_scatter(
            mlp_part[1].astype(jnp.bfloat16), "group", scatter_dimension=0, tiled=True
        ).astype(jnp.float32),
        lax.psum_scatter(
            self_part[2].astype(jnp.bfloat16), "group", scatter_dimension=1, tiled=True
        ).astype(jnp.float32),
        lax.psum_scatter(
            self_part[3].astype(jnp.bfloat16), "group", scatter_dimension=1, tiled=True
        ).astype(jnp.float32),
        lax.psum_scatter(
            mlp_part[2].astype(jnp.bfloat16), "group", scatter_dimension=0, tiled=True
        ).astype(jnp.float32),
    )
    summed = (
        lax.psum(shares[0].astype(jnp.bfloat16), "replica").astype(jnp.float32),
        lax.psum(shares[1].astype(jnp.bfloat16), "replica").astype(jnp.float32),
        lax.psum(shares[2].astype(jnp.bfloat16), "replica").astype(jnp.float32),
        lax.psum(shares[3].astype(jnp.bfloat16), "replica").astype(jnp.float32),
        lax.psum(shares[4].astype(jnp.bfloat16), "replica").astype(jnp.float32),
        lax.psum(shares[5].astype(jnp.bfloat16), "replica").astype(jnp.float32),
        lax.psum(shares[6].astype(jnp.bfloat16), "replica").astype(jnp.float32),
        lax.psum(shares[7].astype(jnp.bfloat16), "replica").astype(jnp.float32),
        lax.psum(shares[8].astype(jnp.bfloat16), "replica").astype(jnp.float32),
    )
    (
        self_qkv_grad,
        self_out_grad,
        cross_qkv_grad,
        cross_out_grad,
        fc1_grad,
        fc2_grad,
        gains_grad,
        biases_grad,
        fc1_bias_grad,
    ) = summed
    return (
        result.reshape(tokens.shape).astype(jnp.bfloat16),
        grad_tokens.reshape(tokens.shape),
        grad_frames.reshape(frames.shape),
        self_qkv_grad,
        self_out_grad,
        cross_qkv_grad,
        cross_out_grad,
        fc1_grad,
        fc2_grad,
        gains_grad,
        biases_grad,
        fc1_bias_grad,
    )


MESH = pl.DeviceIdType.MESH
VMEM_LIMIT = 64 * 1024 * 1024 - 128 * 1024


class Spot:
    def __init__(self):
        self.g = lax.axis_index("group")
        self.r = lax.axis_index("replica")
        self.core = lax.rem(self.r, 2)
        self.z = lax.div(self.r, 2)
        self.zb = lax.rem(self.z, 2)
        self.gx = self.g + 1 - 2 * lax.rem(self.g, 2)
        self.gy = lax.rem(self.g + 2, 4)
        self.gd = self.gx + 2 - 4 * lax.div(self.gx, 2)
        self.rc = self.r + 1 - 2 * self.core
        self.rz = self.r + 2 - 4 * self.zb
        self.x_id = (self.gx, self.r)
        self.y_id = (self.gy, self.r)
        self.d_id = (self.gd, self.r)
        self.c_id = (self.g, self.rc)
        self.z_id = (self.g, self.rz)


def meet(*ids):
    barrier = pltpu.get_barrier_semaphore()
    for device in ids:
        pl.semaphore_signal(barrier, inc=1, device_id=device, device_id_type=MESH)
    pl.semaphore_wait(barrier, len(ids))


GATHER_CHUNKS = (
    [(0, m, 0, 256, 0, 1024, m != 0) for m in range(3)]
    + [(1, None, 0, 256, 0, 1024, False)]
    + [(2, m, 0, 256, 0, 1024, m != 0) for m in range(3)]
    + [(3, None, 0, 256, 0, 1024, False)]
    + [(4, None, 0, 256, 1024 * m, 1024, m != 3) for m in range(4)]
    + [(5, None, 256 * m, 256, 0, 1024, m != 3) for m in range(4)]
)
N_GATHER = len(GATHER_CHUNKS)


class Gather:
    def __init__(self, at, shards, small, fulls, small_full, stages, small_stage, sems):
        self.load_sem, self.put_sem, self.send_sem, self.recv_sem, small_send, small_recv, small_local = sems
        self.at, self.shards, self.fulls = at, shards, fulls
        self.loads = [pltpu.make_async_copy(shards[n], stages[n], self.load_sem.at[n]) for n in range(6)]
        self.small_load = pltpu.make_async_copy(small, small_stage, small_local.at[0])
        self.small_put = pltpu.make_async_copy(small_stage, small_full.at[at.g], small_local.at[1])
        self.small_copies = [
            pltpu.make_async_remote_copy(
                small, small_full.at[at.g], small_send.at[n], small_recv.at[n],
                device_id=device, device_id_type=MESH,
            )
            for n, device in enumerate((at.x_id, at.y_id, at.d_id))
        ]
        self.puts = []
        for n in range(6):
            where = (slice(None), at.g) if n in (0, 2) else (at.g,)
            self.puts.append(pltpu.make_async_copy(stages[n], fulls[n].at[where], self.put_sem.at[n]))
        self.plans = [self.plan(i) for i in range(N_GATHER)]
        self.arrived, self.placed = set(), set()

    def full(self, i, g, start, rows):
        n, lead, first, _, column, columns, _ = GATHER_CHUNKS[i]
        where = (g, pl.ds(first + start, rows), pl.ds(column, columns))
        return self.fulls[n].at[where if lead is None else (lead,) + where]

    def shard(self, i, start, rows):
        n, lead, first, _, column, columns, _ = GATHER_CHUNKS[i]
        where = (pl.ds(first + start, rows), pl.ds(column, columns))
        return self.shards[n].at[where if lead is None else (lead,) + where]

    def plan(self, i):
        at = self.at

        def put(k, src, g, start, rows, device):
            return pltpu.make_async_remote_copy(
                src, self.full(i, g, start, rows), self.send_sem.at[i, k], self.recv_sem.at[i, k],
                device_id=device, device_id_type=MESH,
            )

        rows, split = GATHER_CHUNKS[i][3], GATHER_CHUNKS[i][6]
        half = rows // 2
        base = pl.multiple_of(at.core * half, half)
        core_base = base
        if split:
            half = half // 2
            base = pl.multiple_of(base + at.zb * half, half)
        quarter = half // 2
        mine = self.shard(i, base, half)
        moves = [
            put(0, mine, at.g, base, half, at.x_id),
            put(1, mine, at.g, base, half, at.y_id),
            put(2, self.full(i, at.gy, base + quarter, quarter), at.gy, base + quarter, quarter, at.x_id),
            put(3, self.full(i, at.gx, base, quarter), at.gx, base, quarter, at.y_id),
        ]
        for k, g in enumerate((at.gx, at.gy, at.gd)):
            moves.append(put(4 + k, self.full(i, g, core_base, rows // 2), g, core_base, rows // 2, at.c_id))
        if split:
            for k, g in enumerate((at.gx, at.gy, at.gd)):
                moves.append(put(7 + k, self.full(i, g, base, half), g, base, half, at.z_id))
        return moves, split

    def open(self):
        at = self.at
        for load in self.loads:
            load.start()
        self.small_load.start()
        meet(at.x_id, at.y_id, at.d_id, at.c_id, at.z_id)
        self.begin(0)
        for copy in self.small_copies:
            copy.start()
        self.begin(1)
        self.small_load.wait()
        self.small_put.start()
        for n in range(6):
            self.loads[n].wait()
            self.puts[n].start()

    def small_ready(self):
        self.small_put.wait()
        for copy in self.small_copies:
            copy.wait()

    def begin(self, i):
        moves, _ = self.plans[i]
        moves[0].start()
        moves[1].start()

    def second(self, i):
        moves, split = self.plans[i]
        moves[0].wait_recv()
        moves[1].wait_recv()
        moves[2].start()
        moves[3].start()
        for k in (7, 8) if split else (4, 5):
            moves[k].start()

    def third(self, i):
        moves, split = self.plans[i]
        moves[2].wait_recv()
        moves[3].wait_recv()
        moves[9 if split else 6].start()

    def fourth(self, i):
        moves, split = self.plans[i]
        if split:
            for k in (7, 8, 9):
                moves[k].wait_recv()
            for k in (4, 5, 6):
                moves[k].start()

    ticks = N_GATHER + 2

    def tick(self, i):
        if i < N_GATHER:
            self.second(i)
        if i + 2 < N_GATHER:
            self.begin(i + 2)
        if 0 <= i - 1 < N_GATHER:
            self.third(i - 1)
        if 0 <= i - 2 < N_GATHER:
            self.fourth(i - 2)

    def ready(self, i):
        n = GATHER_CHUNKS[i][0]
        if n not in self.placed:
            self.placed.add(n)
            self.puts[n].wait()
        if i not in self.arrived:
            self.arrived.add(i)
            for k in (4, 5, 6):
                self.plans[i][0][k].wait_recv()

    def close(self):
        for i in range(N_GATHER):
            self.ready(i)
            moves, split = self.plans[i]
            for k in range(10 if split else 7):
                moves[k].wait_send()


def f32(value):
    return value.astype(jnp.float32)


def dot(left, right):
    return jnp.dot(left, right, preferred_element_type=jnp.float32)


def dot_tn(left, right):
    return lax.dot_general(left, right, (((0,), (0,)), ((), ())), preferred_element_type=jnp.float32)


def dot_nt(left, right):
    return lax.dot_general(left, right, (((1,), (1,)), ((), ())), preferred_element_type=jnp.float32)


def loop(count, body):
    def step(i, carry):
        body(i)
        return carry

    lax.fori_loop(0, count, step, 0)


def cut(i, size):
    return pl.ds(pl.multiple_of(i * size, size), size)


def norm_rows(src, dst, gain, shift):
    def body(i):
        values = f32(src[cut(i, 32)])
        center = values - jnp.mean(values, axis=-1, keepdims=True)
        spread = jnp.mean(center * center, axis=-1, keepdims=True)
        dst[cut(i, 32)] = (center * lax.rsqrt(spread + EPSILON) * gain[...] + shift[...]).astype(dst.dtype)

    loop(src.shape[0] // 32, body)


def product(left, weight, store, tile=256):
    def body(j):
        columns = cut(j, tile)
        store(columns, dot(left[...], weight[:, :, columns].reshape(-1, tile)))

    loop(weight.shape[-1] // tile, body)


def attend_pair(p, q, k, v, o, lse, scores, probs, causal):
    columns = cut(p, 128)
    keys, count = k.shape[0], q.shape[0]
    qq, kk, vv = q[:, columns], k[:, columns], v[:, columns]
    lane = lax.broadcasted_iota(jnp.int32, qq.shape, 1)
    vt = vv.T
    block = 128
    sides = []
    for a in range(2):
        qa = jnp.where((lane < 64) if a == 0 else (lane >= 64), qq, jnp.zeros_like(qq))
        scores[...] = dot_nt(kk, qa)

        def rows_of(j):
            part = scores[cut(j, block)]
            if causal:
                key = lax.broadcasted_iota(jnp.int32, part.shape, 0) + j * block
                query = lax.broadcasted_iota(jnp.int32, part.shape, 1)
                part = jnp.where(query >= key, part, -jnp.inf)
            return part

        def top(j, carry):
            return jnp.maximum(carry, jnp.max(rows_of(j), axis=0, keepdims=True))

        highest = lax.fori_loop(0, keys // block, top, jnp.full((1, count), -jnp.inf, jnp.float32))

        def expo(j, carry):
            e = jnp.exp(rows_of(j) - highest)
            scores[cut(j, block)] = e
            return carry + jnp.sum(e, axis=0, keepdims=True)

        total = lax.fori_loop(0, keys // block, expo, jnp.zeros((1, count), jnp.float32))
        share = 1.0 / total

        def rounded(j):
            probs[cut(j, block)] = (scores[cut(j, block)] * share).astype(probs.dtype)

        loop(keys // block, rounded)
        lse[2 * p + a] = jnp.broadcast_to(highest + jnp.log(total), (8, count))
        sides.append(dot(vt[64 * a : 64 * a + 64], probs[...]))
    o[:, columns] = jnp.concatenate(sides, axis=0).T.astype(o.dtype)


def attend_back_pair(p, q, k, v, go, lse, scores, gscores, probs, gs, gq, gk, gv, causal):
    columns = cut(p, 128)
    keys, count = k.shape[0], q.shape[0]
    qq, kk, vv, dd = q[:, columns], k[:, columns], v[:, columns], go[:, columns]
    lane = lax.broadcasted_iota(jnp.int32, qq.shape, 1)
    zero = jnp.zeros_like(qq)
    kt = kk.T
    block = 128
    sides, qs, ds = [], [], []
    for a in range(2):
        here = (lane < 64) if a == 0 else (lane >= 64)
        qa, da = jnp.where(here, qq, zero), jnp.where(here, dd, zero)
        qs.append(qa)
        ds.append(da)
        scores[...] = dot_nt(kk, qa)
        gscores[...] = dot_nt(vv, da)
        line = lse[2 * p + a][0:1]
        across = slice(a * count, (a + 1) * count)

        def first(j, carry):
            part = scores[cut(j, block)]
            if causal:
                key = lax.broadcasted_iota(jnp.int32, part.shape, 0) + j * block
                query = lax.broadcasted_iota(jnp.int32, part.shape, 1)
                part = jnp.where(query >= key, part, -jnp.inf)
            e = jnp.exp(part - line)
            scores[cut(j, block)] = e
            probs[cut(j, block), across] = e.astype(probs.dtype)
            return carry + jnp.sum(e * gscores[cut(j, block)], axis=0, keepdims=True)

        center = lax.fori_loop(0, keys // block, first, jnp.zeros((1, count), jnp.float32))

        def second(j):
            rows = cut(j, block)
            gs[rows, across] = (scores[rows] * (gscores[rows] - center)).astype(gs.dtype)

        loop(keys // block, second)
        sides.append(dot(kt[64 * a : 64 * a + 64], gs[:, across]))
    gv[:, columns] = dot(probs[...], jnp.concatenate(ds, axis=0)).astype(gv.dtype)
    gk[:, columns] = dot(gs[...], jnp.concatenate(qs, axis=0)).astype(gk.dtype)
    side = jnp.concatenate(sides, axis=0).T.astype(jnp.bfloat16)
    gq[:, columns] = (f32(side) * SCALE).astype(gq.dtype)

def woven(ticks, period, first, steps):
    order, now, tick = [], 0.0, 0
    left = list(range(len(steps)))
    while left or tick < ticks:
        due = first + tick * period
        if left and steps[left[0]][0] < tick and (now < due or tick >= ticks):
            now += steps[left[0]][1]
            order.append(("step", left.pop(0)))
        else:
            now = max(now, due)
            order.append(("tick", tick))
            tick += 1
    return order


ACTS = (
    [("n1", (256, 1024), jnp.bfloat16), ("q1", (256, 1024), jnp.bfloat16), ("k1", (256, 1024), jnp.bfloat16)]
    + [("v1", (256, 1024), jnp.bfloat16), ("o1", (256, 1024), jnp.bfloat16), ("lse1", (16, 8, 256), jnp.float32)]
    + [("h1", (256, 1024), jnp.float32), ("n2", (256, 1024), jnp.bfloat16), ("q2", (256, 1024), jnp.bfloat16)]
    + [("k2", (1024, 1024), jnp.bfloat16), ("v2", (1024, 1024), jnp.bfloat16), ("o2", (256, 1024), jnp.bfloat16)]
    + [("lse2", (16, 8, 256), jnp.float32), ("h2", (256, 1024), jnp.float32), ("n3", (256, 1024), jnp.bfloat16)]
    + [("slope", (4, 256, 1024), jnp.float32), ("g", (4, 256, 1024), jnp.bfloat16)]
)
N_ACTS = len(ACTS)
SCALE = 0.125


def set_rows(small_full, rows, hidden):
    for g in range(4):
        for k in range(13):
            rows[k : k + 1, 256 * g : 256 * g + 256] = f32(small_full[g, k : k + 1])
        for k in range(4):
            hidden[g : g + 1, 256 * k : 256 * k + 256] = f32(small_full[g, 13 + k : 14 + k])


def forward_kernel(*refs):
    shards, small, tokens, frames = refs[:6], refs[6], refs[7], refs[8]
    fulls, small_full = refs[9:15], refs[15]
    saved = refs[16 : 16 + N_ACTS]
    refs = refs[16 + N_ACTS :]
    acts = dict(zip([name for name, _, _ in ACTS], refs[:N_ACTS]))
    refs = refs[N_ACTS:]
    stages, small_stage, sems = refs[:6], refs[6], refs[7:14]
    x, kept, table, rows, hidden, ring, scores1, probs1, scores2, probs2, in_sem, ring_sem, save_sem = refs[14:]
    at = Spot()
    gather = Gather(at, shards, small, fulls, small_full, stages, small_stage, sems)

    x_load = pltpu.make_async_copy(tokens, x, in_sem.at[0])
    frames_load = pltpu.make_async_copy(frames, kept, in_sem.at[1])
    table_load = pltpu.make_async_copy(small_full, table, in_sem.at[2])
    x_load.start()
    frames_load.start()
    gather.open()
    saves = []

    def save(*names):
        for name in names:
            k = [n for n, _, _ in ACTS].index(name)
            copy = pltpu.make_async_copy(acts[name], saved[k], save_sem.at[k])
            copy.start()
            saves.append(copy)

    def fetch(i):
        n, lead, _, _, column, columns, _ = GATHER_CHUNKS[i]
        source = fulls[n] if lead is None else fulls[n].at[lead]
        if n == 4:
            source = source.at[:, :, pl.ds(column, columns)]
        return pltpu.make_async_copy(source, ring.at[i % 3], ring_sem.at[i])

    fetched = set()
    done_ticks = [0]

    def weight(i):
        for k in (i, i + 1):
            if k not in fetched and k < 12 and (k == i or k + 2 < done_ticks[0]):
                fetched.add(k)
                gather.ready(k)
                fetch(k).start()
        fetch(i).wait()
        return ring.at[i % 3]

    def row(k):
        return rows.at[k : k + 1]

    def start():
        gather.small_ready()
        table_load.start()
        x_load.wait()
        table_load.wait()
        set_rows(table, rows, hidden)
        norm_rows(x, acts["n1"], row(0), row(3))
        save("n1")

    def project(name, i, source, bias, scale):
        def run():
            w, target = weight(i), acts[name]

            def store(columns, value):
                if bias is not None:
                    value = value + rows[bias : bias + 1, columns]
                if scale:
                    value = value * SCALE
                target[:, columns] = value.astype(target.dtype)

            product(acts[source], w, store)
            save(name)

        return run

    def project_frames(name, i, bias):
        def run():
            if i == 5:
                frames_load.wait()
            w, target = weight(i), acts[name]

            def body(j):
                columns = cut(j, 256)
                value = dot(kept[...], w[:, :, columns].reshape(-1, 256))
                if bias is not None:
                    value = value + rows[bias : bias + 1, columns]
                target[:, columns] = value.astype(target.dtype)

            loop(4, body)
            save(name)

        return run

    def attend(first, count, q, k, v, o, lse, scores, probs, causal, last):
        def run():
            loop(
                count,
                lambda p: attend_pair(
                    p + first, acts[q], acts[k], acts[v], acts[o], acts[lse], scores, probs, causal
                ),
            )
            if last:
                save(o, lse)

        return run

    def join(i, source, base, bias, target, gain, shift, normed):
        def run():
            w, out = weight(i), acts[target]

            def store(columns, value):
                out[:, columns] = f32(base[:, columns]) + value + rows[bias : bias + 1, columns]

            product(acts[source], w, store)
            norm_rows(out, acts[normed], row(gain), row(shift))
            save(target, normed)

        return run

    def expand(m):
        def run():
            w = weight(8 + m)
            slope, g = acts["slope"], acts["g"]

            def store(columns, value):
                z = value + hidden[m : m + 1, columns]
                below = 0.5 + 0.5 * lax.erf(z * math.sqrt(0.5))
                slope[m, :, columns] = below + z * (jnp.exp(-0.5 * z * z) * (1.0 / math.sqrt(2.0 * math.pi)))
                g[m, :, columns] = (z * below).astype(g.dtype)

            product(acts["n3"], w, store)
            if m == 3:
                save("slope", "g")

        return run

    steps = [(0, 3, start)]
    steps += [(2, 3, project("q1", 0, "n1", 3 + 1, True)), (3, 3, project("k1", 1, "n1", None, False))]
    steps += [(4, 3, project("v1", 2, "n1", 3 + 2, False))]
    for part in range(2):
        steps.append((4, 6, attend(4 * part, 4, "q1", "k1", "v1", "o1", "lse1", scores1, probs1, True, part == 1)))
    steps.append((5, 5, join(3, "o1", x, 3 + 3, "h1", 1, 3 + 4, "n2")))
    steps += [(6, 3, project("q2", 4, "n2", 3 + 5, True)), (7, 6, project_frames("k2", 5, None))]
    steps += [(8, 6, project_frames("v2", 6, 3 + 6))]
    for part in range(4):
        steps.append((8, 5, attend(2 * part, 2, "q2", "k2", "v2", "o2", "lse2", scores2, probs2, False, part == 3)))
    steps.append((9, 5, join(7, "o2", acts["h1"], 3 + 7, "h2", 2, 3 + 8, "n3")))
    for m in range(4):
        steps.append((10 + m, 6, expand(m)))
    for kind, i in woven(gather.ticks, 5.5, 4.0, steps):
        if kind == "tick":
            gather.tick(i)
            done_ticks[0] = i + 1
        else:
            steps[i][2]()
    gather.close()
    for copy in saves:
        copy.wait()


def forward_all(shards, small, tokens, frames):
    shapes = []
    for array in shards:
        lead, tail = array.shape[:-2], array.shape[-2:]
        shapes.append(jax.ShapeDtypeStruct(lead + (4,) + tail, array.dtype))
    shapes.append(jax.ShapeDtypeStruct((4,) + small.shape, small.dtype))
    shapes += [jax.ShapeDtypeStruct(shape, dtype) for _, shape, dtype in ACTS]
    anywhere = pl.BlockSpec(memory_space=pl.ANY)
    low = jnp.bfloat16
    return pl.pallas_call(
        forward_kernel,
        name="gather_and_forward",
        out_shape=shapes,
        in_specs=[anywhere] * 9,
        out_specs=[anywhere] * len(shapes),
        scratch_shapes=[pltpu.VMEM(shape, dtype) for _, shape, dtype in ACTS]
        + [pltpu.VMEM(array.shape, array.dtype) for array in shards]
        + [
            pltpu.VMEM(small.shape, small.dtype),
            pltpu.SemaphoreType.DMA((6,)),
            pltpu.SemaphoreType.DMA((6,)),
            pltpu.SemaphoreType.DMA((N_GATHER, 10)),
            pltpu.SemaphoreType.DMA((N_GATHER, 10)),
            pltpu.SemaphoreType.DMA((3,)),
            pltpu.SemaphoreType.DMA((3,)),
            pltpu.SemaphoreType.DMA((2,)),
            pltpu.VMEM(tokens.shape, low),
            pltpu.VMEM(frames.shape, low),
            pltpu.VMEM((4,) + small.shape, low),
            pltpu.VMEM((16, 1024), jnp.float32),
            pltpu.VMEM((8, 1024), jnp.float32),
            pltpu.VMEM((3, 4, 256, 1024), low),
            pltpu.VMEM((256, 256), jnp.float32),
            pltpu.VMEM((256, 256), low),
            pltpu.VMEM((1024, 256), jnp.float32),
            pltpu.VMEM((1024, 256), low),
            pltpu.SemaphoreType.DMA((3,)),
            pltpu.SemaphoreType.DMA((12,)),
            pltpu.SemaphoreType.DMA((N_ACTS,)),
        ],
        compiler_params=pltpu.CompilerParams(
            collective_id=0, has_side_effects=True, vmem_limit_bytes=VMEM_LIMIT
        ),
    )(*shards, small, tokens, frames)


REDUCE_WIDE = 16
RING, OTHERS, HELD, FINALS = 3, 4, 4, 8


def each(rows, body):
    block = min(rows, 16)
    loop(rows // block, lambda i: body(cut(i, block), lambda k: pl.ds(pl.multiple_of(k + i * block, block), block)))


def toggled(bit, flip):
    return bit + flip - 2 * bit * flip


class Lane:
    NAMES = ["other", "one_a", "one_b", "in_a", "in_b", "two_a", "two_b", "fin_a"]
    NAMES += ["fin_b", "acc", "up", "mid", "za", "zb", "tot", "fin"]

    def __init__(self, refs):
        for name, ref in zip(self.NAMES, refs):
            setattr(self, name, ref)


def lane_shapes(ring, others, held, finals, rows, columns, dtype):
    half, quarter = rows // 2, rows // 4
    return [
        pltpu.VMEM((others, 4, half, columns), dtype),
        pltpu.VMEM((ring, 4, quarter, columns), dtype),
        pltpu.VMEM((ring, 4, quarter, columns), dtype),
        pltpu.VMEM((held, 2, quarter, columns), dtype),
        pltpu.VMEM((held, 2, quarter, columns), dtype),
        pltpu.VMEM((ring, quarter, columns), dtype),
        pltpu.VMEM((ring, quarter, columns), dtype),
        pltpu.VMEM((held, quarter, columns), dtype),
        pltpu.VMEM((held, quarter, columns), dtype),
        pltpu.VMEM((ring, half, columns), jnp.float32),
        pltpu.VMEM((ring, half, columns), dtype),
        pltpu.VMEM((ring, half, columns), dtype),
        pltpu.VMEM((held + 1, half, columns), dtype),
        pltpu.VMEM((held, half, columns), dtype),
        pltpu.VMEM((ring, half, columns), dtype),
        pltpu.VMEM((finals, half, columns), dtype),
    ]


class Unit:
    def __init__(self, reduce, u):
        at = reduce.at
        self.u, self.small = u, u == REDUCE_WIDE
        if self.small:
            self.lane, self.source, rows = reduce.thin, reduce.small, 32
            self.s, self.o, self.h, self.f, self.z = 0, 0, 0, 0, 0
        else:
            self.lane, self.source, rows = reduce.wide, reduce.grads.at[u % 2], 256
            self.s, self.o, self.h, self.f = u % RING, u % OTHERS, u % HELD, u % FINALS
            self.z = u % (HELD + 1)
        half = rows // 2
        lane, s, h, f, z = self.lane, self.s, self.h, self.f, self.z
        self.half, self.quarter = half, rows // 4
        self.mine = pl.multiple_of(at.core * half, half)
        self.theirs = pl.multiple_of((1 - at.core) * half, half)

        def move(k, src, dst, device):
            return pltpu.make_async_remote_copy(
                src, dst, reduce.send_sem.at[u, k], reduce.recv_sem.at[u, k],
                device_id=device, device_id_type=MESH,
            )

        self.core = move(0, self.source.at[:, pl.ds(self.theirs, half), :], lane.other.at[self.o], at.c_id)
        self.one_a = move(1, lane.one_a.at[s, pl.ds(2, 2)], lane.in_a.at[h], at.x_id)
        self.one_b = move(2, lane.one_b.at[s, pl.ds(2, 2)], lane.in_b.at[h], at.y_id)
        self.two_a = move(3, lane.two_a.at[s], lane.fin_a.at[h], at.y_id)
        self.two_b = move(4, lane.two_b.at[s], lane.fin_b.at[h], at.x_id)
        self.up = move(5, lane.up.at[s], lane.za.at[z], at.z_id)
        self.mid = move(6, lane.mid.at[s], lane.zb.at[h], reduce.m_id)
        self.down = move(7, lane.tot.at[s], lane.za.at[z], at.z_id)
        self.fin_mid = move(8, lane.tot.at[s], lane.fin.at[f], at.c_id)
        self.fin_end = move(8, lane.za.at[z], lane.fin.at[f], at.c_id)
        target = reduce.target(u)

        def store(k, src, start):
            return pltpu.make_async_copy(src, target(start, half), reduce.out_sem.at[u, k])

        self.own_mid = store(0, lane.tot.at[s], self.mine)
        self.own_end = store(0, lane.za.at[z], self.mine)
        self.rest = store(1, lane.fin.at[f], self.theirs)


class Reduce:
    lag = 7
    ticks = REDUCE_WIDE + 1 + lag

    def __init__(self, at, grads, small, outs, small_out, wide, thin, sems):
        self.at, self.grads, self.small, self.outs, self.small_out = at, grads, small, outs, small_out
        self.wide, self.thin = Lane(wide), Lane(thin)
        self.send_sem, self.recv_sem, self.out_sem, self.credit = sems
        self.bx, self.by = lax.rem(at.g, 2), lax.div(at.g, 2)
        self.middle = lax.div(at.z * (3 - at.z), 2)
        self.is_end, self.is_mid = self.middle == 0, self.middle == 1
        self.m_id = (at.g, at.r + self.middle * (6 - 4 * at.z) + (1 - self.middle) * (2 - 4 * at.zb))
        self.units = [Unit(self, u) for u in range(REDUCE_WIDE + 1)]

    def target(self, u):
        outs = self.outs
        if u == REDUCE_WIDE:
            return lambda start, rows: self.small_out.at[pl.ds(start, rows)]
        if u < 4:
            return lambda start, rows: outs[5].at[pl.ds(256 * u + start, rows)]
        if u < 8:
            return lambda start, rows: outs[4].at[pl.ds(start, rows), pl.ds(1024 * (u - 4), 1024)]
        k, lead = {8: (3, None), 9: (2, 0), 10: (2, 1), 11: (2, 2), 12: (1, None), 13: (0, 0), 14: (0, 1), 15: (0, 2)}[u]
        return lambda start, rows: outs[k].at[(pl.ds(start, rows),) if lead is None else (lead, pl.ds(start, rows))]

    def open(self):
        at = self.at
        barrier = pltpu.get_barrier_semaphore()
        for device in (at.x_id, at.y_id, at.c_id, at.z_id):
            pl.semaphore_signal(barrier, inc=1, device_id=device, device_id_type=MESH)

        @pl.when(self.is_mid)
        def _():
            pl.semaphore_signal(barrier, inc=1, device_id=self.m_id, device_id_type=MESH)

        pl.semaphore_wait(barrier, 4 + self.middle)

    def before(self, unit, depth):
        return self.units[unit.u - depth] if unit.u >= depth and not unit.small else None

    def room(self, u):
        old = self.before(self.units[u], 2)
        if old is not None:
            old.core.wait_send()

    def begin(self, unit):
        if not unit.small and unit.u >= OTHERS:
            pl.semaphore_wait(self.credit, 1)
        unit.core.start()

    def join(self, unit):
        lane, q, s, o = unit.lane, unit.quarter, unit.s, unit.o
        unit.core.wait_recv()
        old = self.before(unit, RING)
        if old is not None:
            old.one_a.wait_send()
            old.one_b.wait_send()
        dtype = lane.one_a.dtype
        bx, by, source, mine = self.bx, self.by, unit.source, unit.mine

        def body(j):
            first, second = lax.rem(j, 2), lax.div(j, 2)
            ga = toggled(bx, second) + 2 * toggled(by, first)
            gb = toggled(bx, first) + 2 * toggled(by, second)
            rows_a, rows_b = pl.ds(mine, q), pl.ds(pl.multiple_of(mine + q, q), q)
            lane.one_a[s, j] = (f32(source[ga, rows_a]) + f32(lane.other[o, ga, 0:q])).astype(dtype)
            lane.one_b[s, j] = (f32(source[gb, rows_b]) + f32(lane.other[o, gb, q : 2 * q])).astype(dtype)

        loop(4, body)
        if not unit.small and unit.u + OTHERS < REDUCE_WIDE:
            pl.semaphore_signal(self.credit, inc=1, device_id=self.at.c_id, device_id_type=MESH)
        unit.one_a.start()
        unit.one_b.start()

    def cross(self, unit):
        lane, q, s, h = unit.lane, unit.quarter, unit.s, unit.h
        unit.one_a.wait_recv()
        unit.one_b.wait_recv()
        old = self.before(unit, RING)
        if old is not None:
            old.two_a.wait_send()
            old.two_b.wait_send()
        dtype = lane.one_a.dtype

        def body(rows, after):
            lane.two_a[s, rows] = (f32(lane.one_a[s, 1, rows]) + f32(lane.in_a[h, 1, rows])).astype(dtype)
            lane.two_b[s, rows] = (f32(lane.one_b[s, 1, rows]) + f32(lane.in_b[h, 1, rows])).astype(dtype)
            lane.acc[s, rows] = f32(lane.one_a[s, 0, rows]) + f32(lane.in_a[h, 0, rows])
            lane.acc[s, after(q)] = f32(lane.one_b[s, 0, rows]) + f32(lane.in_b[h, 0, rows])

        each(q, body)
        unit.two_a.start()
        unit.two_b.start()

    def close(self, unit):
        lane, q, s, h = unit.lane, unit.quarter, unit.s, unit.h
        unit.two_a.wait_recv()
        unit.two_b.wait_recv()
        old = self.before(unit, RING)
        dtype = lane.one_a.dtype

        @pl.when(self.is_end)
        def _():
            if old is not None:
                old.up.wait_send()

            def body(rows, after):
                lane.up[s, rows] = (lane.acc[s, rows] + f32(lane.fin_a[h, rows])).astype(dtype)
                lane.up[s, after(q)] = (lane.acc[s, after(q)] + f32(lane.fin_b[h, rows])).astype(dtype)

            each(q, body)
            unit.up.start()

        @pl.when(self.is_mid)
        def _():
            def body(rows, after):
                lane.acc[s, rows] = lane.acc[s, rows] + f32(lane.fin_a[h, rows])
                lane.acc[s, after(q)] = lane.acc[s, after(q)] + f32(lane.fin_b[h, rows])

            each(q, body)

    def climb(self, unit):
        lane, s, h = unit.lane, unit.s, unit.h
        old = self.before(unit, RING)

        @pl.when(self.is_mid)
        def _():
            unit.up.wait_recv()
            if old is not None:
                old.mid.wait_send()

            def body(rows, after):
                lane.mid[s, rows] = (lane.acc[s, rows] + f32(lane.za[unit.z, rows])).astype(lane.mid.dtype)

            each(unit.half, body)
            unit.mid.start()

    def peak(self, unit):
        lane, s, h = unit.lane, unit.s, unit.h
        old = self.before(unit, RING)

        @pl.when(self.is_mid)
        def _():
            unit.mid.wait_recv()
            if old is not None:
                old.down.wait_send()
                old.fin_mid.wait_send()
                old.own_mid.wait()

            def body(rows, after):
                lane.tot[s, rows] = (f32(lane.mid[s, rows]) + f32(lane.zb[h, rows])).astype(lane.tot.dtype)

            each(unit.half, body)
            unit.down.start()
            unit.fin_mid.start()
            unit.own_mid.start()

    def land(self, unit):
        @pl.when(self.is_end)
        def _():
            unit.down.wait_recv()
            unit.fin_end.start()
            unit.own_end.start()

    def finish(self, unit):
        unit.fin_mid.wait_recv()
        unit.rest.start()
        if unit.u > 0:
            self.units[unit.u - 1].rest.wait()

        @pl.when(self.is_end)
        def _():
            unit.fin_end.wait_send()
            unit.own_end.wait()

    def tick(self, t):
        stages = (self.begin, self.join, self.cross, self.close, self.climb, self.peak, self.land, self.finish)
        for lag, stage in enumerate(stages):
            if 0 <= t - lag <= REDUCE_WIDE:
                stage(self.units[t - lag])

    def shut(self):
        for unit in self.units:
            if unit.small or unit.u + 2 >= REDUCE_WIDE:
                unit.core.wait_send()
            if unit.small or unit.u + RING >= REDUCE_WIDE:
                for move in (unit.one_a, unit.one_b, unit.two_a, unit.two_b):
                    move.wait_send()
                pl.when(self.is_end)(unit.up.wait_send)

                @pl.when(self.is_mid)
                def _(unit=unit):
                    unit.mid.wait_send()
                    unit.down.wait_send()
                    unit.fin_mid.wait_send()
                    unit.own_mid.wait()

        self.units[-1].rest.wait()


def columns_sum(ref, block=64):
    def step(i, carry):
        return carry + jnp.sum(f32(ref[cut(i, block)]), axis=0, keepdims=True)

    return lax.fori_loop(0, ref.shape[0] // block, step, jnp.zeros((1, ref.shape[1]), jnp.float32))


def norm_back_rows(values, grad, gain, base, out, low):
    width = grad.shape[1]

    def step(i, carry):
        rows = cut(i, 32)
        v, d = f32(values[rows]), grad[rows]
        center = v - jnp.mean(v, axis=-1, keepdims=True)
        scale = lax.rsqrt(jnp.mean(center * center, axis=-1, keepdims=True) + EPSILON)
        unit = center * scale
        inner = d * gain[...]
        back = inner - jnp.mean(inner, axis=-1, keepdims=True) - unit * jnp.mean(inner * unit, axis=-1, keepdims=True)
        result = f32(base[rows]) + scale * back
        out[rows] = result
        third = carry[2]
        if low is not None:
            rounded = result.astype(jnp.bfloat16)
            low[rows] = rounded
            third = third + jnp.sum(f32(rounded), axis=0, keepdims=True)
        return (
            carry[0] + jnp.sum(d * unit, axis=0, keepdims=True),
            carry[1] + jnp.sum(d, axis=0, keepdims=True),
            third,
        )

    zero = jnp.zeros((1, width), jnp.float32)
    return lax.fori_loop(0, grad.shape[0] // 32, step, (zero, zero, zero))


BACK_WEIGHTS = [(5, 0), (4, 0), (5, 1), (4, 1), (5, 2), (4, 2), (5, 3), (4, 3)]
BACK_WEIGHTS += [(3, None), (2, 0), (1, None), (0, 0), (0, 1), (0, 2), (2, 1), (2, 2)]

BACK_ROOMS = (
    [("ct", (256, 1024), jnp.bfloat16), ("gk", (1024, 1024), jnp.bfloat16), ("slope", (2, 256, 1024), jnp.float32)]
    + [("dz", (1024, 1024), jnp.bfloat16), ("n3", (256, 1024), jnp.bfloat16), ("h", (256, 1024), jnp.float32)]
    + [("dn", (256, 1024), jnp.float32), ("dh", (256, 1024), jnp.float32), ("out", (256, 1024), jnp.float32)]
    + [("low", (256, 1024), jnp.bfloat16), ("ring", (3, 4, 256, 1024), jnp.bfloat16), ("e2", (256, 1024), jnp.bfloat16)]
    + [("o2", (256, 1024), jnp.bfloat16), ("do2", (256, 1024), jnp.bfloat16), ("q2", (256, 1024), jnp.bfloat16)]
    + [("v2", (1024, 1024), jnp.bfloat16), ("dq2", (256, 1024), jnp.bfloat16), ("dk2", (1024, 1024), jnp.bfloat16)]
    + [("dv2", (1024, 1024), jnp.bfloat16), ("n2", (256, 1024), jnp.bfloat16), ("frames", (1024, 1024), jnp.bfloat16)]
    + [("scores", (1024, 256), jnp.float32), ("gscores", (1024, 256), jnp.float32)]
    + [("probs", (1024, 512), jnp.bfloat16), ("gs", (1024, 512), jnp.bfloat16)]
    + [("lse", (16, 8, 256), jnp.float32), ("table", (4, 32, 256), jnp.bfloat16)]
    + [("rows", (16, 1024), jnp.float32), ("hidden", (8, 1024), jnp.float32)]
    + [("grads", (2, 4, 256, 1024), jnp.bfloat16), ("small", (4, 32, 256), jnp.float32)]
)
BACK_INPUTS = ["tokens", "frames", "cotangent"] + [name for name, _, _ in ACTS]


def backward_kernel(*refs):
    n_in = 7 + len(BACK_INPUTS)
    fulls, small_full = refs[:6], refs[6]
    given = dict(zip(BACK_INPUTS, refs[7:n_in]))
    result, grad_tokens, grad_frames = refs[n_in : n_in + 3]
    outs, small_out = refs[n_in + 3 : n_in + 9], refs[n_in + 9]
    refs = refs[n_in + 10 :]
    room = dict(zip([name for name, _, _ in BACK_ROOMS], refs))
    refs = refs[len(BACK_ROOMS) :]
    lane_count = len(Lane.NAMES)
    wide, thin, refs = refs[:lane_count], refs[lane_count : 2 * lane_count], refs[2 * lane_count :]
    sems, load_sem, ring_sem, store_sem = refs[:4], refs[4], refs[5], refs[6]
    at = Spot()
    reduce = Reduce(at, room["grads"], room["small"], outs, small_out, wide, thin, sems)
    ct, gk, dz, v2, small, rows = room["ct"], room["gk"], room["dz"], room["v2"], room["small"], room["rows"]
    n3, h, dn, dh, out, frames = room["n3"], room["h"], room["dn"], room["dh"], room["out"], room["frames"]

    def quarter(ref, m):
        return ref.at[pl.ds(256 * m, 256)]

    loads = {}

    def plan(name, src, dst):
        loads[name] = pltpu.make_async_copy(src, dst, load_sem.at[len(loads)])

    plan("table", small_full, room["table"])
    plan("ct", given["cotangent"], ct)
    for m in range(4):
        plan(f"g{m}", given["g"].at[m], quarter(gk, m))
        plan(f"slope{m}", given["slope"].at[m], room["slope"].at[m % 2])
    plan("n3", given["n3"], n3)
    plan("h2", given["h2"], h)
    plan("o2", given["o2"], room["o2"])
    plan("q2", given["q2"], room["q2"])
    plan("k2", given["k2"], gk)
    plan("v2", given["v2"], v2)
    plan("lse2", given["lse2"], room["lse"])
    plan("frames", given["frames"], frames)
    plan("n2", given["n2"], room["n2"])
    plan("h1", given["h1"], h)
    q1, k1, v1, o1 = (quarter(gk, m) for m in range(4))
    n1, x, e1 = (quarter(v2, m) for m in range(3))
    do1, dq1, dk1, dv1 = (quarter(dz, m) for m in range(4))
    plan("q1", given["q1"], q1)
    plan("k1", given["k1"], k1)
    plan("v1", given["v1"], v1)
    plan("o1", given["o1"], o1)
    plan("lse1", given["lse1"], room["lse"])
    plan("n1", given["n1"], n1)
    plan("x", given["tokens"], x)
    waited = set()

    def load(*names):
        for name in names:
            loads[name].start()

    def have(*names):
        for name in names:
            if name not in waited:
                waited.add(name)
                loads[name].wait()

    fetched, held = set(), set()

    def fetch(i):
        n, lead = BACK_WEIGHTS[i]
        source = fulls[n]
        if n == 4:
            source = source.at[:, :, pl.ds(1024 * lead, 1024)]
        elif lead is not None:
            source = source.at[lead]
        return pltpu.make_async_copy(source, room["ring"].at[i % 3], ring_sem.at[i])

    def weight(i, ahead=2):
        for k in range(i, min(i + ahead + 1, len(BACK_WEIGHTS))):
            if k not in fetched:
                fetched.add(k)
                fetch(k).start()
        if i not in held:
            held.add(i)
            fetch(i).wait()
        return room["ring"].at[i % 3]

    def note(k, row):
        for g in range(4):
            small[g, k : k + 1, :] = row[:, 256 * g : 256 * g + 256]

    def row(k):
        return rows.at[pl.ds(k, 1)]

    def tall(target, left, w, first):
        def body(g):
            columns = cut(g, 256)
            value = dot_nt(left[...], w[g])
            if not first:
                value = target[:, columns] + value
            target[:, columns] = value.astype(target.dtype)

        loop(4, body)

    def start():
        have("table")
        set_rows(room["table"], rows, room["hidden"])
        small[...] = jnp.zeros_like(small)
        have("ct", "g0", "g1", "g2", "g3")
        note(12, columns_sum(ct))

    def feed(m):
        def run():
            w = weight(2 * m)
            have(f"slope{m}")
            if m == 0:
                have("h2")

            def onward(j):
                columns = cut(j, 256)
                value = dot(quarter(gk, m)[...], w[:, :, columns].reshape(-1, 256))
                if m == 0:
                    value = value + h[:, columns] + rows[12:13, columns]
                else:
                    value = value + out[:, columns]
                out[:, columns] = value

            loop(4, onward)

            def back(g):
                columns = cut(g, 256)
                value = dot_nt(ct[...], w[g]) * room["slope"][m % 2, :, columns]
                dz[256 * m : 256 * m + 256, columns] = value.astype(dz.dtype)

            loop(4, back)
            if m < 2:
                load(f"slope{m + 2}")
            sums = columns_sum(quarter(dz, m))
            for k in range(4):
                small[m, 13 + k : 14 + k, :] = sums[:, 256 * k : 256 * k + 256]
            tall(dn, quarter(dz, m), weight(2 * m + 1), m == 0)

        return run

    def write(ref, target, k):
        copy = pltpu.make_async_copy(ref, target, store_sem.at[k])
        copy.start()
        return copy

    stores = []

    def norm3():
        room["low"][...] = out[...].astype(jnp.bfloat16)
        stores.append(write(room["low"], result, 0))
        gain, shift, column = norm_back_rows(h, dn, row(2), ct, dh, room["e2"])
        note(2, gain)
        note(11, shift)
        note(10, column)
        load("h1")

    def out2():
        load("k2", "lse2")
        tall(room["do2"], room["e2"], weight(8), True)

    def cross(first, count):
        def run():
            have("q2", "k2", "v2", "lse2")
            loop(
                count,
                lambda p: attend_back_pair(
                    p + first, room["q2"], gk, v2, room["do2"], room["lse"], room["scores"], room["gscores"],
                    room["probs"], room["gs"], room["dq2"], room["dk2"], room["dv2"], False,
                ),
            )

        return run

    def norm2():
        load("q1", "k1", "v1", "o1", "n1", "x", "lse1")
        note(8, columns_sum(room["dq2"]))
        note(9, columns_sum(room["dv2"]))
        tall(dn, room["dq2"], weight(9), True)
        have("h1")
        gain, shift, column = norm_back_rows(h, dn, row(1), dh, dh, e1)
        note(1, gain)
        note(7, shift)
        note(6, column)

    def out1():
        tall(do1, e1, weight(10), True)

    def self_back(first, count):
        def run():
            have("q1", "k1", "v1", "lse1")
            part = pl.ds(0, 256)
            loop(
                count,
                lambda p: attend_back_pair(
                    p + first, q1, k1, v1, do1, room["lse"], room["scores"].at[part], room["gscores"].at[part],
                    room["probs"].at[part], room["gs"].at[part], dq1, dk1, dv1, True,
                ),
            )

        return run

    def norm1():
        note(4, columns_sum(dq1))
        note(5, columns_sum(dv1))
        for k, grad in enumerate((dq1, dk1, dv1)):
            tall(dn, grad, weight(11 + k), k == 0)
        have("x")
        gain, shift, _ = norm_back_rows(x, dn, row(0), dh, out, None)
        note(0, gain)
        note(3, shift)
        stores.append(write(out, grad_tokens, 1))

    def frames_back(g):
        def run():
            wk, wv = weight(14, 1), weight(15, 0)
            stage = room["scores"] if g % 2 == 0 else room["gscores"]
            if g >= 2:
                stores[g].wait()

            def body(j):
                lines = cut(j, 256)
                stage[lines] = dot_nt(room["dk2"][lines], wk[g]) + dot_nt(room["dv2"][lines], wv[g])

            loop(4, body)
            stores.append(write(stage, grad_frames.at[:, pl.ds(256 * g, 256)], 2 + g))

        return run

    def outer(u, left, right, tokens=256):
        def body(g):
            columns = cut(g, 256)
            value = dot_tn(left[:, columns], right[...])
            room["grads"][u % 2, g] = value.astype(jnp.bfloat16)

        loop(4, body)

    def grad(u):
        reduce.room(u)
        if u < 4:
            for m in range(4):
                value = dot_tn(gk[256 * m : 256 * m + 256, 256 * u : 256 * u + 256], ct[...])
                room["grads"][u % 2, m] = value.astype(jnp.bfloat16)
        elif u < 8:
            have("n3")
            outer(u, n3, quarter(dz, u - 4))
        elif u == 8:
            have("o2")
            outer(u, room["o2"], room["e2"])
        elif u == 9:
            have("n2")
            outer(u, room["n2"], room["dq2"])
        elif u < 12:
            have("frames")
            outer(u, frames, room["dk2"] if u == 10 else room["dv2"])
        elif u == 12:
            have("o1")
            outer(u, o1, e1)
        elif u < 16:
            have("n1")
            outer(u, n1, (dq1, dk1, dv1)[u - 13])

    steps = [("start", -1, 2, start)]
    steps += [(f"feed{m}", -1, 9, feed(m)) for m in range(4)]
    steps += [("norm3", -1, 3, norm3), ("out2", 3, 2, out2)]
    steps += [(f"cross{k}", 3, 9, cross(2 * k, 2)) for k in range(4)]
    steps += [("norm2", -1, 5, norm2), ("out1", 7, 2, out1)]
    steps += [(f"self{k}", 7, 6, self_back(4 * k, 4)) for k in range(2)]
    steps += [("norm1", -1, 8, norm1)]
    steps += [(f"frames{g}", -1, 4, frames_back(g)) for g in range(4)]
    needs = ["start"] * 4 + [f"feed{m}" for m in range(4)] + ["norm3", "cross3", "cross3", "cross3", "norm2"]
    needs += ["self1"] * 3 + ["norm1"]

    load("table", "ct", "g0", "g1", "g2", "g3", "slope0", "h2", "slope1", "n3", "o2", "q2", "v2", "frames", "n2")
    reduce.open()
    done, now, tick, last = set(), 0.0, 0, -100.0
    left = list(steps)
    while left or tick < reduce.ticks:
        can_tick = tick < reduce.ticks and (tick > REDUCE_WIDE or needs[tick] in done)
        can_step = bool(left) and left[0][1] < tick
        if can_tick and (now - last >= BACK_PERIOD or not can_step):
            now = max(now, last + (BACK_PERIOD if not can_step else 0.0))
            last = now
            if tick < REDUCE_WIDE:
                grad(tick)
                now += 3.0
            reduce.tick(tick)
            now += 2.0
            tick += 1
        else:
            name, _, cost, run = left.pop(0)
            run()
            done.add(name)
            now += cost
    reduce.shut()
    stores[0].wait()
    stores[1].wait()
    stores[4].wait()
    stores[5].wait()


BACK_PERIOD = 7.0


def backward_all(full, tokens, frames, cotangent):
    low, wide = jnp.bfloat16, jnp.float32
    width = 1024
    shapes = [
        jax.ShapeDtypeStruct((256, width), low),
        jax.ShapeDtypeStruct((256, width), wide),
        jax.ShapeDtypeStruct((1024, width), wide),
        jax.ShapeDtypeStruct((3, 256, width), low),
        jax.ShapeDtypeStruct((256, width), low),
        jax.ShapeDtypeStruct((3, 256, width), low),
        jax.ShapeDtypeStruct((256, width), low),
        jax.ShapeDtypeStruct((256, 4 * width), low),
        jax.ShapeDtypeStruct((1024, width), low),
        jax.ShapeDtypeStruct((32, 256), wide),
    ]
    weights = list(full[:7])
    weights[5] = weights[5].reshape(4, 4, 256, width)
    args = (*weights, tokens, frames, cotangent, *full[7:])
    anywhere = pl.BlockSpec(memory_space=pl.ANY)
    return pl.pallas_call(
        backward_kernel,
        name="backward_and_reduce",
        out_shape=shapes,
        in_specs=[anywhere] * len(args),
        out_specs=[anywhere] * len(shapes),
        scratch_shapes=[pltpu.VMEM(shape, dtype) for _, shape, dtype in BACK_ROOMS]
        + lane_shapes(RING, OTHERS, HELD, FINALS, 256, width, low)
        + lane_shapes(1, 1, 1, 1, 32, 256, wide)
        + [
            pltpu.SemaphoreType.DMA((REDUCE_WIDE + 1, 9)),
            pltpu.SemaphoreType.DMA((REDUCE_WIDE + 1, 9)),
            pltpu.SemaphoreType.DMA((REDUCE_WIDE + 1, 2)),
            pltpu.SemaphoreType.REGULAR,
            pltpu.SemaphoreType.DMA((32,)),
            pltpu.SemaphoreType.DMA((len(BACK_WEIGHTS),)),
            pltpu.SemaphoreType.DMA((6,)),
        ],
        compiler_params=pltpu.CompilerParams(
            collective_id=1, has_side_effects=True, vmem_limit_bytes=VMEM_LIMIT
        ),
    )(*args)


def widen_pieces(refs):
    self_qkv, self_out, cross_qkv, cross_out, fc1, fc2 = refs
    pieces = [fc2.at[pl.ds(256 * m, 256)] for m in range(4)]
    pieces += [fc1.at[:, pl.ds(1024 * m, 1024)] for m in range(4)]
    pieces += [cross_out] + [cross_qkv.at[m] for m in range(3)] + [self_out] + [self_qkv.at[m] for m in range(3)]
    return pieces


def widen_kernel(*refs):
    result, grad_tokens, grad_frames, grads, small = *refs[:3], refs[3:9], refs[9]
    outs, gains, biases, hidden = refs[10:19], refs[19], refs[20], refs[21]
    low, high, v_result, v_tokens, v_frames, in_sem, out_sem = refs[22:]
    sources = widen_pieces(grads) + [result, grad_tokens, grad_frames]
    targets = widen_pieces(outs[3:]) + list(outs[:3])
    count = len(sources) - 3
    inside = [low.at[k] for k in range(count)] + [v_result, v_tokens, v_frames]
    ready = [high.at[k] for k in range(count)] + [v_result, v_tokens, v_frames]
    loads = [pltpu.make_async_copy(a, b, in_sem.at[k]) for k, (a, b) in enumerate(zip(sources, inside))]
    stores = [pltpu.make_async_copy(a, b, out_sem.at[k]) for k, (a, b) in enumerate(zip(ready, targets))]
    for load in loads:
        load.start()
    gains[...] = small[0:3]
    biases[...] = small[3:13]
    hidden[...] = small[13:17]
    for k in range(count + 3):
        loads[k].wait()
        if k < count:

            def body(i):
                high[k, cut(i, 64)] = f32(low[k, cut(i, 64)])

            loop(4, body)
        stores[k].start()
    for store in stores:
        store.wait()


def widen_all(done):
    wide = jnp.float32
    anywhere, inside = pl.BlockSpec(memory_space=pl.ANY), pl.BlockSpec(memory_space=pltpu.VMEM)
    shapes = [jax.ShapeDtypeStruct(a.shape, a.dtype if k == 0 else wide) for k, a in enumerate(done[:9])]
    shapes += [jax.ShapeDtypeStruct((rows, 256), wide) for rows in (3, 10, 4)]
    return pl.pallas_call(
        widen_kernel,
        name="widen",
        out_shape=shapes,
        in_specs=[anywhere] * 9 + [inside],
        out_specs=[anywhere] * 9 + [inside] * 3,
        scratch_shapes=[
            pltpu.VMEM((16, 256, 1024), jnp.bfloat16),
            pltpu.VMEM((16, 256, 1024), wide),
            pltpu.VMEM(done[0].shape, done[0].dtype),
            pltpu.VMEM(done[1].shape, wide),
            pltpu.VMEM(done[2].shape, wide),
            pltpu.SemaphoreType.DMA((19,)),
            pltpu.SemaphoreType.DMA((19,)),
        ],
        compiler_params=pltpu.CompilerParams(vmem_limit_bytes=VMEM_LIMIT),
    )(*done)


def shards_here(
    tokens,
    frames,
    cotangent,
    self_qkv,
    self_out,
    cross_qkv,
    cross_out,
    fc1_weight,
    fc2_weight,
    gains,
    biases,
    fc1_bias,
):
    part = gains.shape[1]
    small = jnp.concatenate(
        [gains, biases, fc1_bias.reshape(4, part), jnp.zeros((15, part), jnp.bfloat16)], axis=0
    )
    shards = (self_qkv, self_out, cross_qkv, cross_out, fc1_weight, fc2_weight)
    full = forward_all(shards, small, tokens[0], frames[0])
    done = widen_all(backward_all(full, tokens[0], frames[0], cotangent[0]))
    return (done[0][None], done[1][None], done[2][None], *done[3:11], done[11].reshape(-1))


def solution(mesh):
    in_specs = (
        P(("group", "replica"), None, None),
        P(("group", "replica"), None, None),
        P(("group", "replica"), None, None),
        P(None, "group", None),
        P("group", None),
        P(None, "group", None),
        P("group", None),
        P("group", None),
        P("group", None),
        P(None, "group"),
        P(None, "group"),
        P("group"),
    )
    out_specs = (
        P(("group", "replica"), None, None),
        P(("group", "replica"), None, None),
        P(("group", "replica"), None, None),
        P(None, "group", None),
        P("group", None),
        P(None, "group", None),
        P("group", None),
        P("group", None),
        P("group", None),
        P(None, "group"),
        P(None, "group"),
        P("group"),
    )
    here = mesh.shape["group"] == 4 and mesh.shape["replica"] == 8
    body = shards_here if here else shards_any
    return jax.shard_map(body, mesh=mesh, in_specs=in_specs, out_specs=out_specs, check_vma=False)
```

```python
from functools import partial
import math

import jax
import jax.numpy as jnp
from jax import lax
from jax.experimental import pallas as pl
from jax.experimental.pallas import tpu as pltpu
from jax.sharding import PartitionSpec as P

HEADS = 16
HEAD_DIM = 64
GROUP, REPLICA = "group", "replica"


EPSILON = 1e-05


def layer_norm(values, gain, shift):
    center = values - jnp.mean(values, axis=-1, keepdims=True)
    spread = jnp.mean(center * center, axis=-1, keepdims=True)
    return center * lax.rsqrt(spread + EPSILON) * gain + shift


def norm_back(values, gain, shift, grad):
    result, pullback = jax.vjp(layer_norm, values, gain, shift)
    return pullback(grad)


def dense(left, right):
    return jnp.dot(left, right, preferred_element_type=jnp.float32)


def left_dense(left, right):
    return lax.dot_general(
        left, right, (((0,), (0,)), ((), ())), preferred_element_type=jnp.float32
    )


def right_dense(grad, weight):
    return lax.dot_general(
        grad, weight, (((1,), (1,)), ((), ())), preferred_element_type=jnp.float32
    )


def column_sum(values):
    return jnp.sum(values.astype(jnp.float32), axis=0)


def split_heads(rows, batch):
    return rows.reshape(batch, -1, HEADS, rows.shape[-1] // HEADS)


def scores_of(query_heads, key_heads, masked):
    scores = jnp.einsum(
        "bqhd,bkhd->bhqk", query_heads, key_heads, preferred_element_type=jnp.float32
    )
    if masked:
        shape = (query_heads.shape[1], key_heads.shape[1])
        allowed = lax.broadcasted_iota(jnp.int32, shape, 0) >= lax.broadcasted_iota(
            jnp.int32, shape, 1
        )
        scores = jnp.where(allowed, scores, -jnp.inf)
    return scores


def attend(queries, keys, values, batch, masked):
    query_heads = split_heads(queries, batch)
    key_heads = split_heads(keys, batch)
    value_heads = split_heads(values, batch)
    scores = scores_of(query_heads, key_heads, masked)
    highest = jnp.max(scores, axis=-1, keepdims=True)
    expo = jnp.exp(scores - highest)
    total = jnp.sum(expo, axis=-1, keepdims=True)
    probs = (expo / total).astype(jnp.bfloat16)
    mixed = jnp.einsum("bhqk,bkhd->bqhd", probs, value_heads, preferred_element_type=jnp.float32)
    return (mixed.reshape(queries.shape).astype(jnp.bfloat16), highest + jnp.log(total))


def attend_back(queries, keys, values, grad_mixed, logsum, batch, masked):
    query_heads = split_heads(queries, batch)
    key_heads = split_heads(keys, batch)
    value_heads = split_heads(values, batch)
    grad_heads = split_heads(grad_mixed, batch)
    probs = jnp.exp(scores_of(query_heads, key_heads, masked) - logsum)
    probs_low = probs.astype(jnp.bfloat16)
    grad_probs = jnp.einsum(
        "bqhd,bkhd->bhqk", grad_heads, value_heads, preferred_element_type=jnp.float32
    )
    grad_values = jnp.einsum(
        "bhqk,bqhd->bkhd", probs_low, grad_heads, preferred_element_type=jnp.float32
    )
    center = jnp.sum(probs * grad_probs, axis=-1, keepdims=True)
    grad_scores = (probs * (grad_probs - center)).astype(jnp.bfloat16)
    grad_queries = jnp.einsum(
        "bhqk,bkhd->bqhd", grad_scores, key_heads, preferred_element_type=jnp.float32
    )
    grad_keys = jnp.einsum(
        "bhqk,bqhd->bkhd", grad_scores, query_heads, preferred_element_type=jnp.float32
    )
    return (
        grad_queries.reshape(queries.shape),
        grad_keys.reshape(keys.shape),
        grad_values.reshape(keys.shape),
    )


def forward(tokens, frames, weights):
    self_qkv, self_out, cross_qkv, cross_out, fc1_weight, fc2_weight, gains, biases, fc1_bias = (
        weights
    )
    batch = tokens.shape[0]
    width = tokens.shape[2]
    scale = 1.0 / math.sqrt(HEAD_DIM)
    gain_rows = gains.astype(jnp.float32)
    bias_rows = biases.astype(jnp.float32)
    resid0 = tokens.reshape(-1, width).astype(jnp.float32)
    frame_rows = frames.reshape(-1, width)
    normed1 = layer_norm(resid0, gain_rows[0], bias_rows[0]).astype(jnp.bfloat16)
    query1 = ((dense(normed1, self_qkv[0]) + bias_rows[1]) * scale).astype(jnp.bfloat16)
    key1 = dense(normed1, self_qkv[1]).astype(jnp.bfloat16)
    value1 = (dense(normed1, self_qkv[2]) + bias_rows[2]).astype(jnp.bfloat16)
    mixed1, logsum1 = attend(query1, key1, value1, batch, True)
    resid1 = resid0 + dense(mixed1, self_out) + bias_rows[3]
    normed2 = layer_norm(resid1, gain_rows[1], bias_rows[4]).astype(jnp.bfloat16)
    query2 = ((dense(normed2, cross_qkv[0]) + bias_rows[5]) * scale).astype(jnp.bfloat16)
    key2 = dense(frame_rows, cross_qkv[1]).astype(jnp.bfloat16)
    value2 = (dense(frame_rows, cross_qkv[2]) + bias_rows[6]).astype(jnp.bfloat16)
    mixed2, logsum2 = attend(query2, key2, value2, batch, False)
    resid2 = resid1 + dense(mixed2, cross_out) + bias_rows[7]
    normed3 = layer_norm(resid2, gain_rows[2], bias_rows[8]).astype(jnp.bfloat16)
    hidden_pre = dense(normed3, fc1_weight) + fc1_bias.astype(jnp.float32)
    hidden = jax.nn.gelu(hidden_pre, approximate=False).astype(jnp.bfloat16)
    result = resid2 + dense(hidden, fc2_weight) + bias_rows[9]
    saved = (
        resid0,
        frame_rows,
        normed1,
        query1,
        key1,
        value1,
        mixed1,
        logsum1,
        resid1,
        normed2,
        query2,
        key2,
        value2,
        mixed2,
        logsum2,
        resid2,
        normed3,
        hidden_pre,
        hidden,
    )
    return (result, saved)


def backward(cotangent, weights, saved, settle_mlp, settle_cross, settle_self):
    self_qkv, self_out, cross_qkv, cross_out, fc1_weight, fc2_weight, gains, biases, fc1_bias = (
        weights
    )
    (
        resid0,
        frame_rows,
        normed1,
        query1,
        key1,
        value1,
        mixed1,
        logsum1,
        resid1,
        normed2,
        query2,
        key2,
        value2,
        mixed2,
        logsum2,
        resid2,
        normed3,
        hidden_pre,
        hidden,
    ) = saved
    batch = cotangent.shape[0]
    width = cotangent.shape[2]
    scale = 1.0 / math.sqrt(HEAD_DIM)
    gain_rows = gains.astype(jnp.float32)
    bias_rows = biases.astype(jnp.float32)
    grad_out = cotangent.reshape(-1, width).astype(jnp.float32)
    grad_branch3 = grad_out.astype(jnp.bfloat16)
    fc2_grad = left_dense(hidden, grad_branch3)
    bias9 = column_sum(grad_branch3)
    grad_hidden = right_dense(grad_branch3, fc2_weight)
    unused, gelu_pull = jax.vjp(partial(jax.nn.gelu, approximate=False), hidden_pre)
    grad_pre = gelu_pull(grad_hidden)[0].astype(jnp.bfloat16)
    fc1_grad = left_dense(normed3, grad_pre)
    fc1_bias_grad = column_sum(grad_pre)
    mlp_part = settle_mlp((fc1_grad, fc2_grad, fc1_bias_grad))
    grad_resid2, gain3, shift3 = norm_back(
        resid2, gain_rows[2], bias_rows[8], right_dense(grad_pre, fc1_weight)
    )
    grad_resid2 = grad_out + grad_resid2
    grad_branch2 = grad_resid2.astype(jnp.bfloat16)
    cross_out_grad = left_dense(mixed2, grad_branch2)
    bias7 = column_sum(grad_branch2)
    grad_mixed2 = right_dense(grad_branch2, cross_out).astype(jnp.bfloat16)
    grad_q2, grad_k2, grad_v2 = attend_back(
        query2, key2, value2, grad_mixed2, logsum2, batch, False
    )
    grad_q2 = (grad_q2.astype(jnp.bfloat16).astype(jnp.float32) * scale).astype(jnp.bfloat16)
    grad_k2 = grad_k2.astype(jnp.bfloat16)
    grad_v2 = grad_v2.astype(jnp.bfloat16)
    cross_qkv_grad = [
        left_dense(normed2, grad_q2),
        left_dense(frame_rows, grad_k2),
        left_dense(frame_rows, grad_v2),
    ]
    bias5 = column_sum(grad_q2)
    bias6 = column_sum(grad_v2)
    cross_part = settle_cross((cross_qkv_grad, cross_out_grad))
    grad_frames = right_dense(grad_k2, cross_qkv[1]) + right_dense(grad_v2, cross_qkv[2])
    grad_resid1, gain2, shift2 = norm_back(
        resid1, gain_rows[1], bias_rows[4], right_dense(grad_q2, cross_qkv[0])
    )
    grad_resid1 = grad_resid2 + grad_resid1
    grad_branch1 = grad_resid1.astype(jnp.bfloat16)
    self_out_grad = left_dense(mixed1, grad_branch1)
    bias3 = column_sum(grad_branch1)
    grad_mixed1 = right_dense(grad_branch1, self_out).astype(jnp.bfloat16)
    grad_q1, grad_k1, grad_v1 = attend_back(query1, key1, value1, grad_mixed1, logsum1, batch, True)
    grad_q1 = (grad_q1.astype(jnp.bfloat16).astype(jnp.float32) * scale).astype(jnp.bfloat16)
    grad_k1 = grad_k1.astype(jnp.bfloat16)
    grad_v1 = grad_v1.astype(jnp.bfloat16)
    self_qkv_grad = [
        left_dense(normed1, grad_q1),
        left_dense(normed1, grad_k1),
        left_dense(normed1, grad_v1),
    ]
    bias1 = column_sum(grad_q1)
    bias2 = column_sum(grad_v1)
    grad_normed1 = (
        right_dense(grad_q1, self_qkv[0])
        + right_dense(grad_k1, self_qkv[1])
        + right_dense(grad_v1, self_qkv[2])
    )
    grad_resid0, gain1, shift1 = norm_back(resid0, gain_rows[0], bias_rows[0], grad_normed1)
    grad_tokens = grad_resid1 + grad_resid0
    gains_grad = jnp.stack([gain1, gain2, gain3])
    biases_grad = jnp.stack(
        [shift1, bias1, bias2, bias3, shift2, bias5, bias6, bias7, shift3, bias9]
    )
    self_part = settle_self((self_qkv_grad, self_out_grad, gains_grad, biases_grad))
    return (grad_tokens, grad_frames, mlp_part, cross_part, self_part)


def unchanged(grads):
    return grads


def shards_any(
    tokens,
    frames,
    cotangent,
    self_qkv,
    self_out,
    cross_qkv,
    cross_out,
    fc1_weight,
    fc2_weight,
    gains,
    biases,
    fc1_bias,
):
    weights = (
        lax.all_gather(self_qkv, GROUP, axis=1, tiled=True),
        lax.all_gather(self_out, GROUP, axis=0, tiled=True),
        lax.all_gather(cross_qkv, GROUP, axis=1, tiled=True),
        lax.all_gather(cross_out, GROUP, axis=0, tiled=True),
        lax.all_gather(fc1_weight, GROUP, axis=0, tiled=True),
        lax.all_gather(fc2_weight, GROUP, axis=0, tiled=True),
        lax.all_gather(gains, GROUP, axis=1, tiled=True),
        lax.all_gather(biases, GROUP, axis=1, tiled=True),
        lax.all_gather(fc1_bias, GROUP, axis=0, tiled=True),
    )
    result, saved = forward(tokens, frames, weights)
    grad_tokens, grad_frames, mlp_part, cross_part, self_part = backward(
        cotangent, weights, saved, unchanged, unchanged, unchanged
    )
    shares = (
        lax.psum_scatter(
            jnp.stack(self_part[0]).astype(jnp.bfloat16), GROUP, scatter_dimension=1, tiled=True
        ).astype(jnp.float32),
        lax.psum_scatter(
            self_part[1].astype(jnp.bfloat16), GROUP, scatter_dimension=0, tiled=True
        ).astype(jnp.float32),
        lax.psum_scatter(
            jnp.stack(cross_part[0]).astype(jnp.bfloat16), GROUP, scatter_dimension=1, tiled=True
        ).astype(jnp.float32),
        lax.psum_scatter(
            cross_part[1].astype(jnp.bfloat16), GROUP, scatter_dimension=0, tiled=True
        ).astype(jnp.float32),
        lax.psum_scatter(
            mlp_part[0].astype(jnp.bfloat16), GROUP, scatter_dimension=0, tiled=True
        ).astype(jnp.float32),
        lax.psum_scatter(
            mlp_part[1].astype(jnp.bfloat16), GROUP, scatter_dimension=0, tiled=True
        ).astype(jnp.float32),
        lax.psum_scatter(
            self_part[2].astype(jnp.bfloat16), GROUP, scatter_dimension=1, tiled=True
        ).astype(jnp.float32),
        lax.psum_scatter(
            self_part[3].astype(jnp.bfloat16), GROUP, scatter_dimension=1, tiled=True
        ).astype(jnp.float32),
        lax.psum_scatter(
            mlp_part[2].astype(jnp.bfloat16), GROUP, scatter_dimension=0, tiled=True
        ).astype(jnp.float32),
    )
    summed = (
        lax.psum(shares[0].astype(jnp.bfloat16), REPLICA).astype(jnp.float32),
        lax.psum(shares[1].astype(jnp.bfloat16), REPLICA).astype(jnp.float32),
        lax.psum(shares[2].astype(jnp.bfloat16), REPLICA).astype(jnp.float32),
        lax.psum(shares[3].astype(jnp.bfloat16), REPLICA).astype(jnp.float32),
        lax.psum(shares[4].astype(jnp.bfloat16), REPLICA).astype(jnp.float32),
        lax.psum(shares[5].astype(jnp.bfloat16), REPLICA).astype(jnp.float32),
        lax.psum(shares[6].astype(jnp.bfloat16), REPLICA).astype(jnp.float32),
        lax.psum(shares[7].astype(jnp.bfloat16), REPLICA).astype(jnp.float32),
        lax.psum(shares[8].astype(jnp.bfloat16), REPLICA).astype(jnp.float32),
    )
    (
        self_qkv_grad,
        self_out_grad,
        cross_qkv_grad,
        cross_out_grad,
        fc1_grad,
        fc2_grad,
        gains_grad,
        biases_grad,
        fc1_bias_grad,
    ) = summed
    return (
        result.reshape(tokens.shape).astype(jnp.bfloat16),
        grad_tokens.reshape(tokens.shape),
        grad_frames.reshape(frames.shape),
        self_qkv_grad,
        self_out_grad,
        cross_qkv_grad,
        cross_out_grad,
        fc1_grad,
        fc2_grad,
        gains_grad,
        biases_grad,
        fc1_bias_grad,
    )


MESH = pl.DeviceIdType.MESH
VMEM_LIMIT = 64 * 1024 * 1024 - 128 * 1024


class Spot:
    def __init__(self):
        self.g = lax.axis_index(GROUP)
        self.r = lax.axis_index(REPLICA)
        self.core = lax.rem(self.r, 2)
        self.z = lax.div(self.r, 2)
        self.zb = lax.rem(self.z, 2)
        self.gx = self.g + 1 - 2 * lax.rem(self.g, 2)
        self.gy = lax.rem(self.g + 2, 4)
        self.gd = self.gx + 2 - 4 * lax.div(self.gx, 2)
        self.rc = self.r + 1 - 2 * self.core
        self.rz = self.r + 2 - 4 * self.zb
        self.x_id = (self.gx, self.r)
        self.y_id = (self.gy, self.r)
        self.d_id = (self.gd, self.r)
        self.c_id = (self.g, self.rc)
        self.z_id = (self.g, self.rz)


def meet(*ids):
    barrier = pltpu.get_barrier_semaphore()
    for device in ids:
        pl.semaphore_signal(barrier, inc=1, device_id=device, device_id_type=MESH)
    pl.semaphore_wait(barrier, len(ids))


GATHER_CHUNKS = (
    [(0, m, 0, 256, 0, 1024, m != 0) for m in range(3)]
    + [(1, None, 0, 256, 0, 1024, False)]
    + [(2, m, 0, 256, 0, 1024, m != 0) for m in range(3)]
    + [(3, None, 0, 256, 0, 1024, False)]
    + [(4, None, 0, 256, 1024 * m, 1024, m != 3) for m in range(4)]
    + [(5, None, 256 * m, 256, 0, 1024, m != 3) for m in range(4)]
)
N_GATHER = len(GATHER_CHUNKS)


class Gather:
    def __init__(self, at, shards, small, fulls, small_full, stages, small_stage, sems):
        self.load_sem, self.put_sem, self.send_sem, self.recv_sem, small_send, small_recv, small_local = sems
        self.at, self.shards, self.fulls = at, shards, fulls
        self.loads = [pltpu.make_async_copy(shards[n], stages[n], self.load_sem.at[n]) for n in range(6)]
        self.small_load = pltpu.make_async_copy(small, small_stage, small_local.at[0])
        self.small_put = pltpu.make_async_copy(small_stage, small_full.at[at.g], small_local.at[1])
        self.small_copies = [
            pltpu.make_async_remote_copy(
                small, small_full.at[at.g], small_send.at[n], small_recv.at[n],
                device_id=device, device_id_type=MESH,
            )
            for n, device in enumerate((at.x_id, at.y_id, at.d_id))
        ]
        self.puts = []
        for n in range(6):
            where = (slice(None), at.g) if n in (0, 2) else (at.g,)
            self.puts.append(pltpu.make_async_copy(stages[n], fulls[n].at[where], self.put_sem.at[n]))
        self.plans = [self.plan(i) for i in range(N_GATHER)]
        self.arrived, self.placed = set(), set()

    def full(self, i, g, start, rows):
        n, lead, first, _, column, columns, _ = GATHER_CHUNKS[i]
        where = (g, pl.ds(first + start, rows), pl.ds(column, columns))
        return self.fulls[n].at[where if lead is None else (lead,) + where]

    def shard(self, i, start, rows):
        n, lead, first, _, column, columns, _ = GATHER_CHUNKS[i]
        where = (pl.ds(first + start, rows), pl.ds(column, columns))
        return self.shards[n].at[where if lead is None else (lead,) + where]

    def plan(self, i):
        at = self.at

        def put(k, src, g, start, rows, device):
            return pltpu.make_async_remote_copy(
                src, self.full(i, g, start, rows), self.send_sem.at[i, k], self.recv_sem.at[i, k],
                device_id=device, device_id_type=MESH,
            )

        rows, split = GATHER_CHUNKS[i][3], GATHER_CHUNKS[i][6]
        half = rows // 2
        base = pl.multiple_of(at.core * half, half)
        core_base = base
        if split:
            half = half // 2
            base = pl.multiple_of(base + at.zb * half, half)
        quarter = half // 2
        mine = self.shard(i, base, half)
        moves = [
            put(0, mine, at.g, base, half, at.x_id),
            put(1, mine, at.g, base, half, at.y_id),
            put(2, self.full(i, at.gy, base + quarter, quarter), at.gy, base + quarter, quarter, at.x_id),
            put(3, self.full(i, at.gx, base, quarter), at.gx, base, quarter, at.y_id),
        ]
        for k, g in enumerate((at.gx, at.gy, at.gd)):
            moves.append(put(4 + k, self.full(i, g, core_base, rows // 2), g, core_base, rows // 2, at.c_id))
        if split:
            for k, g in enumerate((at.gx, at.gy, at.gd)):
                moves.append(put(7 + k, self.full(i, g, base, half), g, base, half, at.z_id))
        return moves, split

    def open(self):
        at = self.at
        for load in self.loads:
            load.start()
        self.small_load.start()
        meet(at.x_id, at.y_id, at.d_id, at.c_id, at.z_id)
        self.begin(0)
        for copy in self.small_copies:
            copy.start()
        self.begin(1)
        self.small_load.wait()
        self.small_put.start()
        for n in range(6):
            self.loads[n].wait()
            self.puts[n].start()

    def small_ready(self):
        self.small_put.wait()
        for copy in self.small_copies:
            copy.wait()

    def begin(self, i):
        moves, _ = self.plans[i]
        moves[0].start()
        moves[1].start()

    def second(self, i):
        moves, split = self.plans[i]
        moves[0].wait_recv()
        moves[1].wait_recv()
        moves[2].start()
        moves[3].start()
        for k in (7, 8) if split else (4, 5):
            moves[k].start()

    def third(self, i):
        moves, split = self.plans[i]
        moves[2].wait_recv()
        moves[3].wait_recv()
        moves[9 if split else 6].start()

    def fourth(self, i):
        moves, split = self.plans[i]
        if split:
            for k in (7, 8, 9):
                moves[k].wait_recv()
            for k in (4, 5, 6):
                moves[k].start()

    ticks = N_GATHER + 2

    def tick(self, i):
        if i < N_GATHER:
            self.second(i)
        if i + 2 < N_GATHER:
            self.begin(i + 2)
        if 0 <= i - 1 < N_GATHER:
            self.third(i - 1)
        if 0 <= i - 2 < N_GATHER:
            self.fourth(i - 2)

    def ready(self, i):
        n = GATHER_CHUNKS[i][0]
        if n not in self.placed:
            self.placed.add(n)
            self.puts[n].wait()
        if i not in self.arrived:
            self.arrived.add(i)
            for k in (4, 5, 6):
                self.plans[i][0][k].wait_recv()

    def close(self):
        for i in range(N_GATHER):
            self.ready(i)
            moves, split = self.plans[i]
            for k in range(10 if split else 7):
                moves[k].wait_send()


def f32(value):
    return value.astype(jnp.float32)


def dot(left, right):
    return jnp.dot(left, right, preferred_element_type=jnp.float32)


def dot_tn(left, right):
    return lax.dot_general(left, right, (((0,), (0,)), ((), ())), preferred_element_type=jnp.float32)


def dot_nt(left, right):
    return lax.dot_general(left, right, (((1,), (1,)), ((), ())), preferred_element_type=jnp.float32)


def loop(count, body):
    def step(i, carry):
        body(i)
        return carry

    lax.fori_loop(0, count, step, 0)


def cut(i, size):
    return pl.ds(pl.multiple_of(i * size, size), size)


def norm_rows(src, dst, gain, shift):
    def body(i):
        values = f32(src[cut(i, 32)])
        center = values - jnp.mean(values, axis=-1, keepdims=True)
        spread = jnp.mean(center * center, axis=-1, keepdims=True)
        dst[cut(i, 32)] = (center * lax.rsqrt(spread + EPSILON) * gain[...] + shift[...]).astype(dst.dtype)

    loop(src.shape[0] // 32, body)


def product(left, weight, store, tile=256):
    def body(j):
        columns = cut(j, tile)
        store(columns, dot(left[...], weight[:, :, columns].reshape(-1, tile)))

    loop(weight.shape[-1] // tile, body)


def attend_pair(p, q, k, v, o, lse, scores, probs, causal):
    columns = cut(p, 128)
    keys, count = k.shape[0], q.shape[0]
    qq, kk, vv = q[:, columns], k[:, columns], v[:, columns]
    lane = lax.broadcasted_iota(jnp.int32, qq.shape, 1)
    vt = vv.T
    block = 128
    sides = []
    for a in range(2):
        qa = jnp.where((lane < 64) if a == 0 else (lane >= 64), qq, jnp.zeros_like(qq))
        scores[...] = dot_nt(kk, qa)

        def rows_of(j):
            part = scores[cut(j, block)]
            if causal:
                key = lax.broadcasted_iota(jnp.int32, part.shape, 0) + j * block
                query = lax.broadcasted_iota(jnp.int32, part.shape, 1)
                part = jnp.where(query >= key, part, -jnp.inf)
            return part

        def top(j, carry):
            return jnp.maximum(carry, jnp.max(rows_of(j), axis=0, keepdims=True))

        highest = lax.fori_loop(0, keys // block, top, jnp.full((1, count), -jnp.inf, jnp.float32))

        def expo(j, carry):
            e = jnp.exp(rows_of(j) - highest)
            scores[cut(j, block)] = e
            return carry + jnp.sum(e, axis=0, keepdims=True)

        total = lax.fori_loop(0, keys // block, expo, jnp.zeros((1, count), jnp.float32))
        share = 1.0 / total

        def rounded(j):
            probs[cut(j, block)] = (scores[cut(j, block)] * share).astype(probs.dtype)

        loop(keys // block, rounded)
        lse[2 * p + a] = jnp.broadcast_to(highest + jnp.log(total), (8, count))
        sides.append(dot(vt[64 * a : 64 * a + 64], probs[...]))
    o[:, columns] = jnp.concatenate(sides, axis=0).T.astype(o.dtype)


def attend_back_pair(p, q, k, v, go, lse, scores, gscores, probs, gs, gq, gk, gv, causal):
    columns = cut(p, 128)
    keys, count = k.shape[0], q.shape[0]
    qq, kk, vv, dd = q[:, columns], k[:, columns], v[:, columns], go[:, columns]
    lane = lax.broadcasted_iota(jnp.int32, qq.shape, 1)
    zero = jnp.zeros_like(qq)
    kt = kk.T
    block = 128
    sides, qs, ds = [], [], []
    for a in range(2):
        here = (lane < 64) if a == 0 else (lane >= 64)
        qa, da = jnp.where(here, qq, zero), jnp.where(here, dd, zero)
        qs.append(qa)
        ds.append(da)
        scores[...] = dot_nt(kk, qa)
        gscores[...] = dot_nt(vv, da)
        line = lse[2 * p + a][0:1]
        across = slice(a * count, (a + 1) * count)

        def first(j, carry):
            part = scores[cut(j, block)]
            if causal:
                key = lax.broadcasted_iota(jnp.int32, part.shape, 0) + j * block
                query = lax.broadcasted_iota(jnp.int32, part.shape, 1)
                part = jnp.where(query >= key, part, -jnp.inf)
            e = jnp.exp(part - line)
            scores[cut(j, block)] = e
            probs[cut(j, block), across] = e.astype(probs.dtype)
            return carry + jnp.sum(e * gscores[cut(j, block)], axis=0, keepdims=True)

        center = lax.fori_loop(0, keys // block, first, jnp.zeros((1, count), jnp.float32))

        def second(j):
            rows = cut(j, block)
            gs[rows, across] = (scores[rows] * (gscores[rows] - center)).astype(gs.dtype)

        loop(keys // block, second)
        sides.append(dot(kt[64 * a : 64 * a + 64], gs[:, across]))
    gv[:, columns] = dot(probs[...], jnp.concatenate(ds, axis=0)).astype(gv.dtype)
    gk[:, columns] = dot(gs[...], jnp.concatenate(qs, axis=0)).astype(gk.dtype)
    side = jnp.concatenate(sides, axis=0).T.astype(jnp.bfloat16)
    gq[:, columns] = (f32(side) * SCALE).astype(gq.dtype)

def woven(ticks, period, first, steps):
    order, now, tick = [], 0.0, 0
    left = list(range(len(steps)))
    while left or tick < ticks:
        due = first + tick * period
        if left and steps[left[0]][0] < tick and (now < due or tick >= ticks):
            now += steps[left[0]][1]
            order.append(("step", left.pop(0)))
        else:
            now = max(now, due)
            order.append(("tick", tick))
            tick += 1
    return order


ACTS = (
    [("n1", (256, 1024), jnp.bfloat16), ("q1", (256, 1024), jnp.bfloat16), ("k1", (256, 1024), jnp.bfloat16)]
    + [("v1", (256, 1024), jnp.bfloat16), ("o1", (256, 1024), jnp.bfloat16), ("lse1", (16, 8, 256), jnp.float32)]
    + [("h1", (256, 1024), jnp.float32), ("n2", (256, 1024), jnp.bfloat16), ("q2", (256, 1024), jnp.bfloat16)]
    + [("k2", (1024, 1024), jnp.bfloat16), ("v2", (1024, 1024), jnp.bfloat16), ("o2", (256, 1024), jnp.bfloat16)]
    + [("lse2", (16, 8, 256), jnp.float32), ("h2", (256, 1024), jnp.float32), ("n3", (256, 1024), jnp.bfloat16)]
    + [("slope", (4, 256, 1024), jnp.float32), ("g", (4, 256, 1024), jnp.bfloat16)]
)
N_ACTS = len(ACTS)
SCALE = 0.125


def set_rows(small_full, rows, hidden):
    for g in range(4):
        for k in range(13):
            rows[k : k + 1, 256 * g : 256 * g + 256] = f32(small_full[g, k : k + 1])
        for k in range(4):
            hidden[g : g + 1, 256 * k : 256 * k + 256] = f32(small_full[g, 13 + k : 14 + k])


def forward_kernel(*refs):
    shards, small, tokens, frames = refs[:6], refs[6], refs[7], refs[8]
    fulls, small_full = refs[9:15], refs[15]
    saved = refs[16 : 16 + N_ACTS]
    refs = refs[16 + N_ACTS :]
    acts = dict(zip([name for name, _, _ in ACTS], refs[:N_ACTS]))
    refs = refs[N_ACTS:]
    stages, small_stage, sems = refs[:6], refs[6], refs[7:14]
    x, kept, table, rows, hidden, ring, scores1, probs1, scores2, probs2, in_sem, ring_sem, save_sem = refs[14:]
    at = Spot()
    gather = Gather(at, shards, small, fulls, small_full, stages, small_stage, sems)

    x_load = pltpu.make_async_copy(tokens, x, in_sem.at[0])
    frames_load = pltpu.make_async_copy(frames, kept, in_sem.at[1])
    table_load = pltpu.make_async_copy(small_full, table, in_sem.at[2])
    x_load.start()
    frames_load.start()
    gather.open()
    saves = []

    def save(*names):
        for name in names:
            k = [n for n, _, _ in ACTS].index(name)
            copy = pltpu.make_async_copy(acts[name], saved[k], save_sem.at[k])
            copy.start()
            saves.append(copy)

    def fetch(i):
        n, lead, _, _, column, columns, _ = GATHER_CHUNKS[i]
        source = fulls[n] if lead is None else fulls[n].at[lead]
        if n == 4:
            source = source.at[:, :, pl.ds(column, columns)]
        return pltpu.make_async_copy(source, ring.at[i % 3], ring_sem.at[i])

    fetched = set()
    done_ticks = [0]

    def weight(i):
        for k in (i, i + 1):
            if k not in fetched and k < 12 and (k == i or k + 2 < done_ticks[0]):
                fetched.add(k)
                gather.ready(k)
                fetch(k).start()
        fetch(i).wait()
        return ring.at[i % 3]

    def row(k):
        return rows.at[k : k + 1]

    def start():
        gather.small_ready()
        table_load.start()
        x_load.wait()
        table_load.wait()
        set_rows(table, rows, hidden)
        norm_rows(x, acts["n1"], row(0), row(3))
        save("n1")

    def project(name, i, source, bias, scale):
        def run():
            w, target = weight(i), acts[name]

            def store(columns, value):
                if bias is not None:
                    value = value + rows[bias : bias + 1, columns]
                if scale:
                    value = value * SCALE
                target[:, columns] = value.astype(target.dtype)

            product(acts[source], w, store)
            save(name)

        return run

    def project_frames(name, i, bias):
        def run():
            if i == 5:
                frames_load.wait()
            w, target = weight(i), acts[name]

            def body(j):
                columns = cut(j, 256)
                value = dot(kept[...], w[:, :, columns].reshape(-1, 256))
                if bias is not None:
                    value = value + rows[bias : bias + 1, columns]
                target[:, columns] = value.astype(target.dtype)

            loop(4, body)
            save(name)

        return run

    def attend(first, count, q, k, v, o, lse, scores, probs, causal, last):
        def run():
            loop(
                count,
                lambda p: attend_pair(
                    p + first, acts[q], acts[k], acts[v], acts[o], acts[lse], scores, probs, causal
                ),
            )
            if last:
                save(o, lse)

        return run

    def join(i, source, base, bias, target, gain, shift, normed):
        def run():
            w, out = weight(i), acts[target]

            def store(columns, value):
                out[:, columns] = f32(base[:, columns]) + value + rows[bias : bias + 1, columns]

            product(acts[source], w, store)
            norm_rows(out, acts[normed], row(gain), row(shift))
            save(target, normed)

        return run

    def expand(m):
        def run():
            w = weight(8 + m)
            slope, g = acts["slope"], acts["g"]

            def store(columns, value):
                z = value + hidden[m : m + 1, columns]
                below = 0.5 + 0.5 * lax.erf(z * math.sqrt(0.5))
                slope[m, :, columns] = below + z * (jnp.exp(-0.5 * z * z) * (1.0 / math.sqrt(2.0 * math.pi)))
                g[m, :, columns] = (z * below).astype(g.dtype)

            product(acts["n3"], w, store)
            if m == 3:
                save("slope", "g")

        return run

    steps = [(0, 3, start)]
    steps += [(2, 3, project("q1", 0, "n1", 3 + 1, True)), (3, 3, project("k1", 1, "n1", None, False))]
    steps += [(4, 3, project("v1", 2, "n1", 3 + 2, False))]
    for part in range(2):
        steps.append((4, 6, attend(4 * part, 4, "q1", "k1", "v1", "o1", "lse1", scores1, probs1, True, part == 1)))
    steps.append((5, 5, join(3, "o1", x, 3 + 3, "h1", 1, 3 + 4, "n2")))
    steps += [(6, 3, project("q2", 4, "n2", 3 + 5, True)), (7, 6, project_frames("k2", 5, None))]
    steps += [(8, 6, project_frames("v2", 6, 3 + 6))]
    for part in range(4):
        steps.append((8, 5, attend(2 * part, 2, "q2", "k2", "v2", "o2", "lse2", scores2, probs2, False, part == 3)))
    steps.append((9, 5, join(7, "o2", acts["h1"], 3 + 7, "h2", 2, 3 + 8, "n3")))
    for m in range(4):
        steps.append((10 + m, 6, expand(m)))
    for kind, i in woven(gather.ticks, 5.5, 4.0, steps):
        if kind == "tick":
            gather.tick(i)
            done_ticks[0] = i + 1
        else:
            steps[i][2]()
    gather.close()
    for copy in saves:
        copy.wait()


def forward_all(shards, small, tokens, frames):
    shapes = []
    for array in shards:
        lead, tail = array.shape[:-2], array.shape[-2:]
        shapes.append(jax.ShapeDtypeStruct(lead + (4,) + tail, array.dtype))
    shapes.append(jax.ShapeDtypeStruct((4,) + small.shape, small.dtype))
    shapes += [jax.ShapeDtypeStruct(shape, dtype) for _, shape, dtype in ACTS]
    anywhere = pl.BlockSpec(memory_space=pl.ANY)
    low = jnp.bfloat16
    return pl.pallas_call(
        forward_kernel,
        name="gather_and_forward",
        out_shape=shapes,
        in_specs=[anywhere] * 9,
        out_specs=[anywhere] * len(shapes),
        scratch_shapes=[pltpu.VMEM(shape, dtype) for _, shape, dtype in ACTS]
        + [pltpu.VMEM(array.shape, array.dtype) for array in shards]
        + [
            pltpu.VMEM(small.shape, small.dtype),
            pltpu.SemaphoreType.DMA((6,)),
            pltpu.SemaphoreType.DMA((6,)),
            pltpu.SemaphoreType.DMA((N_GATHER, 10)),
            pltpu.SemaphoreType.DMA((N_GATHER, 10)),
            pltpu.SemaphoreType.DMA((3,)),
            pltpu.SemaphoreType.DMA((3,)),
            pltpu.SemaphoreType.DMA((2,)),
            pltpu.VMEM(tokens.shape, low),
            pltpu.VMEM(frames.shape, low),
            pltpu.VMEM((4,) + small.shape, low),
            pltpu.VMEM((16, 1024), jnp.float32),
            pltpu.VMEM((8, 1024), jnp.float32),
            pltpu.VMEM((3, 4, 256, 1024), low),
            pltpu.VMEM((256, 256), jnp.float32),
            pltpu.VMEM((256, 256), low),
            pltpu.VMEM((1024, 256), jnp.float32),
            pltpu.VMEM((1024, 256), low),
            pltpu.SemaphoreType.DMA((3,)),
            pltpu.SemaphoreType.DMA((12,)),
            pltpu.SemaphoreType.DMA((N_ACTS,)),
        ],
        compiler_params=pltpu.CompilerParams(
            collective_id=0, has_side_effects=True, vmem_limit_bytes=VMEM_LIMIT
        ),
    )(*shards, small, tokens, frames)


REDUCE_WIDE = 16
RING, OTHERS, HELD, FINALS = 3, 4, 4, 8


def each(rows, body):
    block = min(rows, 16)
    loop(rows // block, lambda i: body(cut(i, block), lambda k: pl.ds(pl.multiple_of(k + i * block, block), block)))


def toggled(bit, flip):
    return bit + flip - 2 * bit * flip


class Lane:
    NAMES = ["other", "one_a", "one_b", "in_a", "in_b", "two_a", "two_b", "fin_a"]
    NAMES += ["fin_b", "acc", "up", "mid", "za", "zb", "tot", "fin"]

    def __init__(self, refs):
        for name, ref in zip(self.NAMES, refs):
            setattr(self, name, ref)


def lane_shapes(ring, others, held, finals, rows, columns, dtype):
    half, quarter = rows // 2, rows // 4
    return [
        pltpu.VMEM((others, 4, half, columns), dtype),
        pltpu.VMEM((ring, 4, quarter, columns), dtype),
        pltpu.VMEM((ring, 4, quarter, columns), dtype),
        pltpu.VMEM((held, 2, quarter, columns), dtype),
        pltpu.VMEM((held, 2, quarter, columns), dtype),
        pltpu.VMEM((ring, quarter, columns), dtype),
        pltpu.VMEM((ring, quarter, columns), dtype),
        pltpu.VMEM((held, quarter, columns), dtype),
        pltpu.VMEM((held, quarter, columns), dtype),
        pltpu.VMEM((ring, half, columns), jnp.float32),
        pltpu.VMEM((ring, half, columns), dtype),
        pltpu.VMEM((ring, half, columns), dtype),
        pltpu.VMEM((held + 1, half, columns), dtype),
        pltpu.VMEM((held, half, columns), dtype),
        pltpu.VMEM((ring, half, columns), dtype),
        pltpu.VMEM((finals, half, columns), dtype),
    ]


class Unit:
    def __init__(self, reduce, u):
        at = reduce.at
        self.u, self.small = u, u == REDUCE_WIDE
        if self.small:
            self.lane, self.source, rows = reduce.thin, reduce.small, 32
            self.s, self.o, self.h, self.f, self.z = 0, 0, 0, 0, 0
        else:
            self.lane, self.source, rows = reduce.wide, reduce.grads.at[u % 2], 256
            self.s, self.o, self.h, self.f = u % RING, u % OTHERS, u % HELD, u % FINALS
            self.z = u % (HELD + 1)
        half = rows // 2
        lane, s, h, f, z = self.lane, self.s, self.h, self.f, self.z
        self.half, self.quarter = half, rows // 4
        self.mine = pl.multiple_of(at.core * half, half)
        self.theirs = pl.multiple_of((1 - at.core) * half, half)

        def move(k, src, dst, device):
            return pltpu.make_async_remote_copy(
                src, dst, reduce.send_sem.at[u, k], reduce.recv_sem.at[u, k],
                device_id=device, device_id_type=MESH,
            )

        self.core = move(0, self.source.at[:, pl.ds(self.theirs, half), :], lane.other.at[self.o], at.c_id)
        self.one_a = move(1, lane.one_a.at[s, pl.ds(2, 2)], lane.in_a.at[h], at.x_id)
        self.one_b = move(2, lane.one_b.at[s, pl.ds(2, 2)], lane.in_b.at[h], at.y_id)
        self.two_a = move(3, lane.two_a.at[s], lane.fin_a.at[h], at.y_id)
        self.two_b = move(4, lane.two_b.at[s], lane.fin_b.at[h], at.x_id)
        self.up = move(5, lane.up.at[s], lane.za.at[z], at.z_id)
        self.mid = move(6, lane.mid.at[s], lane.zb.at[h], reduce.m_id)
        self.down = move(7, lane.tot.at[s], lane.za.at[z], at.z_id)
        self.fin_mid = move(8, lane.tot.at[s], lane.fin.at[f], at.c_id)
        self.fin_end = move(8, lane.za.at[z], lane.fin.at[f], at.c_id)
        target = reduce.target(u)

        def store(k, src, start):
            return pltpu.make_async_copy(src, target(start, half), reduce.out_sem.at[u, k])

        self.own_mid = store(0, lane.tot.at[s], self.mine)
        self.own_end = store(0, lane.za.at[z], self.mine)
        self.rest = store(1, lane.fin.at[f], self.theirs)


class Reduce:
    lag = 7
    ticks = REDUCE_WIDE + 1 + lag

    def __init__(self, at, grads, small, outs, small_out, wide, thin, sems):
        self.at, self.grads, self.small, self.outs, self.small_out = at, grads, small, outs, small_out
        self.wide, self.thin = Lane(wide), Lane(thin)
        self.send_sem, self.recv_sem, self.out_sem, self.credit = sems
        self.bx, self.by = lax.rem(at.g, 2), lax.div(at.g, 2)
        self.middle = lax.div(at.z * (3 - at.z), 2)
        self.is_end, self.is_mid = self.middle == 0, self.middle == 1
        self.m_id = (at.g, at.r + self.middle * (6 - 4 * at.z) + (1 - self.middle) * (2 - 4 * at.zb))
        self.units = [Unit(self, u) for u in range(REDUCE_WIDE + 1)]

    def target(self, u):
        outs = self.outs
        if u == REDUCE_WIDE:
            return lambda start, rows: self.small_out.at[pl.ds(start, rows)]
        if u < 4:
            return lambda start, rows: outs[5].at[pl.ds(256 * u + start, rows)]
        if u < 8:
            return lambda start, rows: outs[4].at[pl.ds(start, rows), pl.ds(1024 * (u - 4), 1024)]
        k, lead = {8: (3, None), 9: (2, 0), 10: (2, 1), 11: (2, 2), 12: (1, None), 13: (0, 0), 14: (0, 1), 15: (0, 2)}[u]
        return lambda start, rows: outs[k].at[(pl.ds(start, rows),) if lead is None else (lead, pl.ds(start, rows))]

    def open(self):
        at = self.at
        barrier = pltpu.get_barrier_semaphore()
        for device in (at.x_id, at.y_id, at.c_id, at.z_id):
            pl.semaphore_signal(barrier, inc=1, device_id=device, device_id_type=MESH)

        @pl.when(self.is_mid)
        def _():
            pl.semaphore_signal(barrier, inc=1, device_id=self.m_id, device_id_type=MESH)

        pl.semaphore_wait(barrier, 4 + self.middle)

    def before(self, unit, depth):
        return self.units[unit.u - depth] if unit.u >= depth and not unit.small else None

    def room(self, u):
        old = self.before(self.units[u], 2)
        if old is not None:
            old.core.wait_send()

    def begin(self, unit):
        if not unit.small and unit.u >= OTHERS:
            pl.semaphore_wait(self.credit, 1)
        unit.core.start()

    def join(self, unit):
        lane, q, s, o = unit.lane, unit.quarter, unit.s, unit.o
        unit.core.wait_recv()
        old = self.before(unit, RING)
        if old is not None:
            old.one_a.wait_send()
            old.one_b.wait_send()
        dtype = lane.one_a.dtype
        bx, by, source, mine = self.bx, self.by, unit.source, unit.mine

        def body(j):
            first, second = lax.rem(j, 2), lax.div(j, 2)
            ga = toggled(bx, second) + 2 * toggled(by, first)
            gb = toggled(bx, first) + 2 * toggled(by, second)
            rows_a, rows_b = pl.ds(mine, q), pl.ds(pl.multiple_of(mine + q, q), q)
            lane.one_a[s, j] = (f32(source[ga, rows_a]) + f32(lane.other[o, ga, 0:q])).astype(dtype)
            lane.one_b[s, j] = (f32(source[gb, rows_b]) + f32(lane.other[o, gb, q : 2 * q])).astype(dtype)

        loop(4, body)
        if not unit.small and unit.u + OTHERS < REDUCE_WIDE:
            pl.semaphore_signal(self.credit, inc=1, device_id=self.at.c_id, device_id_type=MESH)
        unit.one_a.start()
        unit.one_b.start()

    def cross(self, unit):
        lane, q, s, h = unit.lane, unit.quarter, unit.s, unit.h
        unit.one_a.wait_recv()
        unit.one_b.wait_recv()
        old = self.before(unit, RING)
        if old is not None:
            old.two_a.wait_send()
            old.two_b.wait_send()
        dtype = lane.one_a.dtype

        def body(rows, after):
            lane.two_a[s, rows] = (f32(lane.one_a[s, 1, rows]) + f32(lane.in_a[h, 1, rows])).astype(dtype)
            lane.two_b[s, rows] = (f32(lane.one_b[s, 1, rows]) + f32(lane.in_b[h, 1, rows])).astype(dtype)
            lane.acc[s, rows] = f32(lane.one_a[s, 0, rows]) + f32(lane.in_a[h, 0, rows])
            lane.acc[s, after(q)] = f32(lane.one_b[s, 0, rows]) + f32(lane.in_b[h, 0, rows])

        each(q, body)
        unit.two_a.start()
        unit.two_b.start()

    def close(self, unit):
        lane, q, s, h = unit.lane, unit.quarter, unit.s, unit.h
        unit.two_a.wait_recv()
        unit.two_b.wait_recv()
        old = self.before(unit, RING)
        dtype = lane.one_a.dtype

        @pl.when(self.is_end)
        def _():
            if old is not None:
                old.up.wait_send()

            def body(rows, after):
                lane.up[s, rows] = (lane.acc[s, rows] + f32(lane.fin_a[h, rows])).astype(dtype)
                lane.up[s, after(q)] = (lane.acc[s, after(q)] + f32(lane.fin_b[h, rows])).astype(dtype)

            each(q, body)
            unit.up.start()

        @pl.when(self.is_mid)
        def _():
            def body(rows, after):
                lane.acc[s, rows] = lane.acc[s, rows] + f32(lane.fin_a[h, rows])
                lane.acc[s, after(q)] = lane.acc[s, after(q)] + f32(lane.fin_b[h, rows])

            each(q, body)

    def climb(self, unit):
        lane, s, h = unit.lane, unit.s, unit.h
        old = self.before(unit, RING)

        @pl.when(self.is_mid)
        def _():
            unit.up.wait_recv()
            if old is not None:
                old.mid.wait_send()

            def body(rows, after):
                lane.mid[s, rows] = (lane.acc[s, rows] + f32(lane.za[unit.z, rows])).astype(lane.mid.dtype)

            each(unit.half, body)
            unit.mid.start()

    def peak(self, unit):
        lane, s, h = unit.lane, unit.s, unit.h
        old = self.before(unit, RING)

        @pl.when(self.is_mid)
        def _():
            unit.mid.wait_recv()
            if old is not None:
                old.down.wait_send()
                old.fin_mid.wait_send()
                old.own_mid.wait()

            def body(rows, after):
                lane.tot[s, rows] = (f32(lane.mid[s, rows]) + f32(lane.zb[h, rows])).astype(lane.tot.dtype)

            each(unit.half, body)
            unit.down.start()
            unit.fin_mid.start()
            unit.own_mid.start()

    def land(self, unit):
        @pl.when(self.is_end)
        def _():
            unit.down.wait_recv()
            unit.fin_end.start()
            unit.own_end.start()

    def finish(self, unit):
        unit.fin_mid.wait_recv()
        unit.rest.start()
        if unit.u > 0:
            self.units[unit.u - 1].rest.wait()

        @pl.when(self.is_end)
        def _():
            unit.fin_end.wait_send()
            unit.own_end.wait()

    def tick(self, t):
        stages = (self.begin, self.join, self.cross, self.close, self.climb, self.peak, self.land, self.finish)
        for lag, stage in enumerate(stages):
            if 0 <= t - lag <= REDUCE_WIDE:
                stage(self.units[t - lag])

    def shut(self):
        for unit in self.units:
            if unit.small or unit.u + 2 >= REDUCE_WIDE:
                unit.core.wait_send()
            if unit.small or unit.u + RING >= REDUCE_WIDE:
                for move in (unit.one_a, unit.one_b, unit.two_a, unit.two_b):
                    move.wait_send()
                pl.when(self.is_end)(unit.up.wait_send)

                @pl.when(self.is_mid)
                def _(unit=unit):
                    unit.mid.wait_send()
                    unit.down.wait_send()
                    unit.fin_mid.wait_send()
                    unit.own_mid.wait()

        self.units[-1].rest.wait()


def columns_sum(ref, block=64):
    def step(i, carry):
        return carry + jnp.sum(f32(ref[cut(i, block)]), axis=0, keepdims=True)

    return lax.fori_loop(0, ref.shape[0] // block, step, jnp.zeros((1, ref.shape[1]), jnp.float32))


def norm_back_rows(values, grad, gain, base, out, low):
    width = grad.shape[1]

    def step(i, carry):
        rows = cut(i, 32)
        v, d = f32(values[rows]), grad[rows]
        center = v - jnp.mean(v, axis=-1, keepdims=True)
        scale = lax.rsqrt(jnp.mean(center * center, axis=-1, keepdims=True) + EPSILON)
        unit = center * scale
        inner = d * gain[...]
        back = inner - jnp.mean(inner, axis=-1, keepdims=True) - unit * jnp.mean(inner * unit, axis=-1, keepdims=True)
        result = f32(base[rows]) + scale * back
        out[rows] = result
        third = carry[2]
        if low is not None:
            rounded = result.astype(jnp.bfloat16)
            low[rows] = rounded
            third = third + jnp.sum(f32(rounded), axis=0, keepdims=True)
        return (
            carry[0] + jnp.sum(d * unit, axis=0, keepdims=True),
            carry[1] + jnp.sum(d, axis=0, keepdims=True),
            third,
        )

    zero = jnp.zeros((1, width), jnp.float32)
    return lax.fori_loop(0, grad.shape[0] // 32, step, (zero, zero, zero))


BACK_WEIGHTS = [(5, 0), (4, 0), (5, 1), (4, 1), (5, 2), (4, 2), (5, 3), (4, 3)]
BACK_WEIGHTS += [(3, None), (2, 0), (1, None), (0, 0), (0, 1), (0, 2), (2, 1), (2, 2)]

BACK_ROOMS = (
    [("ct", (256, 1024), jnp.bfloat16), ("gk", (1024, 1024), jnp.bfloat16), ("slope", (2, 256, 1024), jnp.float32)]
    + [("dz", (1024, 1024), jnp.bfloat16), ("n3", (256, 1024), jnp.bfloat16), ("h", (256, 1024), jnp.float32)]
    + [("dn", (256, 1024), jnp.float32), ("dh", (256, 1024), jnp.float32), ("out", (256, 1024), jnp.float32)]
    + [("low", (256, 1024), jnp.bfloat16), ("ring", (3, 4, 256, 1024), jnp.bfloat16), ("e2", (256, 1024), jnp.bfloat16)]
    + [("o2", (256, 1024), jnp.bfloat16), ("do2", (256, 1024), jnp.bfloat16), ("q2", (256, 1024), jnp.bfloat16)]
    + [("v2", (1024, 1024), jnp.bfloat16), ("dq2", (256, 1024), jnp.bfloat16), ("dk2", (1024, 1024), jnp.bfloat16)]
    + [("dv2", (1024, 1024), jnp.bfloat16), ("n2", (256, 1024), jnp.bfloat16), ("frames", (1024, 1024), jnp.bfloat16)]
    + [("scores", (1024, 256), jnp.float32), ("gscores", (1024, 256), jnp.float32)]
    + [("probs", (1024, 512), jnp.bfloat16), ("gs", (1024, 512), jnp.bfloat16)]
    + [("lse", (16, 8, 256), jnp.float32), ("table", (4, 32, 256), jnp.bfloat16)]
    + [("rows", (16, 1024), jnp.float32), ("hidden", (8, 1024), jnp.float32)]
    + [("grads", (2, 4, 256, 1024), jnp.bfloat16), ("small", (4, 32, 256), jnp.float32)]
)
BACK_INPUTS = ["tokens", "frames", "cotangent"] + [name for name, _, _ in ACTS]


class Rooms:
    def __init__(self, names, refs):
        for name, ref in zip(names, refs):
            setattr(self, name, ref)


def backward_kernel(*refs):
    n_in = 7 + len(BACK_INPUTS)
    fulls, small_full = refs[:6], refs[6]
    given = dict(zip(BACK_INPUTS, refs[7:n_in]))
    result, grad_tokens, grad_frames = refs[n_in : n_in + 3]
    outs, small_out = refs[n_in + 3 : n_in + 9], refs[n_in + 9]
    refs = refs[n_in + 10 :]
    room = Rooms([name for name, _, _ in BACK_ROOMS], refs)
    refs = refs[len(BACK_ROOMS) :]
    lane_count = len(Lane.NAMES)
    wide, thin, refs = refs[:lane_count], refs[lane_count : 2 * lane_count], refs[2 * lane_count :]
    sems, load_sem, ring_sem, store_sem = refs[:4], refs[4], refs[5], refs[6]
    at = Spot()
    reduce = Reduce(at, room.grads, room.small, outs, small_out, wide, thin, sems)
    ct, gk, dz, v2, small, rows = room.ct, room.gk, room.dz, room.v2, room.small, room.rows
    n3, h, dn, dh, out, frames = room.n3, room.h, room.dn, room.dh, room.out, room.frames

    def quarter(ref, m):
        return ref.at[pl.ds(256 * m, 256)]

    loads = {}

    def plan(name, src, dst):
        loads[name] = pltpu.make_async_copy(src, dst, load_sem.at[len(loads)])

    plan("table", small_full, room.table)
    plan("ct", given["cotangent"], ct)
    for m in range(4):
        plan(f"g{m}", given["g"].at[m], quarter(gk, m))
        plan(f"slope{m}", given["slope"].at[m], room.slope.at[m % 2])
    plan("n3", given["n3"], n3)
    plan("h2", given["h2"], h)
    plan("o2", given["o2"], room.o2)
    plan("q2", given["q2"], room.q2)
    plan("k2", given["k2"], gk)
    plan("v2", given["v2"], v2)
    plan("lse2", given["lse2"], room.lse)
    plan("frames", given["frames"], frames)
    plan("n2", given["n2"], room.n2)
    plan("h1", given["h1"], h)
    q1, k1, v1, o1 = (quarter(gk, m) for m in range(4))
    n1, x, e1 = (quarter(v2, m) for m in range(3))
    do1, dq1, dk1, dv1 = (quarter(dz, m) for m in range(4))
    plan("q1", given["q1"], q1)
    plan("k1", given["k1"], k1)
    plan("v1", given["v1"], v1)
    plan("o1", given["o1"], o1)
    plan("lse1", given["lse1"], room.lse)
    plan("n1", given["n1"], n1)
    plan("x", given["tokens"], x)
    waited = set()

    def load(*names):
        for name in names:
            loads[name].start()

    def have(*names):
        for name in names:
            if name not in waited:
                waited.add(name)
                loads[name].wait()

    fetched, held = set(), set()

    def fetch(i):
        n, lead = BACK_WEIGHTS[i]
        source = fulls[n]
        if n == 4:
            source = source.at[:, :, pl.ds(1024 * lead, 1024)]
        elif lead is not None:
            source = source.at[lead]
        return pltpu.make_async_copy(source, room.ring.at[i % 3], ring_sem.at[i])

    def weight(i, ahead=2):
        for k in range(i, min(i + ahead + 1, len(BACK_WEIGHTS))):
            if k not in fetched:
                fetched.add(k)
                fetch(k).start()
        if i not in held:
            held.add(i)
            fetch(i).wait()
        return room.ring.at[i % 3]

    def note(k, row):
        for g in range(4):
            small[g, k : k + 1, :] = row[:, 256 * g : 256 * g + 256]

    def row(k):
        return rows.at[pl.ds(k, 1)]

    def tall(target, left, w, first):
        def body(g):
            columns = cut(g, 256)
            value = dot_nt(left[...], w[g])
            if not first:
                value = target[:, columns] + value
            target[:, columns] = value.astype(target.dtype)

        loop(4, body)

    def start():
        have("table")
        set_rows(room.table, rows, room.hidden)
        small[...] = jnp.zeros_like(small)
        have("ct", "g0", "g1", "g2", "g3")
        note(12, columns_sum(ct))

    def feed(m):
        def run():
            w = weight(2 * m)
            have(f"slope{m}")
            if m == 0:
                have("h2")

            def onward(j):
                columns = cut(j, 256)
                value = dot(quarter(gk, m)[...], w[:, :, columns].reshape(-1, 256))
                if m == 0:
                    value = value + h[:, columns] + rows[12:13, columns]
                else:
                    value = value + out[:, columns]
                out[:, columns] = value

            loop(4, onward)

            def back(g):
                columns = cut(g, 256)
                value = dot_nt(ct[...], w[g]) * room.slope[m % 2, :, columns]
                dz[256 * m : 256 * m + 256, columns] = value.astype(dz.dtype)

            loop(4, back)
            if m < 2:
                load(f"slope{m + 2}")
            sums = columns_sum(quarter(dz, m))
            for k in range(4):
                small[m, 13 + k : 14 + k, :] = sums[:, 256 * k : 256 * k + 256]
            tall(dn, quarter(dz, m), weight(2 * m + 1), m == 0)

        return run

    def write(ref, target, k):
        copy = pltpu.make_async_copy(ref, target, store_sem.at[k])
        copy.start()
        return copy

    stores = []

    def norm3():
        room.low[...] = out[...].astype(jnp.bfloat16)
        stores.append(write(room.low, result, 0))
        gain, shift, column = norm_back_rows(h, dn, row(2), ct, dh, room.e2)
        note(2, gain)
        note(11, shift)
        note(10, column)
        load("h1")

    def out2():
        load("k2", "lse2")
        tall(room.do2, room.e2, weight(8), True)

    def cross(first, count):
        def run():
            have("q2", "k2", "v2", "lse2")
            loop(
                count,
                lambda p: attend_back_pair(
                    p + first, room.q2, gk, v2, room.do2, room.lse, room.scores, room.gscores,
                    room.probs, room.gs, room.dq2, room.dk2, room.dv2, False,
                ),
            )

        return run

    def norm2():
        load("q1", "k1", "v1", "o1", "n1", "x", "lse1")
        note(8, columns_sum(room.dq2))
        note(9, columns_sum(room.dv2))
        tall(dn, room.dq2, weight(9), True)
        have("h1")
        gain, shift, column = norm_back_rows(h, dn, row(1), dh, dh, e1)
        note(1, gain)
        note(7, shift)
        note(6, column)

    def out1():
        tall(do1, e1, weight(10), True)

    def self_back(first, count):
        def run():
            have("q1", "k1", "v1", "lse1")
            part = pl.ds(0, 256)
            loop(
                count,
                lambda p: attend_back_pair(
                    p + first, q1, k1, v1, do1, room.lse, room.scores.at[part], room.gscores.at[part],
                    room.probs.at[part], room.gs.at[part], dq1, dk1, dv1, True,
                ),
            )

        return run

    def norm1():
        note(4, columns_sum(dq1))
        note(5, columns_sum(dv1))
        for k, grad in enumerate((dq1, dk1, dv1)):
            tall(dn, grad, weight(11 + k), k == 0)
        have("x")
        gain, shift, _ = norm_back_rows(x, dn, row(0), dh, out, None)
        note(0, gain)
        note(3, shift)
        stores.append(write(out, grad_tokens, 1))

    def frames_back(g):
        def run():
            wk, wv = weight(14, 1), weight(15, 0)
            stage = room.scores if g % 2 == 0 else room.gscores
            if g >= 2:
                stores[g].wait()

            def body(j):
                lines = cut(j, 256)
                stage[lines] = dot_nt(room.dk2[lines], wk[g]) + dot_nt(room.dv2[lines], wv[g])

            loop(4, body)
            stores.append(write(stage, grad_frames.at[:, pl.ds(256 * g, 256)], 2 + g))

        return run

    def outer(u, left, right, tokens=256):
        def body(g):
            columns = cut(g, 256)
            value = dot_tn(left[:, columns], right[...])
            room.grads[u % 2, g] = value.astype(jnp.bfloat16)

        loop(4, body)

    def grad(u):
        reduce.room(u)
        if u < 4:
            for m in range(4):
                value = dot_tn(gk[256 * m : 256 * m + 256, 256 * u : 256 * u + 256], ct[...])
                room.grads[u % 2, m] = value.astype(jnp.bfloat16)
        elif u < 8:
            have("n3")
            outer(u, n3, quarter(dz, u - 4))
        elif u == 8:
            have("o2")
            outer(u, room.o2, room.e2)
        elif u == 9:
            have("n2")
            outer(u, room.n2, room.dq2)
        elif u < 12:
            have("frames")
            outer(u, frames, room.dk2 if u == 10 else room.dv2)
        elif u == 12:
            have("o1")
            outer(u, o1, e1)
        elif u < 16:
            have("n1")
            outer(u, n1, (dq1, dk1, dv1)[u - 13])

    steps = [("start", -1, 2, start)]
    steps += [(f"feed{m}", -1, 9, feed(m)) for m in range(4)]
    steps += [("norm3", -1, 3, norm3), ("out2", 3, 2, out2)]
    steps += [(f"cross{k}", 3, 9, cross(2 * k, 2)) for k in range(4)]
    steps += [("norm2", -1, 5, norm2), ("out1", 7, 2, out1)]
    steps += [(f"self{k}", 7, 6, self_back(4 * k, 4)) for k in range(2)]
    steps += [("norm1", -1, 8, norm1)]
    steps += [(f"frames{g}", -1, 4, frames_back(g)) for g in range(4)]
    needs = ["start"] * 4 + [f"feed{m}" for m in range(4)] + ["norm3", "cross3", "cross3", "cross3", "norm2"]
    needs += ["self1"] * 3 + ["norm1"]

    load("table", "ct", "g0", "g1", "g2", "g3", "slope0", "h2", "slope1", "n3", "o2", "q2", "v2", "frames", "n2")
    reduce.open()
    done, now, tick, last = set(), 0.0, 0, -100.0
    left = list(steps)
    while left or tick < reduce.ticks:
        can_tick = tick < reduce.ticks and (tick > REDUCE_WIDE or needs[tick] in done)
        can_step = bool(left) and left[0][1] < tick
        if can_tick and (now - last >= BACK_PERIOD or not can_step):
            now = max(now, last + (BACK_PERIOD if not can_step else 0.0))
            last = now
            if tick < REDUCE_WIDE:
                grad(tick)
                now += 3.0
            reduce.tick(tick)
            now += 2.0
            tick += 1
        else:
            name, _, cost, run = left.pop(0)
            run()
            done.add(name)
            now += cost
    reduce.shut()
    stores[0].wait()
    stores[1].wait()
    stores[4].wait()
    stores[5].wait()


BACK_PERIOD = 7.0


def backward_all(full, tokens, frames, cotangent):
    low, wide = jnp.bfloat16, jnp.float32
    width = 1024
    shapes = [
        jax.ShapeDtypeStruct((256, width), low),
        jax.ShapeDtypeStruct((256, width), wide),
        jax.ShapeDtypeStruct((1024, width), wide),
        jax.ShapeDtypeStruct((3, 256, width), low),
        jax.ShapeDtypeStruct((256, width), low),
        jax.ShapeDtypeStruct((3, 256, width), low),
        jax.ShapeDtypeStruct((256, width), low),
        jax.ShapeDtypeStruct((256, 4 * width), low),
        jax.ShapeDtypeStruct((1024, width), low),
        jax.ShapeDtypeStruct((32, 256), wide),
    ]
    weights = list(full[:7])
    weights[5] = weights[5].reshape(4, 4, 256, width)
    args = (*weights, tokens, frames, cotangent, *full[7:])
    anywhere = pl.BlockSpec(memory_space=pl.ANY)
    return pl.pallas_call(
        backward_kernel,
        name="backward_and_reduce",
        out_shape=shapes,
        in_specs=[anywhere] * len(args),
        out_specs=[anywhere] * len(shapes),
        scratch_shapes=[pltpu.VMEM(shape, dtype) for _, shape, dtype in BACK_ROOMS]
        + lane_shapes(RING, OTHERS, HELD, FINALS, 256, width, low)
        + lane_shapes(1, 1, 1, 1, 32, 256, wide)
        + [
            pltpu.SemaphoreType.DMA((REDUCE_WIDE + 1, 9)),
            pltpu.SemaphoreType.DMA((REDUCE_WIDE + 1, 9)),
            pltpu.SemaphoreType.DMA((REDUCE_WIDE + 1, 2)),
            pltpu.SemaphoreType.REGULAR,
            pltpu.SemaphoreType.DMA((32,)),
            pltpu.SemaphoreType.DMA((len(BACK_WEIGHTS),)),
            pltpu.SemaphoreType.DMA((6,)),
        ],
        compiler_params=pltpu.CompilerParams(
            collective_id=1, has_side_effects=True, vmem_limit_bytes=VMEM_LIMIT
        ),
    )(*args)


def widen_pieces(refs):
    self_qkv, self_out, cross_qkv, cross_out, fc1, fc2 = refs
    pieces = [fc2.at[pl.ds(256 * m, 256)] for m in range(4)]
    pieces += [fc1.at[:, pl.ds(1024 * m, 1024)] for m in range(4)]
    pieces += [cross_out] + [cross_qkv.at[m] for m in range(3)] + [self_out] + [self_qkv.at[m] for m in range(3)]
    return pieces


def widen_kernel(*refs):
    result, grad_tokens, grad_frames, grads, small = *refs[:3], refs[3:9], refs[9]
    outs, gains, biases, hidden = refs[10:19], refs[19], refs[20], refs[21]
    low, high, v_result, v_tokens, v_frames, in_sem, out_sem = refs[22:]
    sources = widen_pieces(grads) + [result, grad_tokens, grad_frames]
    targets = widen_pieces(outs[3:]) + list(outs[:3])
    count = len(sources) - 3
    inside = [low.at[k] for k in range(count)] + [v_result, v_tokens, v_frames]
    ready = [high.at[k] for k in range(count)] + [v_result, v_tokens, v_frames]
    loads = [pltpu.make_async_copy(a, b, in_sem.at[k]) for k, (a, b) in enumerate(zip(sources, inside))]
    stores = [pltpu.make_async_copy(a, b, out_sem.at[k]) for k, (a, b) in enumerate(zip(ready, targets))]
    for load in loads:
        load.start()
    gains[...] = small[0:3]
    biases[...] = small[3:13]
    hidden[...] = small[13:17]
    for k in range(count + 3):
        loads[k].wait()
        if k < count:

            def body(i):
                high[k, cut(i, 64)] = f32(low[k, cut(i, 64)])

            loop(4, body)
        stores[k].start()
    for store in stores:
        store.wait()


def widen_all(done):
    wide = jnp.float32
    anywhere, inside = pl.BlockSpec(memory_space=pl.ANY), pl.BlockSpec(memory_space=pltpu.VMEM)
    shapes = [jax.ShapeDtypeStruct(a.shape, a.dtype if k == 0 else wide) for k, a in enumerate(done[:9])]
    shapes += [jax.ShapeDtypeStruct((rows, 256), wide) for rows in (3, 10, 4)]
    return pl.pallas_call(
        widen_kernel,
        name="widen",
        out_shape=shapes,
        in_specs=[anywhere] * 9 + [inside],
        out_specs=[anywhere] * 9 + [inside] * 3,
        scratch_shapes=[
            pltpu.VMEM((16, 256, 1024), jnp.bfloat16),
            pltpu.VMEM((16, 256, 1024), wide),
            pltpu.VMEM(done[0].shape, done[0].dtype),
            pltpu.VMEM(done[1].shape, wide),
            pltpu.VMEM(done[2].shape, wide),
            pltpu.SemaphoreType.DMA((19,)),
            pltpu.SemaphoreType.DMA((19,)),
        ],
        compiler_params=pltpu.CompilerParams(vmem_limit_bytes=VMEM_LIMIT),
    )(*done)


def shards_here(
    tokens,
    frames,
    cotangent,
    self_qkv,
    self_out,
    cross_qkv,
    cross_out,
    fc1_weight,
    fc2_weight,
    gains,
    biases,
    fc1_bias,
):
    part = gains.shape[1]
    small = jnp.concatenate(
        [gains, biases, fc1_bias.reshape(4, part), jnp.zeros((15, part), jnp.bfloat16)], axis=0
    )
    shards = (self_qkv, self_out, cross_qkv, cross_out, fc1_weight, fc2_weight)
    full = forward_all(shards, small, tokens[0], frames[0])
    done = widen_all(backward_all(full, tokens[0], frames[0], cotangent[0]))
    return (done[0][None], done[1][None], done[2][None], *done[3:11], done[11].reshape(-1))


def solution(mesh):
    in_specs = (
        P((GROUP, REPLICA), None, None),
        P((GROUP, REPLICA), None, None),
        P((GROUP, REPLICA), None, None),
        P(None, GROUP, None),
        P(GROUP, None),
        P(None, GROUP, None),
        P(GROUP, None),
        P(GROUP, None),
        P(GROUP, None),
        P(None, GROUP),
        P(None, GROUP),
        P(GROUP),
    )
    out_specs = (
        P((GROUP, REPLICA), None, None),
        P((GROUP, REPLICA), None, None),
        P((GROUP, REPLICA), None, None),
        P(None, GROUP, None),
        P(GROUP, None),
        P(None, GROUP, None),
        P(GROUP, None),
        P(GROUP, None),
        P(GROUP, None),
        P(None, GROUP),
        P(None, GROUP),
        P(GROUP),
    )
    here = mesh.shape[GROUP] == 4 and mesh.shape[REPLICA] == 8
    body = shards_here if here else shards_any
    return jax.shard_map(body, mesh=mesh, in_specs=in_specs, out_specs=out_specs, check_vma=False)
```

```python
from functools import partial
import math

import jax
import jax.numpy as jnp
from jax import lax
from jax.experimental import pallas as pl
from jax.experimental.pallas import tpu as pltpu
from jax.sharding import PartitionSpec as P

HEADS = 16
HEAD_DIM = 64
GROUP, REPLICA = "group", "replica"


EPSILON = 1e-05


def layer_norm(values, gain, shift):
    center = values - jnp.mean(values, axis=-1, keepdims=True)
    spread = jnp.mean(center * center, axis=-1, keepdims=True)
    return center * lax.rsqrt(spread + EPSILON) * gain + shift


def norm_back(values, gain, shift, grad):
    result, pullback = jax.vjp(layer_norm, values, gain, shift)
    return pullback(grad)


def dense(left, right):
    return jnp.dot(left, right, preferred_element_type=jnp.float32)


def left_dense(left, right):
    return lax.dot_general(
        left, right, (((0,), (0,)), ((), ())), preferred_element_type=jnp.float32
    )


def right_dense(grad, weight):
    return lax.dot_general(
        grad, weight, (((1,), (1,)), ((), ())), preferred_element_type=jnp.float32
    )


def column_sum(values):
    return jnp.sum(values.astype(jnp.float32), axis=0)


def split_heads(rows, batch):
    return rows.reshape(batch, -1, HEADS, rows.shape[-1] // HEADS)


def scores_of(query_heads, key_heads, masked):
    scores = jnp.einsum(
        "bqhd,bkhd->bhqk", query_heads, key_heads, preferred_element_type=jnp.float32
    )
    if masked:
        shape = (query_heads.shape[1], key_heads.shape[1])
        allowed = lax.broadcasted_iota(jnp.int32, shape, 0) >= lax.broadcasted_iota(
            jnp.int32, shape, 1
        )
        scores = jnp.where(allowed, scores, -jnp.inf)
    return scores


def attend(queries, keys, values, batch, masked):
    query_heads = split_heads(queries, batch)
    key_heads = split_heads(keys, batch)
    value_heads = split_heads(values, batch)
    scores = scores_of(query_heads, key_heads, masked)
    highest = jnp.max(scores, axis=-1, keepdims=True)
    expo = jnp.exp(scores - highest)
    total = jnp.sum(expo, axis=-1, keepdims=True)
    probs = (expo / total).astype(jnp.bfloat16)
    mixed = jnp.einsum("bhqk,bkhd->bqhd", probs, value_heads, preferred_element_type=jnp.float32)
    return (mixed.reshape(queries.shape).astype(jnp.bfloat16), highest + jnp.log(total))


def attend_back(queries, keys, values, grad_mixed, logsum, batch, masked):
    query_heads = split_heads(queries, batch)
    key_heads = split_heads(keys, batch)
    value_heads = split_heads(values, batch)
    grad_heads = split_heads(grad_mixed, batch)
    probs = jnp.exp(scores_of(query_heads, key_heads, masked) - logsum)
    probs_low = probs.astype(jnp.bfloat16)
    grad_probs = jnp.einsum(
        "bqhd,bkhd->bhqk", grad_heads, value_heads, preferred_element_type=jnp.float32
    )
    grad_values = jnp.einsum(
        "bhqk,bqhd->bkhd", probs_low, grad_heads, preferred_element_type=jnp.float32
    )
    center = jnp.sum(probs * grad_probs, axis=-1, keepdims=True)
    grad_scores = (probs * (grad_probs - center)).astype(jnp.bfloat16)
    grad_queries = jnp.einsum(
        "bhqk,bkhd->bqhd", grad_scores, key_heads, preferred_element_type=jnp.float32
    )
    grad_keys = jnp.einsum(
        "bhqk,bqhd->bkhd", grad_scores, query_heads, preferred_element_type=jnp.float32
    )
    return (
        grad_queries.reshape(queries.shape),
        grad_keys.reshape(keys.shape),
        grad_values.reshape(keys.shape),
    )


def forward(tokens, frames, weights):
    self_qkv, self_out, cross_qkv, cross_out, fc1_weight, fc2_weight, gains, biases, fc1_bias = (
        weights
    )
    batch = tokens.shape[0]
    width = tokens.shape[2]
    scale = 1.0 / math.sqrt(HEAD_DIM)
    gain_rows = gains.astype(jnp.float32)
    bias_rows = biases.astype(jnp.float32)
    resid0 = tokens.reshape(-1, width).astype(jnp.float32)
    frame_rows = frames.reshape(-1, width)
    normed1 = layer_norm(resid0, gain_rows[0], bias_rows[0]).astype(jnp.bfloat16)
    query1 = ((dense(normed1, self_qkv[0]) + bias_rows[1]) * scale).astype(jnp.bfloat16)
    key1 = dense(normed1, self_qkv[1]).astype(jnp.bfloat16)
    value1 = (dense(normed1, self_qkv[2]) + bias_rows[2]).astype(jnp.bfloat16)
    mixed1, logsum1 = attend(query1, key1, value1, batch, True)
    resid1 = resid0 + dense(mixed1, self_out) + bias_rows[3]
    normed2 = layer_norm(resid1, gain_rows[1], bias_rows[4]).astype(jnp.bfloat16)
    query2 = ((dense(normed2, cross_qkv[0]) + bias_rows[5]) * scale).astype(jnp.bfloat16)
    key2 = dense(frame_rows, cross_qkv[1]).astype(jnp.bfloat16)
    value2 = (dense(frame_rows, cross_qkv[2]) + bias_rows[6]).astype(jnp.bfloat16)
    mixed2, logsum2 = attend(query2, key2, value2, batch, False)
    resid2 = resid1 + dense(mixed2, cross_out) + bias_rows[7]
    normed3 = layer_norm(resid2, gain_rows[2], bias_rows[8]).astype(jnp.bfloat16)
    hidden_pre = dense(normed3, fc1_weight) + fc1_bias.astype(jnp.float32)
    hidden = jax.nn.gelu(hidden_pre, approximate=False).astype(jnp.bfloat16)
    result = resid2 + dense(hidden, fc2_weight) + bias_rows[9]
    saved = (
        resid0,
        frame_rows,
        normed1,
        query1,
        key1,
        value1,
        mixed1,
        logsum1,
        resid1,
        normed2,
        query2,
        key2,
        value2,
        mixed2,
        logsum2,
        resid2,
        normed3,
        hidden_pre,
        hidden,
    )
    return (result, saved)


def backward(cotangent, weights, saved, settle_mlp, settle_cross, settle_self):
    self_qkv, self_out, cross_qkv, cross_out, fc1_weight, fc2_weight, gains, biases, fc1_bias = (
        weights
    )
    (
        resid0,
        frame_rows,
        normed1,
        query1,
        key1,
        value1,
        mixed1,
        logsum1,
        resid1,
        normed2,
        query2,
        key2,
        value2,
        mixed2,
        logsum2,
        resid2,
        normed3,
        hidden_pre,
        hidden,
    ) = saved
    batch = cotangent.shape[0]
    width = cotangent.shape[2]
    scale = 1.0 / math.sqrt(HEAD_DIM)
    gain_rows = gains.astype(jnp.float32)
    bias_rows = biases.astype(jnp.float32)
    grad_out = cotangent.reshape(-1, width).astype(jnp.float32)
    grad_branch3 = grad_out.astype(jnp.bfloat16)
    fc2_grad = left_dense(hidden, grad_branch3)
    bias9 = column_sum(grad_branch3)
    grad_hidden = right_dense(grad_branch3, fc2_weight)
    unused, gelu_pull = jax.vjp(partial(jax.nn.gelu, approximate=False), hidden_pre)
    grad_pre = gelu_pull(grad_hidden)[0].astype(jnp.bfloat16)
    fc1_grad = left_dense(normed3, grad_pre)
    fc1_bias_grad = column_sum(grad_pre)
    mlp_part = settle_mlp((fc1_grad, fc2_grad, fc1_bias_grad))
    grad_resid2, gain3, shift3 = norm_back(
        resid2, gain_rows[2], bias_rows[8], right_dense(grad_pre, fc1_weight)
    )
    grad_resid2 = grad_out + grad_resid2
    grad_branch2 = grad_resid2.astype(jnp.bfloat16)
    cross_out_grad = left_dense(mixed2, grad_branch2)
    bias7 = column_sum(grad_branch2)
    grad_mixed2 = right_dense(grad_branch2, cross_out).astype(jnp.bfloat16)
    grad_q2, grad_k2, grad_v2 = attend_back(
        query2, key2, value2, grad_mixed2, logsum2, batch, False
    )
    grad_q2 = (grad_q2.astype(jnp.bfloat16).astype(jnp.float32) * scale).astype(jnp.bfloat16)
    grad_k2 = grad_k2.astype(jnp.bfloat16)
    grad_v2 = grad_v2.astype(jnp.bfloat16)
    cross_qkv_grad = [
        left_dense(normed2, grad_q2),
        left_dense(frame_rows, grad_k2),
        left_dense(frame_rows, grad_v2),
    ]
    bias5 = column_sum(grad_q2)
    bias6 = column_sum(grad_v2)
    cross_part = settle_cross((cross_qkv_grad, cross_out_grad))
    grad_frames = right_dense(grad_k2, cross_qkv[1]) + right_dense(grad_v2, cross_qkv[2])
    grad_resid1, gain2, shift2 = norm_back(
        resid1, gain_rows[1], bias_rows[4], right_dense(grad_q2, cross_qkv[0])
    )
    grad_resid1 = grad_resid2 + grad_resid1
    grad_branch1 = grad_resid1.astype(jnp.bfloat16)
    self_out_grad = left_dense(mixed1, grad_branch1)
    bias3 = column_sum(grad_branch1)
    grad_mixed1 = right_dense(grad_branch1, self_out).astype(jnp.bfloat16)
    grad_q1, grad_k1, grad_v1 = attend_back(query1, key1, value1, grad_mixed1, logsum1, batch, True)
    grad_q1 = (grad_q1.astype(jnp.bfloat16).astype(jnp.float32) * scale).astype(jnp.bfloat16)
    grad_k1 = grad_k1.astype(jnp.bfloat16)
    grad_v1 = grad_v1.astype(jnp.bfloat16)
    self_qkv_grad = [
        left_dense(normed1, grad_q1),
        left_dense(normed1, grad_k1),
        left_dense(normed1, grad_v1),
    ]
    bias1 = column_sum(grad_q1)
    bias2 = column_sum(grad_v1)
    grad_normed1 = (
        right_dense(grad_q1, self_qkv[0])
        + right_dense(grad_k1, self_qkv[1])
        + right_dense(grad_v1, self_qkv[2])
    )
    grad_resid0, gain1, shift1 = norm_back(resid0, gain_rows[0], bias_rows[0], grad_normed1)
    grad_tokens = grad_resid1 + grad_resid0
    gains_grad = jnp.stack([gain1, gain2, gain3])
    biases_grad = jnp.stack(
        [shift1, bias1, bias2, bias3, shift2, bias5, bias6, bias7, shift3, bias9]
    )
    self_part = settle_self((self_qkv_grad, self_out_grad, gains_grad, biases_grad))
    return (grad_tokens, grad_frames, mlp_part, cross_part, self_part)


def unchanged(grads):
    return grads


def shards_any(
    tokens,
    frames,
    cotangent,
    self_qkv,
    self_out,
    cross_qkv,
    cross_out,
    fc1_weight,
    fc2_weight,
    gains,
    biases,
    fc1_bias,
):
    weights = (
        lax.all_gather(self_qkv, GROUP, axis=1, tiled=True),
        lax.all_gather(self_out, GROUP, axis=0, tiled=True),
        lax.all_gather(cross_qkv, GROUP, axis=1, tiled=True),
        lax.all_gather(cross_out, GROUP, axis=0, tiled=True),
        lax.all_gather(fc1_weight, GROUP, axis=0, tiled=True),
        lax.all_gather(fc2_weight, GROUP, axis=0, tiled=True),
        lax.all_gather(gains, GROUP, axis=1, tiled=True),
        lax.all_gather(biases, GROUP, axis=1, tiled=True),
        lax.all_gather(fc1_bias, GROUP, axis=0, tiled=True),
    )
    result, saved = forward(tokens, frames, weights)
    grad_tokens, grad_frames, mlp_part, cross_part, self_part = backward(
        cotangent, weights, saved, unchanged, unchanged, unchanged
    )
    shares = (
        lax.psum_scatter(
            jnp.stack(self_part[0]).astype(jnp.bfloat16), GROUP, scatter_dimension=1, tiled=True
        ).astype(jnp.float32),
        lax.psum_scatter(
            self_part[1].astype(jnp.bfloat16), GROUP, scatter_dimension=0, tiled=True
        ).astype(jnp.float32),
        lax.psum_scatter(
            jnp.stack(cross_part[0]).astype(jnp.bfloat16), GROUP, scatter_dimension=1, tiled=True
        ).astype(jnp.float32),
        lax.psum_scatter(
            cross_part[1].astype(jnp.bfloat16), GROUP, scatter_dimension=0, tiled=True
        ).astype(jnp.float32),
        lax.psum_scatter(
            mlp_part[0].astype(jnp.bfloat16), GROUP, scatter_dimension=0, tiled=True
        ).astype(jnp.float32),
        lax.psum_scatter(
            mlp_part[1].astype(jnp.bfloat16), GROUP, scatter_dimension=0, tiled=True
        ).astype(jnp.float32),
        lax.psum_scatter(
            self_part[2].astype(jnp.bfloat16), GROUP, scatter_dimension=1, tiled=True
        ).astype(jnp.float32),
        lax.psum_scatter(
            self_part[3].astype(jnp.bfloat16), GROUP, scatter_dimension=1, tiled=True
        ).astype(jnp.float32),
        lax.psum_scatter(
            mlp_part[2].astype(jnp.bfloat16), GROUP, scatter_dimension=0, tiled=True
        ).astype(jnp.float32),
    )
    summed = (
        lax.psum(shares[0].astype(jnp.bfloat16), REPLICA).astype(jnp.float32),
        lax.psum(shares[1].astype(jnp.bfloat16), REPLICA).astype(jnp.float32),
        lax.psum(shares[2].astype(jnp.bfloat16), REPLICA).astype(jnp.float32),
        lax.psum(shares[3].astype(jnp.bfloat16), REPLICA).astype(jnp.float32),
        lax.psum(shares[4].astype(jnp.bfloat16), REPLICA).astype(jnp.float32),
        lax.psum(shares[5].astype(jnp.bfloat16), REPLICA).astype(jnp.float32),
        lax.psum(shares[6].astype(jnp.bfloat16), REPLICA).astype(jnp.float32),
        lax.psum(shares[7].astype(jnp.bfloat16), REPLICA).astype(jnp.float32),
        lax.psum(shares[8].astype(jnp.bfloat16), REPLICA).astype(jnp.float32),
    )
    (
        self_qkv_grad,
        self_out_grad,
        cross_qkv_grad,
        cross_out_grad,
        fc1_grad,
        fc2_grad,
        gains_grad,
        biases_grad,
        fc1_bias_grad,
    ) = summed
    return (
        result.reshape(tokens.shape).astype(jnp.bfloat16),
        grad_tokens.reshape(tokens.shape),
        grad_frames.reshape(frames.shape),
        self_qkv_grad,
        self_out_grad,
        cross_qkv_grad,
        cross_out_grad,
        fc1_grad,
        fc2_grad,
        gains_grad,
        biases_grad,
        fc1_bias_grad,
    )


MESH = pl.DeviceIdType.MESH
VMEM_LIMIT = 64 * 1024 * 1024 - 128 * 1024


class Spot:
    def __init__(self):
        self.g = lax.axis_index(GROUP)
        self.r = lax.axis_index(REPLICA)
        self.core = lax.rem(self.r, 2)
        self.z = lax.div(self.r, 2)
        self.zb = lax.rem(self.z, 2)
        self.gx = self.g + 1 - 2 * lax.rem(self.g, 2)
        self.gy = lax.rem(self.g + 2, 4)
        self.gd = self.gx + 2 - 4 * lax.div(self.gx, 2)
        self.rc = self.r + 1 - 2 * self.core
        self.rz = self.r + 2 - 4 * self.zb
        self.x_id = (self.gx, self.r)
        self.y_id = (self.gy, self.r)
        self.d_id = (self.gd, self.r)
        self.c_id = (self.g, self.rc)
        self.z_id = (self.g, self.rz)


def meet(*ids):
    barrier = pltpu.get_barrier_semaphore()
    for device in ids:
        pl.semaphore_signal(barrier, inc=1, device_id=device, device_id_type=MESH)
    pl.semaphore_wait(barrier, len(ids))


GATHER_CHUNKS = (
    [(0, m, 0, 256, 0, 1024, m != 0) for m in range(3)]
    + [(1, None, 0, 256, 0, 1024, False)]
    + [(2, m, 0, 256, 0, 1024, m != 0) for m in range(3)]
    + [(3, None, 0, 256, 0, 1024, False)]
    + [(4, None, 0, 256, 1024 * m, 1024, m != 3) for m in range(4)]
    + [(5, None, 256 * m, 256, 0, 1024, m != 3) for m in range(4)]
)
N_GATHER = len(GATHER_CHUNKS)


class Gather:
    def __init__(self, at, shards, small, fulls, small_full, stages, small_stage, sems):
        self.load_sem, self.put_sem, self.send_sem, self.recv_sem, small_send, small_recv, small_local = sems
        self.at, self.shards, self.fulls = at, shards, fulls
        self.loads = [pltpu.make_async_copy(shards[n], stages[n], self.load_sem.at[n]) for n in range(6)]
        self.small_load = pltpu.make_async_copy(small, small_stage, small_local.at[0])
        self.small_put = pltpu.make_async_copy(small_stage, small_full.at[at.g], small_local.at[1])
        self.small_copies = [
            pltpu.make_async_remote_copy(
                small, small_full.at[at.g], small_send.at[n], small_recv.at[n],
                device_id=device, device_id_type=MESH,
            )
            for n, device in enumerate((at.x_id, at.y_id, at.d_id))
        ]
        self.puts = []
        for n in range(6):
            where = (slice(None), at.g) if n in (0, 2) else (at.g,)
            self.puts.append(pltpu.make_async_copy(stages[n], fulls[n].at[where], self.put_sem.at[n]))
        self.plans = [self.plan(i) for i in range(N_GATHER)]
        self.arrived, self.placed = set(), set()

    def full(self, i, g, start, rows):
        n, lead, first, _, column, columns, _ = GATHER_CHUNKS[i]
        where = (g, pl.ds(first + start, rows), pl.ds(column, columns))
        return self.fulls[n].at[where if lead is None else (lead,) + where]

    def shard(self, i, start, rows):
        n, lead, first, _, column, columns, _ = GATHER_CHUNKS[i]
        where = (pl.ds(first + start, rows), pl.ds(column, columns))
        return self.shards[n].at[where if lead is None else (lead,) + where]

    def plan(self, i):
        at = self.at

        def put(k, src, g, start, rows, device):
            return pltpu.make_async_remote_copy(
                src, self.full(i, g, start, rows), self.send_sem.at[i, k], self.recv_sem.at[i, k],
                device_id=device, device_id_type=MESH,
            )

        rows, split = GATHER_CHUNKS[i][3], GATHER_CHUNKS[i][6]
        half = rows // 2
        base = pl.multiple_of(at.core * half, half)
        core_base = base
        if split:
            half = half // 2
            base = pl.multiple_of(base + at.zb * half, half)
        quarter = half // 2
        mine = self.shard(i, base, half)
        moves = [
            put(0, mine, at.g, base, half, at.x_id),
            put(1, mine, at.g, base, half, at.y_id),
            put(2, self.full(i, at.gy, base + quarter, quarter), at.gy, base + quarter, quarter, at.x_id),
            put(3, self.full(i, at.gx, base, quarter), at.gx, base, quarter, at.y_id),
        ]
        for k, g in enumerate((at.gx, at.gy, at.gd)):
            moves.append(put(4 + k, self.full(i, g, core_base, rows // 2), g, core_base, rows // 2, at.c_id))
        if split:
            for k, g in enumerate((at.gx, at.gy, at.gd)):
                moves.append(put(7 + k, self.full(i, g, base, half), g, base, half, at.z_id))
        return moves, split

    def open(self):
        at = self.at
        for load in self.loads:
            load.start()
        self.small_load.start()
        meet(at.x_id, at.y_id, at.d_id, at.c_id, at.z_id)
        self.begin(0)
        for copy in self.small_copies:
            copy.start()
        self.begin(1)
        self.small_load.wait()
        self.small_put.start()
        for n in range(6):
            self.loads[n].wait()
            self.puts[n].start()

    def small_ready(self):
        self.small_put.wait()
        for copy in self.small_copies:
            copy.wait()

    def begin(self, i):
        moves, _ = self.plans[i]
        moves[0].start()
        moves[1].start()

    def second(self, i):
        moves, split = self.plans[i]
        moves[0].wait_recv()
        moves[1].wait_recv()
        moves[2].start()
        moves[3].start()
        for k in (7, 8) if split else (4, 5):
            moves[k].start()

    def third(self, i):
        moves, split = self.plans[i]
        moves[2].wait_recv()
        moves[3].wait_recv()
        moves[9 if split else 6].start()

    def fourth(self, i):
        moves, split = self.plans[i]
        if split:
            for k in (7, 8, 9):
                moves[k].wait_recv()
            for k in (4, 5, 6):
                moves[k].start()

    ticks = N_GATHER + 2

    def tick(self, i):
        if i < N_GATHER:
            self.second(i)
        if i + 2 < N_GATHER:
            self.begin(i + 2)
        if 0 <= i - 1 < N_GATHER:
            self.third(i - 1)
        if 0 <= i - 2 < N_GATHER:
            self.fourth(i - 2)

    def ready(self, i):
        n = GATHER_CHUNKS[i][0]
        if n not in self.placed:
            self.placed.add(n)
            self.puts[n].wait()
        if i not in self.arrived:
            self.arrived.add(i)
            for k in (4, 5, 6):
                self.plans[i][0][k].wait_recv()

    def close(self):
        for i in range(N_GATHER):
            self.ready(i)
            moves, split = self.plans[i]
            for k in range(10 if split else 7):
                moves[k].wait_send()


def f32(value):
    return value.astype(jnp.float32)


def dot(left, right):
    return jnp.dot(left, right, preferred_element_type=jnp.float32)


def dot_tn(left, right):
    return lax.dot_general(left, right, (((0,), (0,)), ((), ())), preferred_element_type=jnp.float32)


def dot_nt(left, right):
    return lax.dot_general(left, right, (((1,), (1,)), ((), ())), preferred_element_type=jnp.float32)


def loop(count, body):
    def step(i, carry):
        body(i)
        return carry

    lax.fori_loop(0, count, step, 0)


def cut(i, size):
    return pl.ds(pl.multiple_of(i * size, size), size)


def norm_rows(src, dst, gain, shift):
    def body(i):
        values = f32(src[cut(i, 32)])
        center = values - jnp.mean(values, axis=-1, keepdims=True)
        spread = jnp.mean(center * center, axis=-1, keepdims=True)
        dst[cut(i, 32)] = (center * lax.rsqrt(spread + EPSILON) * gain[...] + shift[...]).astype(dst.dtype)

    loop(src.shape[0] // 32, body)


def product(left, weight, store, tile=256):
    def body(j):
        columns = cut(j, tile)
        store(columns, dot(left[...], weight[:, :, columns].reshape(-1, tile)))

    loop(weight.shape[-1] // tile, body)


def attend_pair(p, q, k, v, o, lse, scores, probs, causal):
    columns = cut(p, 128)
    keys, count = k.shape[0], q.shape[0]
    qq, kk, vv = q[:, columns], k[:, columns], v[:, columns]
    lane = lax.broadcasted_iota(jnp.int32, qq.shape, 1)
    vt = vv.T
    block = 128
    sides = []
    for a in range(2):
        qa = jnp.where((lane < 64) if a == 0 else (lane >= 64), qq, jnp.zeros_like(qq))
        scores[...] = dot_nt(kk, qa)

        def rows_of(j):
            part = scores[cut(j, block)]
            if causal:
                key = lax.broadcasted_iota(jnp.int32, part.shape, 0) + j * block
                query = lax.broadcasted_iota(jnp.int32, part.shape, 1)
                part = jnp.where(query >= key, part, -jnp.inf)
            return part

        def top(j, carry):
            return jnp.maximum(carry, jnp.max(rows_of(j), axis=0, keepdims=True))

        highest = lax.fori_loop(0, keys // block, top, jnp.full((1, count), -jnp.inf, jnp.float32))

        def expo(j, carry):
            e = jnp.exp(rows_of(j) - highest)
            scores[cut(j, block)] = e
            return carry + jnp.sum(e, axis=0, keepdims=True)

        total = lax.fori_loop(0, keys // block, expo, jnp.zeros((1, count), jnp.float32))
        share = 1.0 / total

        def rounded(j):
            probs[cut(j, block)] = (scores[cut(j, block)] * share).astype(probs.dtype)

        loop(keys // block, rounded)
        lse[2 * p + a] = jnp.broadcast_to(highest + jnp.log(total), (8, count))
        sides.append(dot(vt[64 * a : 64 * a + 64], probs[...]))
    o[:, columns] = jnp.concatenate(sides, axis=0).T.astype(o.dtype)


def attend_back_pair(p, q, k, v, go, lse, scores, gscores, probs, gs, gq, gk, gv, causal):
    columns = cut(p, 128)
    keys, count = k.shape[0], q.shape[0]
    qq, kk, vv, dd = q[:, columns], k[:, columns], v[:, columns], go[:, columns]
    lane = lax.broadcasted_iota(jnp.int32, qq.shape, 1)
    zero = jnp.zeros_like(qq)
    kt = kk.T
    block = 128
    sides, qs, ds = [], [], []
    for a in range(2):
        here = (lane < 64) if a == 0 else (lane >= 64)
        qa, da = jnp.where(here, qq, zero), jnp.where(here, dd, zero)
        qs.append(qa)
        ds.append(da)
        scores[...] = dot_nt(kk, qa)
        gscores[...] = dot_nt(vv, da)
        line = lse[2 * p + a][0:1]
        across = slice(a * count, (a + 1) * count)

        def first(j, carry):
            part = scores[cut(j, block)]
            if causal:
                key = lax.broadcasted_iota(jnp.int32, part.shape, 0) + j * block
                query = lax.broadcasted_iota(jnp.int32, part.shape, 1)
                part = jnp.where(query >= key, part, -jnp.inf)
            e = jnp.exp(part - line)
            scores[cut(j, block)] = e
            probs[cut(j, block), across] = e.astype(probs.dtype)
            return carry + jnp.sum(e * gscores[cut(j, block)], axis=0, keepdims=True)

        center = lax.fori_loop(0, keys // block, first, jnp.zeros((1, count), jnp.float32))

        def second(j):
            rows = cut(j, block)
            gs[rows, across] = (scores[rows] * (gscores[rows] - center)).astype(gs.dtype)

        loop(keys // block, second)
        sides.append(dot(kt[64 * a : 64 * a + 64], gs[:, across]))
    gv[:, columns] = dot(probs[...], jnp.concatenate(ds, axis=0)).astype(gv.dtype)
    gk[:, columns] = dot(gs[...], jnp.concatenate(qs, axis=0)).astype(gk.dtype)
    side = jnp.concatenate(sides, axis=0).T.astype(jnp.bfloat16)
    gq[:, columns] = (f32(side) * SCALE).astype(gq.dtype)

def woven(ticks, period, first, steps):
    order, now, tick = [], 0.0, 0
    left = list(range(len(steps)))
    while left or tick < ticks:
        due = first + tick * period
        if left and steps[left[0]][0] < tick and (now < due or tick >= ticks):
            now += steps[left[0]][1]
            order.append(("step", left.pop(0)))
        else:
            now = max(now, due)
            order.append(("tick", tick))
            tick += 1
    return order


ACTS = (
    [("n1", (256, 1024), jnp.bfloat16), ("q1", (256, 1024), jnp.bfloat16), ("k1", (256, 1024), jnp.bfloat16)]
    + [("v1", (256, 1024), jnp.bfloat16), ("o1", (256, 1024), jnp.bfloat16), ("lse1", (16, 8, 256), jnp.float32)]
    + [("h1", (256, 1024), jnp.float32), ("n2", (256, 1024), jnp.bfloat16), ("q2", (256, 1024), jnp.bfloat16)]
    + [("k2", (1024, 1024), jnp.bfloat16), ("v2", (1024, 1024), jnp.bfloat16), ("o2", (256, 1024), jnp.bfloat16)]
    + [("lse2", (16, 8, 256), jnp.float32), ("h2", (256, 1024), jnp.float32), ("n3", (256, 1024), jnp.bfloat16)]
    + [("slope", (4, 256, 1024), jnp.float32), ("g", (4, 256, 1024), jnp.bfloat16)]
)
N_ACTS = len(ACTS)
SCALE = 0.125


def set_rows(small_full, rows, hidden):
    for g in range(4):
        for k in range(13):
            rows[k : k + 1, 256 * g : 256 * g + 256] = f32(small_full[g, k : k + 1])
        for k in range(4):
            hidden[g : g + 1, 256 * k : 256 * k + 256] = f32(small_full[g, 13 + k : 14 + k])


def forward_kernel(*refs):
    shards, small, tokens, frames = refs[:6], refs[6], refs[7], refs[8]
    fulls, small_full = refs[9:15], refs[15]
    saved = refs[16 : 16 + N_ACTS]
    refs = refs[16 + N_ACTS :]
    acts = dict(zip([name for name, _, _ in ACTS], refs[:N_ACTS]))
    refs = refs[N_ACTS:]
    stages, small_stage, sems = refs[:6], refs[6], refs[7:14]
    x, kept, table, rows, hidden, ring, scores1, probs1, scores2, probs2, in_sem, ring_sem, save_sem = refs[14:]
    at = Spot()
    gather = Gather(at, shards, small, fulls, small_full, stages, small_stage, sems)

    x_load = pltpu.make_async_copy(tokens, x, in_sem.at[0])
    frames_load = pltpu.make_async_copy(frames, kept, in_sem.at[1])
    table_load = pltpu.make_async_copy(small_full, table, in_sem.at[2])
    x_load.start()
    frames_load.start()
    gather.open()
    saves = []

    def save(*names):
        for name in names:
            k = [n for n, _, _ in ACTS].index(name)
            copy = pltpu.make_async_copy(acts[name], saved[k], save_sem.at[k])
            copy.start()
            saves.append(copy)

    def fetch(i):
        n, lead, _, _, column, columns, _ = GATHER_CHUNKS[i]
        source = fulls[n] if lead is None else fulls[n].at[lead]
        if n == 4:
            source = source.at[:, :, pl.ds(column, columns)]
        return pltpu.make_async_copy(source, ring.at[i % 3], ring_sem.at[i])

    fetched = set()
    done_ticks = [0]

    def weight(i):
        for k in (i, i + 1):
            if k not in fetched and k < 12 and (k == i or k + 2 < done_ticks[0]):
                fetched.add(k)
                gather.ready(k)
                fetch(k).start()
        fetch(i).wait()
        return ring.at[i % 3]

    def row(k):
        return rows.at[k : k + 1]

    def start():
        gather.small_ready()
        table_load.start()
        x_load.wait()
        table_load.wait()
        set_rows(table, rows, hidden)
        norm_rows(x, acts["n1"], row(0), row(3))
        save("n1")

    def project(name, i, source, bias, scale):
        def run():
            w, target = weight(i), acts[name]

            def store(columns, value):
                if bias is not None:
                    value = value + rows[bias : bias + 1, columns]
                if scale:
                    value = value * SCALE
                target[:, columns] = value.astype(target.dtype)

            product(acts[source], w, store)
            save(name)

        return run

    def project_frames(name, i, bias):
        def run():
            if i == 5:
                frames_load.wait()
            w, target = weight(i), acts[name]

            def body(j):
                columns = cut(j, 256)
                value = dot(kept[...], w[:, :, columns].reshape(-1, 256))
                if bias is not None:
                    value = value + rows[bias : bias + 1, columns]
                target[:, columns] = value.astype(target.dtype)

            loop(4, body)
            save(name)

        return run

    def attend(first, count, q, k, v, o, lse, scores, probs, causal, last):
        def run():
            loop(
                count,
                lambda p: attend_pair(
                    p + first, acts[q], acts[k], acts[v], acts[o], acts[lse], scores, probs, causal
                ),
            )
            if last:
                save(o, lse)

        return run

    def join(i, source, base, bias, target, gain, shift, normed):
        def run():
            w, out = weight(i), acts[target]

            def store(columns, value):
                out[:, columns] = f32(base[:, columns]) + value + rows[bias : bias + 1, columns]

            product(acts[source], w, store)
            norm_rows(out, acts[normed], row(gain), row(shift))
            save(target, normed)

        return run

    def expand(m):
        def run():
            w = weight(8 + m)
            slope, g = acts["slope"], acts["g"]

            def store(columns, value):
                z = value + hidden[m : m + 1, columns]
                below = 0.5 + 0.5 * lax.erf(z * math.sqrt(0.5))
                slope[m, :, columns] = below + z * (jnp.exp(-0.5 * z * z) * (1.0 / math.sqrt(2.0 * math.pi)))
                g[m, :, columns] = (z * below).astype(g.dtype)

            product(acts["n3"], w, store)
            if m == 3:
                save("slope", "g")

        return run

    steps = [(0, 3, start)]
    steps += [(2, 3, project("q1", 0, "n1", 3 + 1, True)), (3, 3, project("k1", 1, "n1", None, False))]
    steps += [(4, 3, project("v1", 2, "n1", 3 + 2, False))]
    for part in range(2):
        steps.append((4, 6, attend(4 * part, 4, "q1", "k1", "v1", "o1", "lse1", scores1, probs1, True, part == 1)))
    steps.append((5, 5, join(3, "o1", x, 3 + 3, "h1", 1, 3 + 4, "n2")))
    steps += [(6, 3, project("q2", 4, "n2", 3 + 5, True)), (7, 6, project_frames("k2", 5, None))]
    steps += [(8, 6, project_frames("v2", 6, 3 + 6))]
    for part in range(8):
        steps.append((8, 2.5, attend(part, 1, "q2", "k2", "v2", "o2", "lse2", scores2, probs2, False, part == 7)))
    steps.append((9, 5, join(7, "o2", acts["h1"], 3 + 7, "h2", 2, 3 + 8, "n3")))
    for m in range(4):
        steps.append((10 + m, 6, expand(m)))
    for kind, i in woven(gather.ticks, 5.5, 5.0, steps):
        if kind == "tick":
            gather.tick(i)
            done_ticks[0] = i + 1
        else:
            steps[i][2]()
    gather.close()
    for copy in saves:
        copy.wait()


def forward_all(shards, small, tokens, frames):
    shapes = []
    for array in shards:
        lead, tail = array.shape[:-2], array.shape[-2:]
        shapes.append(jax.ShapeDtypeStruct(lead + (4,) + tail, array.dtype))
    shapes.append(jax.ShapeDtypeStruct((4,) + small.shape, small.dtype))
    shapes += [jax.ShapeDtypeStruct(shape, dtype) for _, shape, dtype in ACTS]
    anywhere = pl.BlockSpec(memory_space=pl.ANY)
    low = jnp.bfloat16
    return pl.pallas_call(
        forward_kernel,
        name="gather_and_forward",
        out_shape=shapes,
        in_specs=[anywhere] * 9,
        out_specs=[anywhere] * len(shapes),
        scratch_shapes=[pltpu.VMEM(shape, dtype) for _, shape, dtype in ACTS]
        + [pltpu.VMEM(array.shape, array.dtype) for array in shards]
        + [
            pltpu.VMEM(small.shape, small.dtype),
            pltpu.SemaphoreType.DMA((6,)),
            pltpu.SemaphoreType.DMA((6,)),
            pltpu.SemaphoreType.DMA((N_GATHER, 10)),
            pltpu.SemaphoreType.DMA((N_GATHER, 10)),
            pltpu.SemaphoreType.DMA((3,)),
            pltpu.SemaphoreType.DMA((3,)),
            pltpu.SemaphoreType.DMA((2,)),
            pltpu.VMEM(tokens.shape, low),
            pltpu.VMEM(frames.shape, low),
            pltpu.VMEM((4,) + small.shape, low),
            pltpu.VMEM((16, 1024), jnp.float32),
            pltpu.VMEM((8, 1024), jnp.float32),
            pltpu.VMEM((3, 4, 256, 1024), low),
            pltpu.VMEM((256, 256), jnp.float32),
            pltpu.VMEM((256, 256), low),
            pltpu.VMEM((1024, 256), jnp.float32),
            pltpu.VMEM((1024, 256), low),
            pltpu.SemaphoreType.DMA((3,)),
            pltpu.SemaphoreType.DMA((12,)),
            pltpu.SemaphoreType.DMA((N_ACTS,)),
        ],
        compiler_params=pltpu.CompilerParams(
            collective_id=0, has_side_effects=True, vmem_limit_bytes=VMEM_LIMIT
        ),
    )(*shards, small, tokens, frames)


REDUCE_WIDE = 16
RING, OTHERS, HELD, FINALS = 3, 4, 4, 8


def each(rows, body):
    block = min(rows, 16)
    loop(rows // block, lambda i: body(cut(i, block), lambda k: pl.ds(pl.multiple_of(k + i * block, block), block)))


def toggled(bit, flip):
    return bit + flip - 2 * bit * flip


class Lane:
    NAMES = ["other", "one_a", "one_b", "in_a", "in_b", "two_a", "two_b", "fin_a"]
    NAMES += ["fin_b", "acc", "up", "mid", "za", "zb", "tot", "fin"]

    def __init__(self, refs):
        for name, ref in zip(self.NAMES, refs):
            setattr(self, name, ref)


def lane_shapes(ring, others, held, finals, rows, columns, dtype):
    half, quarter = rows // 2, rows // 4
    return [
        pltpu.VMEM((others, 4, half, columns), dtype),
        pltpu.VMEM((ring, 4, quarter, columns), dtype),
        pltpu.VMEM((ring, 4, quarter, columns), dtype),
        pltpu.VMEM((held, 2, quarter, columns), dtype),
        pltpu.VMEM((held, 2, quarter, columns), dtype),
        pltpu.VMEM((ring, quarter, columns), dtype),
        pltpu.VMEM((ring, quarter, columns), dtype),
        pltpu.VMEM((held, quarter, columns), dtype),
        pltpu.VMEM((held, quarter, columns), dtype),
        pltpu.VMEM((ring, half, columns), jnp.float32),
        pltpu.VMEM((ring, half, columns), dtype),
        pltpu.VMEM((ring, half, columns), dtype),
        pltpu.VMEM((held + 1, half, columns), dtype),
        pltpu.VMEM((held, half, columns), dtype),
        pltpu.VMEM((ring, half, columns), dtype),
        pltpu.VMEM((finals, half, columns), dtype),
    ]


class Unit:
    def __init__(self, reduce, u):
        at = reduce.at
        self.u, self.small = u, u == REDUCE_WIDE
        if self.small:
            self.lane, self.source, rows = reduce.thin, reduce.small, 32
            self.s, self.o, self.h, self.f, self.z = 0, 0, 0, 0, 0
        else:
            self.lane, self.source, rows = reduce.wide, reduce.grads.at[u % 2], 256
            self.s, self.o, self.h, self.f = u % RING, u % OTHERS, u % HELD, u % FINALS
            self.z = u % (HELD + 1)
        half = rows // 2
        lane, s, h, f, z = self.lane, self.s, self.h, self.f, self.z
        self.half, self.quarter = half, rows // 4
        self.mine = pl.multiple_of(at.core * half, half)
        self.theirs = pl.multiple_of((1 - at.core) * half, half)

        def move(k, src, dst, device):
            return pltpu.make_async_remote_copy(
                src, dst, reduce.send_sem.at[u, k], reduce.recv_sem.at[u, k],
                device_id=device, device_id_type=MESH,
            )

        self.core = move(0, self.source.at[:, pl.ds(self.theirs, half), :], lane.other.at[self.o], at.c_id)
        self.one_a = move(1, lane.one_a.at[s, pl.ds(2, 2)], lane.in_a.at[h], at.x_id)
        self.one_b = move(2, lane.one_b.at[s, pl.ds(2, 2)], lane.in_b.at[h], at.y_id)
        self.two_a = move(3, lane.two_a.at[s], lane.fin_a.at[h], at.y_id)
        self.two_b = move(4, lane.two_b.at[s], lane.fin_b.at[h], at.x_id)
        self.up = move(5, lane.up.at[s], lane.za.at[z], at.z_id)
        self.mid = move(6, lane.mid.at[s], lane.zb.at[h], reduce.m_id)
        self.down = move(7, lane.tot.at[s], lane.za.at[z], at.z_id)
        self.fin_mid = move(8, lane.tot.at[s], lane.fin.at[f], at.c_id)
        self.fin_end = move(8, lane.za.at[z], lane.fin.at[f], at.c_id)
        target = reduce.target(u)

        def store(k, src, start):
            return pltpu.make_async_copy(src, target(start, half), reduce.out_sem.at[u, k])

        self.own_mid = store(0, lane.tot.at[s], self.mine)
        self.own_end = store(0, lane.za.at[z], self.mine)
        self.rest = store(1, lane.fin.at[f], self.theirs)


class Reduce:
    lag = 7
    ticks = REDUCE_WIDE + 1 + lag

    def __init__(self, at, grads, small, outs, small_out, wide, thin, sems):
        self.at, self.grads, self.small, self.outs, self.small_out = at, grads, small, outs, small_out
        self.wide, self.thin = Lane(wide), Lane(thin)
        self.send_sem, self.recv_sem, self.out_sem, self.credit = sems
        self.bx, self.by = lax.rem(at.g, 2), lax.div(at.g, 2)
        self.middle = lax.div(at.z * (3 - at.z), 2)
        self.is_end, self.is_mid = self.middle == 0, self.middle == 1
        self.m_id = (at.g, at.r + self.middle * (6 - 4 * at.z) + (1 - self.middle) * (2 - 4 * at.zb))
        self.units = [Unit(self, u) for u in range(REDUCE_WIDE + 1)]

    def target(self, u):
        outs = self.outs
        if u == REDUCE_WIDE:
            return lambda start, rows: self.small_out.at[pl.ds(start, rows)]
        if u < 4:
            return lambda start, rows: outs[5].at[pl.ds(256 * u + start, rows)]
        if u < 8:
            return lambda start, rows: outs[4].at[pl.ds(start, rows), pl.ds(1024 * (u - 4), 1024)]
        k, lead = {8: (3, None), 9: (2, 0), 10: (2, 1), 11: (2, 2), 12: (1, None), 13: (0, 0), 14: (0, 1), 15: (0, 2)}[u]
        return lambda start, rows: outs[k].at[(pl.ds(start, rows),) if lead is None else (lead, pl.ds(start, rows))]

    def open(self):
        at = self.at
        barrier = pltpu.get_barrier_semaphore()
        for device in (at.x_id, at.y_id, at.c_id, at.z_id):
            pl.semaphore_signal(barrier, inc=1, device_id=device, device_id_type=MESH)

        @pl.when(self.is_mid)
        def _():
            pl.semaphore_signal(barrier, inc=1, device_id=self.m_id, device_id_type=MESH)

        pl.semaphore_wait(barrier, 4 + self.middle)

    def before(self, unit, depth):
        return self.units[unit.u - depth] if unit.u >= depth and not unit.small else None

    def room(self, u):
        old = self.before(self.units[u], 2)
        if old is not None:
            old.core.wait_send()

    def begin(self, unit):
        if not unit.small and unit.u >= OTHERS:
            pl.semaphore_wait(self.credit, 1)
        unit.core.start()

    def join(self, unit):
        lane, q, s, o = unit.lane, unit.quarter, unit.s, unit.o
        unit.core.wait_recv()
        old = self.before(unit, RING)
        if old is not None:
            old.one_a.wait_send()
            old.one_b.wait_send()
        dtype = lane.one_a.dtype
        bx, by, source, mine = self.bx, self.by, unit.source, unit.mine

        def body(j):
            first, second = lax.rem(j, 2), lax.div(j, 2)
            ga = toggled(bx, second) + 2 * toggled(by, first)
            gb = toggled(bx, first) + 2 * toggled(by, second)
            rows_a, rows_b = pl.ds(mine, q), pl.ds(pl.multiple_of(mine + q, q), q)
            lane.one_a[s, j] = (f32(source[ga, rows_a]) + f32(lane.other[o, ga, 0:q])).astype(dtype)
            lane.one_b[s, j] = (f32(source[gb, rows_b]) + f32(lane.other[o, gb, q : 2 * q])).astype(dtype)

        loop(4, body)
        if not unit.small and unit.u + OTHERS < REDUCE_WIDE:
            pl.semaphore_signal(self.credit, inc=1, device_id=self.at.c_id, device_id_type=MESH)
        unit.one_a.start()
        unit.one_b.start()

    def cross(self, unit):
        lane, q, s, h = unit.lane, unit.quarter, unit.s, unit.h
        unit.one_a.wait_recv()
        unit.one_b.wait_recv()
        old = self.before(unit, RING)
        if old is not None:
            old.two_a.wait_send()
            old.two_b.wait_send()
        dtype = lane.one_a.dtype

        def body(rows, after):
            lane.two_a[s, rows] = (f32(lane.one_a[s, 1, rows]) + f32(lane.in_a[h, 1, rows])).astype(dtype)
            lane.two_b[s, rows] = (f32(lane.one_b[s, 1, rows]) + f32(lane.in_b[h, 1, rows])).astype(dtype)
            lane.acc[s, rows] = f32(lane.one_a[s, 0, rows]) + f32(lane.in_a[h, 0, rows])
            lane.acc[s, after(q)] = f32(lane.one_b[s, 0, rows]) + f32(lane.in_b[h, 0, rows])

        each(q, body)
        unit.two_a.start()
        unit.two_b.start()

    def close(self, unit):
        lane, q, s, h = unit.lane, unit.quarter, unit.s, unit.h
        unit.two_a.wait_recv()
        unit.two_b.wait_recv()
        old = self.before(unit, RING)
        dtype = lane.one_a.dtype

        @pl.when(self.is_end)
        def _():
            if old is not None:
                old.up.wait_send()

            def body(rows, after):
                lane.up[s, rows] = (lane.acc[s, rows] + f32(lane.fin_a[h, rows])).astype(dtype)
                lane.up[s, after(q)] = (lane.acc[s, after(q)] + f32(lane.fin_b[h, rows])).astype(dtype)

            each(q, body)
            unit.up.start()

        @pl.when(self.is_mid)
        def _():
            def body(rows, after):
                lane.acc[s, rows] = lane.acc[s, rows] + f32(lane.fin_a[h, rows])
                lane.acc[s, after(q)] = lane.acc[s, after(q)] + f32(lane.fin_b[h, rows])

            each(q, body)

    def climb(self, unit):
        lane, s, h = unit.lane, unit.s, unit.h
        old = self.before(unit, RING)

        @pl.when(self.is_mid)
        def _():
            unit.up.wait_recv()
            if old is not None:
                old.mid.wait_send()

            def body(rows, after):
                lane.mid[s, rows] = (lane.acc[s, rows] + f32(lane.za[unit.z, rows])).astype(lane.mid.dtype)

            each(unit.half, body)
            unit.mid.start()

    def peak(self, unit):
        lane, s, h = unit.lane, unit.s, unit.h
        old = self.before(unit, RING)

        @pl.when(self.is_mid)
        def _():
            unit.mid.wait_recv()
            if old is not None:
                old.down.wait_send()
                old.fin_mid.wait_send()
                old.own_mid.wait()

            def body(rows, after):
                lane.tot[s, rows] = (f32(lane.mid[s, rows]) + f32(lane.zb[h, rows])).astype(lane.tot.dtype)

            each(unit.half, body)
            unit.down.start()
            unit.fin_mid.start()
            unit.own_mid.start()

    def land(self, unit):
        @pl.when(self.is_end)
        def _():
            unit.down.wait_recv()
            unit.fin_end.start()
            unit.own_end.start()

    def finish(self, unit):
        unit.fin_mid.wait_recv()
        unit.rest.start()
        if unit.u > 0:
            self.units[unit.u - 1].rest.wait()

        @pl.when(self.is_end)
        def _():
            unit.fin_end.wait_send()
            unit.own_end.wait()

    def tick(self, t):
        stages = (self.begin, self.join, self.cross, self.close, self.climb, self.peak, self.land, self.finish)
        for lag, stage in enumerate(stages):
            if 0 <= t - lag <= REDUCE_WIDE:
                stage(self.units[t - lag])

    def shut(self):
        for unit in self.units:
            if unit.small or unit.u + 2 >= REDUCE_WIDE:
                unit.core.wait_send()
            if unit.small or unit.u + RING >= REDUCE_WIDE:
                for move in (unit.one_a, unit.one_b, unit.two_a, unit.two_b):
                    move.wait_send()
                pl.when(self.is_end)(unit.up.wait_send)

                @pl.when(self.is_mid)
                def _(unit=unit):
                    unit.mid.wait_send()
                    unit.down.wait_send()
                    unit.fin_mid.wait_send()
                    unit.own_mid.wait()

        self.units[-1].rest.wait()


def columns_sum(ref, block=64):
    def step(i, carry):
        return carry + jnp.sum(f32(ref[cut(i, block)]), axis=0, keepdims=True)

    return lax.fori_loop(0, ref.shape[0] // block, step, jnp.zeros((1, ref.shape[1]), jnp.float32))


def norm_back_rows(values, grad, gain, base, out, low):
    width = grad.shape[1]

    def step(i, carry):
        rows = cut(i, 32)
        v, d = f32(values[rows]), grad[rows]
        center = v - jnp.mean(v, axis=-1, keepdims=True)
        scale = lax.rsqrt(jnp.mean(center * center, axis=-1, keepdims=True) + EPSILON)
        unit = center * scale
        inner = d * gain[...]
        back = inner - jnp.mean(inner, axis=-1, keepdims=True) - unit * jnp.mean(inner * unit, axis=-1, keepdims=True)
        result = f32(base[rows]) + scale * back
        out[rows] = result
        third = carry[2]
        if low is not None:
            rounded = result.astype(jnp.bfloat16)
            low[rows] = rounded
            third = third + jnp.sum(f32(rounded), axis=0, keepdims=True)
        return (
            carry[0] + jnp.sum(d * unit, axis=0, keepdims=True),
            carry[1] + jnp.sum(d, axis=0, keepdims=True),
            third,
        )

    zero = jnp.zeros((1, width), jnp.float32)
    return lax.fori_loop(0, grad.shape[0] // 32, step, (zero, zero, zero))


BACK_WEIGHTS = [(5, 0), (4, 0), (5, 1), (4, 1), (5, 2), (4, 2), (5, 3), (4, 3)]
BACK_WEIGHTS += [(3, None), (2, 0), (1, None), (0, 0), (0, 1), (0, 2), (2, 1), (2, 2)]

BACK_ROOMS = (
    [("ct", (256, 1024), jnp.bfloat16), ("gk", (1024, 1024), jnp.bfloat16), ("slope", (2, 256, 1024), jnp.float32)]
    + [("dz", (1024, 1024), jnp.bfloat16), ("n3", (256, 1024), jnp.bfloat16), ("h", (256, 1024), jnp.float32)]
    + [("dn", (256, 1024), jnp.float32), ("dh", (256, 1024), jnp.float32), ("out", (256, 1024), jnp.float32)]
    + [("low", (256, 1024), jnp.bfloat16), ("ring", (3, 4, 256, 1024), jnp.bfloat16), ("e2", (256, 1024), jnp.bfloat16)]
    + [("o2", (256, 1024), jnp.bfloat16), ("do2", (256, 1024), jnp.bfloat16), ("q2", (256, 1024), jnp.bfloat16)]
    + [("v2", (1024, 1024), jnp.bfloat16), ("dq2", (256, 1024), jnp.bfloat16), ("dk2", (1024, 1024), jnp.bfloat16)]
    + [("dv2", (1024, 1024), jnp.bfloat16), ("n2", (256, 1024), jnp.bfloat16), ("frames", (1024, 1024), jnp.bfloat16)]
    + [("scores", (1024, 256), jnp.float32), ("gscores", (1024, 256), jnp.float32)]
    + [("probs", (1024, 512), jnp.bfloat16), ("gs", (1024, 512), jnp.bfloat16)]
    + [("lse", (16, 8, 256), jnp.float32), ("table", (4, 32, 256), jnp.bfloat16)]
    + [("rows", (16, 1024), jnp.float32), ("hidden", (8, 1024), jnp.float32)]
    + [("grads", (2, 4, 256, 1024), jnp.bfloat16), ("small", (4, 32, 256), jnp.float32)]
)
BACK_INPUTS = ["tokens", "frames", "cotangent"] + [name for name, _, _ in ACTS]


class Rooms:
    def __init__(self, names, refs):
        for name, ref in zip(names, refs):
            setattr(self, name, ref)


def backward_kernel(*refs):
    n_in = 7 + len(BACK_INPUTS)
    fulls, small_full = refs[:6], refs[6]
    given = dict(zip(BACK_INPUTS, refs[7:n_in]))
    result, grad_tokens, grad_frames = refs[n_in : n_in + 3]
    outs, small_out = refs[n_in + 3 : n_in + 9], refs[n_in + 9]
    refs = refs[n_in + 10 :]
    room = Rooms([name for name, _, _ in BACK_ROOMS], refs)
    refs = refs[len(BACK_ROOMS) :]
    lane_count = len(Lane.NAMES)
    wide, thin, refs = refs[:lane_count], refs[lane_count : 2 * lane_count], refs[2 * lane_count :]
    sems, load_sem, ring_sem, store_sem = refs[:4], refs[4], refs[5], refs[6]
    at = Spot()
    reduce = Reduce(at, room.grads, room.small, outs, small_out, wide, thin, sems)
    ct, gk, dz, v2, small, rows = room.ct, room.gk, room.dz, room.v2, room.small, room.rows
    n3, h, dn, dh, out, frames = room.n3, room.h, room.dn, room.dh, room.out, room.frames

    def quarter(ref, m):
        return ref.at[pl.ds(256 * m, 256)]

    loads = {}

    def plan(name, src, dst):
        loads[name] = pltpu.make_async_copy(src, dst, load_sem.at[len(loads)])

    plan("table", small_full, room.table)
    plan("ct", given["cotangent"], ct)
    for m in range(4):
        plan(f"g{m}", given["g"].at[m], quarter(gk, m))
        plan(f"slope{m}", given["slope"].at[m], room.slope.at[m % 2])
    plan("n3", given["n3"], n3)
    plan("h2", given["h2"], h)
    plan("o2", given["o2"], room.o2)
    plan("q2", given["q2"], room.q2)
    plan("k2", given["k2"], gk)
    plan("v2", given["v2"], v2)
    plan("lse2", given["lse2"], room.lse)
    plan("frames", given["frames"], frames)
    plan("n2", given["n2"], room.n2)
    plan("h1", given["h1"], h)
    q1, k1, v1, o1 = (quarter(gk, m) for m in range(4))
    n1, x, e1 = (quarter(v2, m) for m in range(3))
    do1, dq1, dk1, dv1 = (quarter(dz, m) for m in range(4))
    plan("q1", given["q1"], q1)
    plan("k1", given["k1"], k1)
    plan("v1", given["v1"], v1)
    plan("o1", given["o1"], o1)
    plan("lse1", given["lse1"], room.lse)
    plan("n1", given["n1"], n1)
    plan("x", given["tokens"], x)
    waited = set()

    def load(*names):
        for name in names:
            loads[name].start()

    def have(*names):
        for name in names:
            if name not in waited:
                waited.add(name)
                loads[name].wait()

    fetched, held = set(), set()

    def fetch(i):
        n, lead = BACK_WEIGHTS[i]
        source = fulls[n]
        if n == 4:
            source = source.at[:, :, pl.ds(1024 * lead, 1024)]
        elif lead is not None:
            source = source.at[lead]
        return pltpu.make_async_copy(source, room.ring.at[i % 3], ring_sem.at[i])

    def weight(i, ahead=2):
        for k in range(i, min(i + ahead + 1, len(BACK_WEIGHTS))):
            if k not in fetched:
                fetched.add(k)
                fetch(k).start()
        if i not in held:
            held.add(i)
            fetch(i).wait()
        return room.ring.at[i % 3]

    def note(k, row):
        for g in range(4):
            small[g, k : k + 1, :] = row[:, 256 * g : 256 * g + 256]

    def row(k):
        return rows.at[pl.ds(k, 1)]

    def tall(target, left, w, first):
        def body(g):
            columns = cut(g, 256)
            value = dot_nt(left[...], w[g])
            if not first:
                value = target[:, columns] + value
            target[:, columns] = value.astype(target.dtype)

        loop(4, body)

    def start():
        have("table")
        set_rows(room.table, rows, room.hidden)
        small[...] = jnp.zeros_like(small)
        have("ct", "g0", "g1", "g2", "g3")
        note(12, columns_sum(ct))

    def feed(m):
        def run():
            w = weight(2 * m)
            have(f"slope{m}")
            if m == 0:
                have("h2")

            def onward(j):
                columns = cut(j, 256)
                value = dot(quarter(gk, m)[...], w[:, :, columns].reshape(-1, 256))
                if m == 0:
                    value = value + h[:, columns] + rows[12:13, columns]
                else:
                    value = value + out[:, columns]
                out[:, columns] = value

            loop(4, onward)

            def back(g):
                columns = cut(g, 256)
                value = dot_nt(ct[...], w[g]) * room.slope[m % 2, :, columns]
                dz[256 * m : 256 * m + 256, columns] = value.astype(dz.dtype)

            loop(4, back)
            if m < 2:
                load(f"slope{m + 2}")
            sums = columns_sum(quarter(dz, m))
            for k in range(4):
                small[m, 13 + k : 14 + k, :] = sums[:, 256 * k : 256 * k + 256]
            tall(dn, quarter(dz, m), weight(2 * m + 1), m == 0)

        return run

    def write(ref, target, k):
        copy = pltpu.make_async_copy(ref, target, store_sem.at[k])
        copy.start()
        return copy

    stores = []

    def norm3():
        room.low[...] = out[...].astype(jnp.bfloat16)
        stores.append(write(room.low, result, 0))
        gain, shift, column = norm_back_rows(h, dn, row(2), ct, dh, room.e2)
        note(2, gain)
        note(11, shift)
        note(10, column)
        load("h1")

    def out2():
        load("k2", "lse2")
        tall(room.do2, room.e2, weight(8), True)

    def cross(first, count):
        def run():
            have("q2", "k2", "v2", "lse2")
            loop(
                count,
                lambda p: attend_back_pair(
                    p + first, room.q2, gk, v2, room.do2, room.lse, room.scores, room.gscores,
                    room.probs, room.gs, room.dq2, room.dk2, room.dv2, False,
                ),
            )

        return run

    def norm2():
        load("q1", "k1", "v1", "o1", "n1", "x", "lse1")
        note(8, columns_sum(room.dq2))
        note(9, columns_sum(room.dv2))
        tall(dn, room.dq2, weight(9), True)
        have("h1")
        gain, shift, column = norm_back_rows(h, dn, row(1), dh, dh, e1)
        note(1, gain)
        note(7, shift)
        note(6, column)

    def out1():
        tall(do1, e1, weight(10), True)

    def self_back(first, count):
        def run():
            have("q1", "k1", "v1", "lse1")
            part = pl.ds(0, 256)
            loop(
                count,
                lambda p: attend_back_pair(
                    p + first, q1, k1, v1, do1, room.lse, room.scores.at[part], room.gscores.at[part],
                    room.probs.at[part], room.gs.at[part], dq1, dk1, dv1, True,
                ),
            )

        return run

    def norm1():
        note(4, columns_sum(dq1))
        note(5, columns_sum(dv1))
        for k, grad in enumerate((dq1, dk1, dv1)):
            tall(dn, grad, weight(11 + k), k == 0)
        have("x")
        gain, shift, _ = norm_back_rows(x, dn, row(0), dh, out, None)
        note(0, gain)
        note(3, shift)
        stores.append(write(out, grad_tokens, 1))

    def frames_back(g):
        def run():
            wk, wv = weight(14, 1), weight(15, 0)
            stage = room.scores if g % 2 == 0 else room.gscores
            if g >= 2:
                stores[g].wait()

            def body(j):
                lines = cut(j, 256)
                stage[lines] = dot_nt(room.dk2[lines], wk[g]) + dot_nt(room.dv2[lines], wv[g])

            loop(4, body)
            stores.append(write(stage, grad_frames.at[:, pl.ds(256 * g, 256)], 2 + g))

        return run

    def outer(u, left, right, tokens=256):
        def body(g):
            columns = cut(g, 256)
            value = dot_tn(left[:, columns], right[...])
            room.grads[u % 2, g] = value.astype(jnp.bfloat16)

        loop(4, body)

    def grad(u):
        reduce.room(u)
        if u < 4:
            for m in range(4):
                value = dot_tn(gk[256 * m : 256 * m + 256, 256 * u : 256 * u + 256], ct[...])
                room.grads[u % 2, m] = value.astype(jnp.bfloat16)
        elif u < 8:
            have("n3")
            outer(u, n3, quarter(dz, u - 4))
        elif u == 8:
            have("o2")
            outer(u, room.o2, room.e2)
        elif u == 9:
            have("n2")
            outer(u, room.n2, room.dq2)
        elif u < 12:
            have("frames")
            outer(u, frames, room.dk2 if u == 10 else room.dv2)
        elif u == 12:
            have("o1")
            outer(u, o1, e1)
        elif u < 16:
            have("n1")
            outer(u, n1, (dq1, dk1, dv1)[u - 13])

    steps = [("start", -1, 2, start)]
    steps += [(f"feed{m}", -1, 9, feed(m)) for m in range(4)]
    steps += [("norm3", -1, 3, norm3), ("out2", 3, 2, out2)]
    steps += [(f"cross{k}", 3, 9, cross(2 * k, 2)) for k in range(4)]
    steps += [("norm2", -1, 5, norm2), ("out1", 7, 2, out1)]
    steps += [(f"self{k}", 7, 6, self_back(4 * k, 4)) for k in range(2)]
    steps += [("norm1", -1, 8, norm1)]
    steps += [(f"frames{g}", -1, 4, frames_back(g)) for g in range(4)]
    needs = ["start"] * 4 + [f"feed{m}" for m in range(4)] + ["norm3", "cross3", "cross3", "cross3", "norm2"]
    needs += ["self1"] * 3 + ["norm1"]

    load("table", "ct", "g0", "g1", "g2", "g3", "slope0", "h2", "slope1", "n3", "o2", "q2", "v2", "frames", "n2")
    reduce.open()
    done, now, tick, last = set(), 0.0, 0, -100.0
    left = list(steps)
    while left or tick < reduce.ticks:
        can_tick = tick < reduce.ticks and (tick > REDUCE_WIDE or needs[tick] in done)
        can_step = bool(left) and left[0][1] < tick
        if can_tick and (now - last >= BACK_PERIOD or not can_step):
            now = max(now, last + (BACK_PERIOD if not can_step else 0.0))
            last = now
            if tick < REDUCE_WIDE:
                grad(tick)
                now += 3.0
            reduce.tick(tick)
            now += 2.0
            tick += 1
        else:
            name, _, cost, run = left.pop(0)
            run()
            done.add(name)
            now += cost
    reduce.shut()
    stores[0].wait()
    stores[1].wait()
    stores[4].wait()
    stores[5].wait()


BACK_PERIOD = 5.5


def backward_all(full, tokens, frames, cotangent):
    low, wide = jnp.bfloat16, jnp.float32
    width = 1024
    shapes = [
        jax.ShapeDtypeStruct((256, width), low),
        jax.ShapeDtypeStruct((256, width), wide),
        jax.ShapeDtypeStruct((1024, width), wide),
        jax.ShapeDtypeStruct((3, 256, width), low),
        jax.ShapeDtypeStruct((256, width), low),
        jax.ShapeDtypeStruct((3, 256, width), low),
        jax.ShapeDtypeStruct((256, width), low),
        jax.ShapeDtypeStruct((256, 4 * width), low),
        jax.ShapeDtypeStruct((1024, width), low),
        jax.ShapeDtypeStruct((32, 256), wide),
    ]
    weights = list(full[:7])
    weights[5] = weights[5].reshape(4, 4, 256, width)
    args = (*weights, tokens, frames, cotangent, *full[7:])
    anywhere = pl.BlockSpec(memory_space=pl.ANY)
    return pl.pallas_call(
        backward_kernel,
        name="backward_and_reduce",
        out_shape=shapes,
        in_specs=[anywhere] * len(args),
        out_specs=[anywhere] * len(shapes),
        scratch_shapes=[pltpu.VMEM(shape, dtype) for _, shape, dtype in BACK_ROOMS]
        + lane_shapes(RING, OTHERS, HELD, FINALS, 256, width, low)
        + lane_shapes(1, 1, 1, 1, 32, 256, wide)
        + [
            pltpu.SemaphoreType.DMA((REDUCE_WIDE + 1, 9)),
            pltpu.SemaphoreType.DMA((REDUCE_WIDE + 1, 9)),
            pltpu.SemaphoreType.DMA((REDUCE_WIDE + 1, 2)),
            pltpu.SemaphoreType.REGULAR,
            pltpu.SemaphoreType.DMA((32,)),
            pltpu.SemaphoreType.DMA((len(BACK_WEIGHTS),)),
            pltpu.SemaphoreType.DMA((6,)),
        ],
        compiler_params=pltpu.CompilerParams(
            collective_id=1, has_side_effects=True, vmem_limit_bytes=VMEM_LIMIT
        ),
    )(*args)


def widen_pieces(refs):
    self_qkv, self_out, cross_qkv, cross_out, fc1, fc2 = refs
    pieces = [fc2.at[pl.ds(256 * m, 256)] for m in range(4)]
    pieces += [fc1.at[:, pl.ds(1024 * m, 1024)] for m in range(4)]
    pieces += [cross_out] + [cross_qkv.at[m] for m in range(3)] + [self_out] + [self_qkv.at[m] for m in range(3)]
    return pieces


def widen_kernel(*refs):
    result, grad_tokens, grad_frames, grads, small = *refs[:3], refs[3:9], refs[9]
    outs, gains, biases, hidden = refs[10:19], refs[19], refs[20], refs[21]
    low, high, v_result, v_tokens, v_frames, in_sem, out_sem = refs[22:]
    sources = widen_pieces(grads) + [result, grad_tokens, grad_frames]
    targets = widen_pieces(outs[3:]) + list(outs[:3])
    count = len(sources) - 3
    inside = [low.at[k] for k in range(count)] + [v_result, v_tokens, v_frames]
    ready = [high.at[k] for k in range(count)] + [v_result, v_tokens, v_frames]
    loads = [pltpu.make_async_copy(a, b, in_sem.at[k]) for k, (a, b) in enumerate(zip(sources, inside))]
    stores = [pltpu.make_async_copy(a, b, out_sem.at[k]) for k, (a, b) in enumerate(zip(ready, targets))]
    for load in loads:
        load.start()
    gains[...] = small[0:3]
    biases[...] = small[3:13]
    hidden[...] = small[13:17]
    for k in range(count + 3):
        loads[k].wait()
        if k < count:

            def body(i):
                high[k, cut(i, 64)] = f32(low[k, cut(i, 64)])

            loop(4, body)
        stores[k].start()
    for store in stores:
        store.wait()


def widen_all(done):
    wide = jnp.float32
    anywhere, inside = pl.BlockSpec(memory_space=pl.ANY), pl.BlockSpec(memory_space=pltpu.VMEM)
    shapes = [jax.ShapeDtypeStruct(a.shape, a.dtype if k == 0 else wide) for k, a in enumerate(done[:9])]
    shapes += [jax.ShapeDtypeStruct((rows, 256), wide) for rows in (3, 10, 4)]
    return pl.pallas_call(
        widen_kernel,
        name="widen",
        out_shape=shapes,
        in_specs=[anywhere] * 9 + [inside],
        out_specs=[anywhere] * 9 + [inside] * 3,
        scratch_shapes=[
            pltpu.VMEM((16, 256, 1024), jnp.bfloat16),
            pltpu.VMEM((16, 256, 1024), wide),
            pltpu.VMEM(done[0].shape, done[0].dtype),
            pltpu.VMEM(done[1].shape, wide),
            pltpu.VMEM(done[2].shape, wide),
            pltpu.SemaphoreType.DMA((19,)),
            pltpu.SemaphoreType.DMA((19,)),
        ],
        compiler_params=pltpu.CompilerParams(vmem_limit_bytes=VMEM_LIMIT),
    )(*done)


def shards_here(
    tokens,
    frames,
    cotangent,
    self_qkv,
    self_out,
    cross_qkv,
    cross_out,
    fc1_weight,
    fc2_weight,
    gains,
    biases,
    fc1_bias,
):
    part = gains.shape[1]
    small = jnp.concatenate(
        [gains, biases, fc1_bias.reshape(4, part), jnp.zeros((15, part), jnp.bfloat16)], axis=0
    )
    shards = (self_qkv, self_out, cross_qkv, cross_out, fc1_weight, fc2_weight)
    full = forward_all(shards, small, tokens[0], frames[0])
    done = widen_all(backward_all(full, tokens[0], frames[0], cotangent[0]))
    return (done[0][None], done[1][None], done[2][None], *done[3:11], done[11].reshape(-1))


def solution(mesh):
    in_specs = (
        P((GROUP, REPLICA), None, None),
        P((GROUP, REPLICA), None, None),
        P((GROUP, REPLICA), None, None),
        P(None, GROUP, None),
        P(GROUP, None),
        P(None, GROUP, None),
        P(GROUP, None),
        P(GROUP, None),
        P(GROUP, None),
        P(None, GROUP),
        P(None, GROUP),
        P(GROUP),
    )
    out_specs = (
        P((GROUP, REPLICA), None, None),
        P((GROUP, REPLICA), None, None),
        P((GROUP, REPLICA), None, None),
        P(None, GROUP, None),
        P(GROUP, None),
        P(None, GROUP, None),
        P(GROUP, None),
        P(GROUP, None),
        P(GROUP, None),
        P(None, GROUP),
        P(None, GROUP),
        P(GROUP),
    )
    here = mesh.shape[GROUP] == 4 and mesh.shape[REPLICA] == 8
    body = shards_here if here else shards_any
    return jax.shard_map(body, mesh=mesh, in_specs=in_specs, out_specs=out_specs, check_vma=False)
```
